32 devices in a mesh: dp: 4 (over z), expert: 8 (over y, x, core).
Axes of the slice: x: 2, y: 2, z: 4, core: 2. Of those that a mesh axis runs over, the one named last changes fastest.
Arguments:
- tokens: bfloat16 [8192, 1536], P(('dp', 'expert')), may hold values from -6 to 6
- segment_ids: int32 [8192], P('dp'), may hold values from 0 to 7, never falling along the last dimension, each value on 1 to 2048 neighbouring positions
- expert_ids: int32 [8192, 8], P(('dp', 'expert')), may hold values from 0 to 15, all different within a row; in each aligned block of 256 rows (0 to 255, 256 to 511, ...) at most 160 rows name the same one
- w_query: bfloat16 [1536, 1536], P(('dp', 'expert')), may hold values from -0.5 to 0.5
- w_key_value: bfloat16 [1536, 1024], P(('dp', 'expert')), may hold values from -0.5 to 0.5
- w_out: bfloat16 [1536, 1536], P(None, ('dp', 'expert')), may hold values from -1.75 to 1.75
- w_router: bfloat16 [1536, 16], P(('dp', 'expert')), may hold values from -0.078125 to 0.078125
- norm_attn: bfloat16 [1536], P(('dp', 'expert')), may hold values from 0.5 to 1.5
- norm_moe: bfloat16 [1536], P(('dp', 'expert')), may hold values from 0.5 to 1.5
- w_gate_up: bfloat16 [16, 1536, 1024], P('expert'), may hold values from -0.15625 to 0.15625
- w_down: bfloat16 [16, 512, 1536], P('expert'), may hold values from -6 to 6
- grad_out: bfloat16 [8192, 1536], P(('dp', 'expert')), may hold values from -6 to 6
Outputs:
- result: bfloat16 [8192, 1536], P(('dp', 'expert'))
- grad_tokens: bfloat16 [8192, 1536], P(('dp', 'expert'))
- grad_w_query: float32 [1536, 1536], P(('dp', 'expert'))
- grad_w_key_value: float32 [1536, 1024], P(('dp', 'expert'))
- grad_w_out: float32 [1536, 1536], P(None, ('dp', 'expert'))
- grad_w_router: float32 [1536, 16], P(('dp', 'expert'))
- grad_norm_attn: float32 [1536], P(('dp', 'expert'))
- grad_norm_moe: float32 [1536], P(('dp', 'expert'))
- grad_w_gate_up: float32 [16, 1536, 1024], P('expert', 'dp')
- grad_w_down: float32 [16, 512, 1536], P('expert', None, 'dp')
The draws below stay inside these ranges and needn't reach their ends.
Inputs may be any that keep to these rules, and one draw needn't show every extreme that they name: `expert_ids`: within the 256 tokens of one device a row names 8 different experts, and no expert is named more than 160 times; in every draw some expert is named exactly 160 times by one device's tokens.
All inputs are finite; a program needn't handle non-finite values.
Results may differ from the reference program's by a relative error of at most 0.02.
Values may be sent and summed in bfloat16 or wider, within the bound.
No kernel may reach another device: no remote copies, remote signals or barrier semaphores. Data moves between devices by JAX's collectives and lax.ppermute only.
A program may use at most 256 MiB of HBM per device.

```python
import math
import jax
import jax.numpy as jnp
import numpy as np
from jax import lax

D = 1536
HEADS = 24
KV_HEADS = 8
HEAD_DIM = 64
FF = 512
TOP = 8
TOK_DEV = 256
EXPERTS = 16
SEQ_LEN = 2048
TOKENS = 8192
CAP = 160
N_EXPERT = 8


def with_spikes(values, key, source, target, blocks, factor):
    def block_of(dim):
        return (jnp.arange(values.shape[dim]) // (values.shape[dim] // blocks)).reshape((-1,) + (1,) * (values.ndim - 1 - dim))

    one_side = jax.random.permutation(key, blocks)[block_of(target)]
    far = (block_of(target) + blocks // 2) % blocks
    return jnp.where((block_of(source) == one_side) | (block_of(source) == far), factor * values, values)


def levels(key, shape, split, least, high):
    gain, own = 1.0, jax.random.fold_in(key, 6)
    for dim, parts in split:
        steps = jnp.exp(jax.random.uniform(jax.random.fold_in(own, dim), (parts,), jnp.float32, least / len(split), high / len(split)))
        gain = gain * jnp.repeat(steps, shape[dim] // parts).reshape([-1 if axis == dim else 1 for axis in range(len(shape))])
    return gain


def profile(number_of, total, reach, lean):
    weights = [(1 << 20) // math.isqrt(rank ** lean) + 1 for rank in range(2, number_of + 1)]
    spare, given = total - reach - (number_of - 1), [1] * (number_of - 1)
    while spare > 0:
        movable = [i for i in range(number_of - 1) if given[i] < reach]
        pool, left = sum([weights[i] for i in movable]), spare
        for i in movable:
            extra = min(reach - given[i], max(1, left * weights[i] // pool), spare)
            given[i] = given[i] + extra
            spare = spare - extra
    return np.array([reach] + given)


def ragged_sizes(key, count, total, bound, slope):
    if count == 2:
        one = jax.random.randint(key, (), max(1, total - bound), min(bound, total - 1) + 1)
        return jnp.stack([one, total - one])
    lengths = jnp.asarray(profile(count, total, bound, slope), jnp.int32)
    couples = (count - 1) // 2
    donor, taker = lengths[1:1 + 2 * couples:2], lengths[2:2 + 2 * couples:2]
    margin = jnp.minimum(donor - 1, bound - taker)
    passed = jax.random.randint(jax.random.fold_in(key, 1), (couples,), 0, 1 << 20) % (margin + 1)
    lengths = lengths.at[1:1 + 2 * couples:2].set(donor - passed).at[2:2 + 2 * couples:2].set(taker + passed)
    return lengths[jax.random.permutation(jax.random.fold_in(key, 2), count)]


def shared_out(rng, own, number, rows, number_of, top, reach, slope):
    sequence = jax.random.permutation(rng, number_of)
    crowded, usual = load_shares(number_of, rows * top, reach, slope, True), load_shares(number_of, rows * top, reach, slope, False)
    places = jnp.arange(number_of)

    def named(sizes, turn):
        used = int((sizes > 0).sum())
        fixed = max(1, used // 4)
        moved = fixed + (places - fixed + turn * (used - fixed)) % max(1, number_of - fixed)
        return jnp.zeros((number_of,), jnp.int32).at[sequence[jnp.where(places < fixed, places, moved)]].set(jnp.asarray(sizes, jnp.int32))

    sizes = jnp.where(number % 4 == 0, named(crowded, number // 4), named(usual, number - number // 4 - 1))
    mixed = jax.random.permutation(jax.random.fold_in(own, 3), number_of)
    source_of, sink = mixed[0:number_of // 2 * 2:2], mixed[1:number_of // 2 * 2:2]
    slack = jnp.minimum(sizes[source_of] - 1, reach - sizes[sink]) // 2
    slack = jnp.where((source_of == sequence[0]) | (sink == sequence[0]) | (sizes[sink] == 0), 0, jnp.maximum(slack, 0))
    moved = jax.random.randint(jax.random.fold_in(own, 4), (number_of // 2,), 0, 1 << 20) % (slack + 1)
    sizes = sizes.at[source_of].add(-moved).at[sink].add(moved)
    members = jnp.searchsorted(jnp.cumsum(sizes), jnp.arange(rows * top), side="right").astype(jnp.int32)
    listing = members.reshape(top, rows).T
    listing = listing[jax.random.permutation(jax.random.fold_in(own, 1), rows)]
    turn = jax.random.randint(jax.random.fold_in(own, 2), (rows, 1), 0, top)
    return jnp.take_along_axis(listing, (jnp.arange(top)[None, :] + turn) % top, axis=1)


def load_shares(number_of, total, most, skew, full):
    portions = [(1 << 20) // math.isqrt(standing ** skew) + 1 for standing in range(1, number_of + 1)]
    largest = most if full else min(most, max(-(-total // number_of), total * portions[0] // sum(portions)))
    least = 1 if total - largest >= number_of - 1 else 0
    counts, surplus = [largest] + [least] * (number_of - 1), total - largest - least * (number_of - 1)
    while surplus > 0:
        free = [i for i in range(1, number_of) if counts[i] < largest] or [i for i in range(1, number_of) if counts[i] < most]
        pool, budget = sum([portions[i] for i in free]), surplus
        for i in free:
            extra = min(most - counts[i], max(1, budget * portions[i] // pool), surplus)
            counts[i] = counts[i] + extra
            surplus = surplus - extra
    return np.array(counts)


def normal_values(own_key, shape, width, reach, shards=(), kind=jnp.bfloat16):
    result = width * jax.random.normal(own_key, shape, jnp.float32)
    if shards:
        result = result * levels(own_key, shape, shards, -0.22, 0.18)
    return jnp.clip(result, -reach, reach).astype(kind)


def bell_draw_with(own_key, shape, spread, bound, cuts, heavy, held_as=jnp.bfloat16):
    result = spread * jax.random.normal(own_key, shape, jnp.float32)
    if cuts:
        result = result * levels(own_key, shape, cuts, -0.22, 0.18)
    return jnp.clip(with_spikes(result, jax.random.fold_in(own_key, 3), *heavy), -bound, bound).astype(held_as)


def setup_inputs(seed: int = 0) -> dict:
    keys = jax.random.split(jax.random.key(seed), 13)
    tokens = normal_values(keys[0], (TOKENS, D), 1.0, 6.0, ((0, 32),))
    segment_ids = jnp.searchsorted(jnp.cumsum(ragged_sizes(keys[1], TOKENS * 2 // SEQ_LEN, TOKENS, SEQ_LEN, 2)), jnp.arange(TOKENS), side="right").astype(jnp.int32)
    expert_ids_keys = jax.random.split(jax.random.fold_in(keys[2], 1), TOKENS // TOK_DEV)
    expert_ids_turns = jax.random.permutation(jax.random.fold_in(keys[2], 3), TOKENS // TOK_DEV)
    expert_ids = jax.vmap(lambda own, number: shared_out(jax.random.fold_in(keys[2], 2), own, number, TOK_DEV, EXPERTS, TOP, CAP, 2))(expert_ids_keys, expert_ids_turns).reshape((TOKENS, TOP))
    w_query = normal_values(keys[3], (D, HEADS * HEAD_DIM), (D // 12) ** -0.5, 0.5, ((0, 32),))
    w_key_value = normal_values(keys[4], (D, 2 * KV_HEADS * HEAD_DIM), (D // 12) ** -0.5, 0.5, ((0, 32),))
    w_out = normal_values(keys[5], (HEADS * HEAD_DIM, D), (HEADS // 2) ** -0.5, 1.75, ((1, 32),))
    w_router = normal_values(keys[6], (D, EXPERTS), (4 * D) ** -0.5, 0.078125, ((0, 32),))
    norm_attn = jnp.clip(1.0 + 0.1 * jax.random.normal(keys[7], (D,), jnp.float32), 0.5, 1.5).astype(jnp.bfloat16)
    norm_moe = jnp.clip(1.0 + 0.1 * jax.random.normal(keys[8], (D,), jnp.float32), 0.5, 1.5).astype(jnp.bfloat16)
    w_gate_up = normal_values(keys[9], (EXPERTS, D, 2 * FF), D ** -0.5, 0.15625, ((0, 8),))
    w_down = normal_values(keys[10], (EXPERTS, FF, D), 1.0, 6.0, ((0, 8),))
    grad_out = bell_draw_with(keys[11], (TOKENS, D), 1.0, 6.0, ((0, 32),), (0, 1, 32, 2.75))
    return {"tokens": tokens, "segment_ids": segment_ids, "expert_ids": expert_ids, "w_query": w_query, "w_key_value": w_key_value, "w_out": w_out, "w_router": w_router, "norm_attn": norm_attn, "norm_moe": norm_moe, "w_gate_up": w_gate_up, "w_down": w_down, "grad_out": grad_out}


@jax.custom_vjp
def low(v):
    return lax.optimization_barrier(v.astype(jnp.bfloat16)).astype(jnp.float32)

@jax.custom_vjp
def low_back(v):
    return v

def low_keep(v):
    return (low(v), None)

def low_pass(kept, grad):
    return (grad,)

def back_keep(v):
    return (v, None)

def back_low(kept, grad):
    return (low(grad),)
low.defvjp(low_keep, low_pass)
low_back.defvjp(back_keep, back_low)
HIGHEST_PREC = lax.Precision.HIGHEST
RESIDUAL = 0.22
ATTN_SCALE = 0.015625
EPSILON = 1e-06
ROPE_BASE = 10000.0
MASKED = -1e+30

def rms_scale(values, gain_vec):
    return values * lax.rsqrt(lax.optimization_barrier(jnp.mean(values * values, axis=-1, keepdims=True)) + EPSILON) * gain_vec

def rope_tables(position):
    half_dim = HEAD_DIM // 2
    frequency = ROPE_BASE ** (-(jnp.arange(half_dim, dtype=jnp.float32) * 2.0 / HEAD_DIM))
    angles = position.astype(jnp.float32)[:, None] * frequency[None, :]
    return (jnp.cos(angles), jnp.sin(angles))

def rotate(flat_rows, cosine, sine_table):
    row_count = flat_rows.shape[0]
    pieces = flat_rows.reshape(row_count, -1, HEAD_DIM)
    half_dim = HEAD_DIM // 2
    first_half = pieces[..., :half_dim]
    second_half = pieces[..., half_dim:]
    cos_part = cosine[:, None, :]
    sin_part = sine_table[:, None, :]
    turned = jnp.concatenate([first_half * cos_part - second_half * sin_part, second_half * cos_part + first_half * sin_part], axis=-1)
    return turned.reshape(row_count, -1)

def attend_block(query_block, query_seg, query_pos, key_rows, value_rows, key_seg, key_pos):
    group_size = HEADS // KV_HEADS
    block_rows = query_block.shape[0]
    query_heads = query_block.reshape(block_rows, KV_HEADS, group_size, HEAD_DIM)
    key_heads = key_rows.reshape(-1, KV_HEADS, HEAD_DIM)
    value_heads = value_rows.reshape(-1, KV_HEADS, HEAD_DIM)
    raw_scores = low_back(jnp.einsum('qngd,knd->ngqk', query_heads, key_heads, precision=HIGHEST_PREC))
    allowed = (query_seg[:, None] == key_seg[None, :]) & (query_pos[:, None] >= key_pos[None, :]) & (query_pos[:, None] // SEQ_LEN == key_pos[None, :] // SEQ_LEN)
    scores = jnp.where(allowed[None, None], raw_scores * ATTN_SCALE, MASKED)
    largest = lax.optimization_barrier(jnp.max(scores, axis=-1, keepdims=True))
    exponent = jnp.exp(scores - largest)
    probability = exponent / lax.optimization_barrier(jnp.sum(exponent, axis=-1, keepdims=True))
    mixed = jnp.einsum('ngqk,knd->qngd', low(probability), value_heads, precision=HIGHEST_PREC)
    return mixed.reshape(block_rows, HEADS * HEAD_DIM)

def slot_index(route_ids):
    one_hot = (route_ids[..., None] == jnp.arange(EXPERTS, dtype=jnp.int32)).astype(jnp.int32)
    rank_table = jnp.cumsum(one_hot, axis=-2) - 1
    slot_number = lax.optimization_barrier(jnp.sum(rank_table * one_hot, axis=-1))
    return (route_ids * CAP + slot_number).astype(jnp.int32)

def block_forward(tokens_f, w_query, w_key_value, w_out, w_router, norm_attn, norm_moe, w_gate_up, w_down, seg_ids, route_ids, start):
    token_count = tokens_f.shape[0]
    token_pos = start + jnp.arange(token_count, dtype=jnp.int32)
    cosine, sine_table = rope_tables(token_pos % SEQ_LEN)
    normed = low(rms_scale(tokens_f, norm_attn))
    queries = low_back(jnp.dot(normed, w_query, precision=HIGHEST_PREC))
    key_value = jnp.dot(normed, w_key_value, precision=HIGHEST_PREC)
    pair_width = KV_HEADS * HEAD_DIM
    keys_raw = low_back(key_value[:, :pair_width])
    values_low = low(low_back(key_value[:, pair_width:]))
    queries_low = low(rotate(queries, cosine, sine_table))
    keys_low = low(rotate(keys_raw, cosine, sine_table))
    block_rows = min(512, token_count)
    checked = jax.checkpoint(attend_block)

    def one_block(block_index):
        row_start = block_index * block_rows
        return checked(lax.dynamic_slice_in_dim(queries_low, row_start, block_rows, 0), lax.dynamic_slice_in_dim(seg_ids, row_start, block_rows, 0), lax.dynamic_slice_in_dim(token_pos, row_start, block_rows, 0), keys_low, values_low, seg_ids, token_pos)
    attended = lax.map(one_block, jnp.arange(token_count // block_rows, dtype=jnp.int32)).reshape(token_count, HEADS * HEAD_DIM)
    mixed_low = low(low_back(attended))
    after_attn = tokens_f + RESIDUAL * low_back(jnp.dot(mixed_low, w_out, precision=HIGHEST_PREC))
    normed_moe = low(rms_scale(after_attn, norm_moe))
    logits = low_back(jnp.dot(normed_moe, w_router, precision=HIGHEST_PREC))
    chosen = jnp.take_along_axis(logits, route_ids, axis=1)
    gate_weights = jax.nn.softmax(chosen, axis=-1)
    block_count = token_count // TOK_DEV
    targets = slot_index(route_ids.reshape(block_count, TOK_DEV * TOP))
    routed = low_back(jnp.repeat(normed_moe, TOP, axis=0)).reshape(block_count, TOK_DEV * TOP, D)
    buffers = jax.vmap(lambda target, rows_in: jnp.zeros((EXPERTS * CAP, D), jnp.float32).at[target].set(rows_in))(targets, routed)
    buffers = buffers.reshape(block_count, EXPERTS, CAP, D)
    gate_up = low_back(jnp.einsum('becd,edf->becf', buffers, w_gate_up, precision=HIGHEST_PREC))
    activated = low(jax.nn.silu(gate_up[..., :FF]) * gate_up[..., FF:])
    expert_out = low(low_back(jnp.einsum('becf,efd->becd', activated, w_down, precision=HIGHEST_PREC)))
    returned = jax.vmap(lambda table_rows, target: table_rows[target])(expert_out.reshape(block_count, EXPERTS * CAP, D), targets)
    returned = returned.reshape(token_count, TOP, D)
    combined = lax.optimization_barrier(jnp.sum(gate_weights[:, :, None] * returned, axis=1))
    return after_attn + RESIDUAL * combined

def reference(tokens, segment_ids, expert_ids, w_query, w_key_value, w_out, w_router, norm_attn, norm_moe, w_gate_up, w_down, grad_out):
    weights = tuple((weight.astype(jnp.float32) for weight in (w_query, w_key_value, w_out, w_router, norm_attn, norm_moe, w_gate_up, w_down)))
    group_rows = TOK_DEV * N_EXPERT

    def one_group(totals, group_index):
        row_start = group_index * group_rows
        piece = lax.dynamic_slice_in_dim(tokens, row_start, group_rows, 0).astype(jnp.float32)
        seg_piece = lax.dynamic_slice_in_dim(segment_ids, row_start, group_rows, 0)
        route_piece = lax.dynamic_slice_in_dim(expert_ids, row_start, group_rows, 0)
        cotangent = lax.dynamic_slice_in_dim(grad_out, row_start, group_rows, 0).astype(jnp.float32)

        def forward(tokens_f, wq_f, wkv_f, wo_f, wr_f, gain_one, gain_two, wgu_f, wd_f):
            return block_forward(tokens_f, wq_f, wkv_f, wo_f, wr_f, gain_one, gain_two, wgu_f, wd_f, seg_piece, route_piece, row_start)
        output, pull_back = jax.vjp(forward, piece, *weights)
        gradients = pull_back(cotangent)
        new_totals = tuple((total_sum + gradient for total_sum, gradient in zip(totals, gradients[1:])))
        return (new_totals, (output.astype(jnp.bfloat16), gradients[0].astype(jnp.bfloat16)))
    zero_totals = tuple((jnp.zeros(weight.shape, jnp.float32) for weight in weights))
    totals, (outputs, input_grads) = lax.scan(one_group, zero_totals, jnp.arange(TOKENS // group_rows, dtype=jnp.int32))
    return (outputs.reshape(TOKENS, D), input_grads.reshape(TOKENS, D), totals[0], totals[1], totals[2], totals[3], totals[4], totals[5], totals[6], totals[7])
```

```python
import functools

import jax
import jax.numpy as jnp
from jax import lax
from jax.experimental import pallas as pl
from jax.experimental.pallas import tpu as pltpu
from jax.sharding import PartitionSpec as P

D = 1536
HEADS = 24
KV_HEADS = 8
HEAD_DIM = 64
FF = 512
TOP = 8
EXP_DEV = 2

RESIDUAL = 0.22
ATTN_SCALE = 0.015625
LOG2E = 1.4426950408889634
EPSILON = 1e-06
ROPE_BASE = 10000.0
MASKED = -1e30

GROUP = HEADS // KV_HEADS
HALF = HEAD_DIM // 2
BLK = 256
BF = jnp.bfloat16
F32 = jnp.float32
BOTH = ("dp", "expert")


def dot(a, b, ca, cb):
    return lax.dot_general(a, b, (((ca,), (cb,)), ((), ())), preferred_element_type=F32)


def rms_scale(values, gain_vec):
    return (
        values * lax.rsqrt(jnp.mean(values * values, axis=-1, keepdims=True) + EPSILON) * gain_vec
    )


def rotate_t(rows_t, cosine, sine):
    pieces = rows_t.reshape(-1, 2, HALF, rows_t.shape[1])
    first, second = pieces[:, 0], pieces[:, 1]
    turned = jnp.stack(
        [first * cosine - second * sine, second * cosine + first * sine], axis=1
    )
    return turned.reshape(rows_t.shape)


def side_by_side(block):
    return jnp.concatenate(
        [block[h * HEAD_DIM : (h + 1) * HEAD_DIM] for h in range(GROUP)], axis=1
    )


def stacked(wide):
    width = wide.shape[1] // GROUP
    return jnp.concatenate([wide[:, h * width : (h + 1) * width] for h in range(GROUP)], axis=0)


def allowed_keys(start_ref, block, key_block):
    lane = lax.broadcasted_iota(jnp.int32, (1, BLK), 1) + block * BLK
    reach = lane - start_ref[...]
    lane3 = jnp.concatenate([lane] * GROUP, axis=1)
    reach3 = jnp.concatenate([reach] * GROUP, axis=1)
    key_pos = lax.broadcasted_iota(jnp.int32, (BLK, 1), 0) + key_block * BLK
    back = lane3 - key_pos
    return (back >= 0) & (back <= reach3)


def attn_fwd_kernel(first_ref, q_ref, k_ref, vt_ref, start_ref, a_ref, o_ref, lse_ref):
    block = pl.program_id(0)
    query = side_by_side(q_ref[...])
    width = GROUP * BLK

    def step(key_block, carry):
        largest, total, acc = carry
        keys = k_ref[pl.ds(pl.multiple_of(key_block * BLK, BLK), BLK), :]
        values = vt_ref[:, pl.ds(pl.multiple_of(key_block * BLK, BLK), BLK)]
        scores = dot(keys, query, 1, 0) * (ATTN_SCALE * LOG2E)
        scores = jnp.where(allowed_keys(start_ref, block, key_block), scores, MASKED)
        now = jnp.maximum(largest, jnp.max(scores, axis=0, keepdims=True))
        power = jnp.exp2(scores - now)
        fade = jnp.exp2(largest - now)
        total = total * fade + jnp.sum(power, axis=0, keepdims=True)
        acc = acc * fade + dot(values, power.astype(BF), 1, 0)
        return now, total, acc

    largest, total, acc = lax.fori_loop(
        first_ref[block],
        block + 1,
        step,
        (
            jnp.full((1, width), MASKED, F32),
            jnp.zeros((1, width), F32),
            jnp.zeros((HEAD_DIM, width), F32),
        ),
    )
    out = stacked(acc / total)
    o_ref[...] = out
    a_ref[...] = out.astype(BF)
    lse = largest + jnp.log2(total)
    lse_ref[...] = jnp.concatenate(
        [lse[:, h * BLK : (h + 1) * BLK] for h in range(GROUP)]
        + [jnp.zeros((8 - GROUP, BLK), F32)],
        axis=0,
    )


def attn_bwd_kernel(
    first_ref, q_ref, da_ref, o_ref, lse_ref, k_ref, kt_ref, v_ref, start_ref,
    dq_ref, dk_ref, dv_ref, dk_acc, dv_acc,
):
    block = pl.program_id(0)

    @pl.when(block == 0)
    def _():
        dk_acc[...] = jnp.zeros_like(dk_acc)
        dv_acc[...] = jnp.zeros_like(dv_acc)

    query_t = side_by_side(q_ref[...])
    query = query_t.astype(F32).T.astype(BF)
    grad_t = side_by_side(da_ref[0])
    grad_f = grad_t.astype(F32)
    grad = grad_f.T.astype(BF)
    delta = jnp.sum(side_by_side(o_ref[...]) * grad_f, axis=0, keepdims=True)
    lse = jnp.concatenate([lse_ref[h : h + 1, :] for h in range(GROUP)], axis=1)

    def step(key_block, dq):
        rows = pl.ds(pl.multiple_of(key_block * BLK, BLK), BLK)
        keys = k_ref[rows, :]
        scores = dot(keys, query_t, 1, 0) * (ATTN_SCALE * LOG2E)
        scores = jnp.where(allowed_keys(start_ref, block, key_block), scores, MASKED)
        prob = jnp.exp2(scores - lse)
        grad_prob = dot(v_ref[rows, :], grad_t, 1, 0)
        grad_score = (prob * (grad_prob - delta) * ATTN_SCALE).astype(BF)
        dv_acc[rows, :] += dot(prob.astype(BF), grad, 1, 0)
        dk_acc[rows, :] += dot(grad_score, query, 1, 0)
        return dq + dot(kt_ref[:, rows], grad_score, 1, 0)

    dq = lax.fori_loop(
        first_ref[block], block + 1, step, jnp.zeros((HEAD_DIM, GROUP * BLK), F32)
    )
    dq_ref[...] = stacked(dq)

    @pl.when(block == pl.num_programs(0) - 1)
    def _():
        dk_ref[...] = dk_acc[...].T
        dv_ref[...] = dv_acc[...].T


def attn_forward(first, q_t, k, v_t, start):
    seq = q_t.shape[1]
    rows = GROUP * HEAD_DIM
    column = lambda g, first: (0, g)
    whole = lambda g, first: (0, 0)
    return pl.pallas_call(
        attn_fwd_kernel,
        grid_spec=pltpu.PrefetchScalarGridSpec(
            num_scalar_prefetch=1,
            grid=(seq // BLK,),
            in_specs=[
                pl.BlockSpec((rows, BLK), column),
                pl.BlockSpec((seq, HEAD_DIM), whole),
                pl.BlockSpec((HEAD_DIM, seq), whole),
                pl.BlockSpec((1, BLK), column),
            ],
            out_specs=[
                pl.BlockSpec((rows, BLK), column),
                pl.BlockSpec((rows, BLK), column),
                pl.BlockSpec((8, BLK), column),
            ],
        ),
        out_shape=[
            jax.ShapeDtypeStruct((rows, seq), BF),
            jax.ShapeDtypeStruct((rows, seq), F32),
            jax.ShapeDtypeStruct((8, seq), F32),
        ],
        cost_estimate=pl.CostEstimate(
            flops=4 * rows * seq * seq, bytes_accessed=8 * rows * seq, transcendentals=GROUP * seq * seq
        ),
        name="attn_fwd",
    )(first, q_t, k, v_t, start)


def attn_backward(first, q_t, da, o_t, lse, k, k_t, v, start):
    seq = q_t.shape[1]
    rows = GROUP * HEAD_DIM
    column = lambda g, first: (0, g)
    whole = lambda g, first: (0, 0)
    return pl.pallas_call(
        attn_bwd_kernel,
        grid_spec=pltpu.PrefetchScalarGridSpec(
            num_scalar_prefetch=1,
            grid=(seq // BLK,),
            in_specs=[
                pl.BlockSpec((rows, BLK), column),
                pl.BlockSpec((1, rows, BLK), lambda g, first: (g, 0, 0)),
                pl.BlockSpec((rows, BLK), column),
                pl.BlockSpec((8, BLK), column),
                pl.BlockSpec((seq, HEAD_DIM), whole),
                pl.BlockSpec((HEAD_DIM, seq), whole),
                pl.BlockSpec((seq, HEAD_DIM), whole),
                pl.BlockSpec((1, BLK), column),
            ],
            out_specs=[
                pl.BlockSpec((rows, BLK), column),
                pl.BlockSpec((HEAD_DIM, seq), whole),
                pl.BlockSpec((HEAD_DIM, seq), whole),
            ],
            scratch_shapes=[
                pltpu.VMEM((seq, HEAD_DIM), F32),
                pltpu.VMEM((seq, HEAD_DIM), F32),
            ],
        ),
        out_shape=[
            jax.ShapeDtypeStruct((rows, seq), F32),
            jax.ShapeDtypeStruct((HEAD_DIM, seq), F32),
            jax.ShapeDtypeStruct((HEAD_DIM, seq), F32),
        ],
        cost_estimate=pl.CostEstimate(
            flops=10 * rows * seq * seq, bytes_accessed=12 * rows * seq, transcendentals=GROUP * seq * seq
        ),
        name="attn_bwd",
    )(first, q_t, da, o_t, lse, k, k_t, v, start)


def swap(values, bit):
    count = lax.axis_size("expert")
    return lax.ppermute(values, "expert", [(i, i ^ bit) for i in range(count)])


def scatter_sum(partial):
    me = lax.axis_index("expert")
    core, chip = me % 2, me // 2
    rows = partial.shape[0] // 8
    half = rows // 2
    terms = partial.reshape(4, 2, rows, -1)
    keep = lax.dynamic_index_in_dim(terms, core, 1, False)
    give = lax.dynamic_index_in_dim(terms, 1 - core, 1, False)
    got = swap(give, 1)

    def pair(which, low, high):
        a = lax.dynamic_index_in_dim(keep, chip ^ which, 0, False)[low:high]
        b = lax.dynamic_index_in_dim(got, chip ^ which, 0, False)[low:high]
        return a.astype(F32) + b.astype(F32)

    far_a = swap(pair(3, 0, half).astype(BF), 2)
    far_b = swap(pair(3, half, rows).astype(BF), 4)
    via_y = jnp.concatenate(
        [pair(2, 0, half) + far_a.astype(F32), pair(2, half, rows)], axis=0
    ).astype(BF)
    via_x = jnp.concatenate(
        [pair(1, 0, half), pair(1, half, rows) + far_b.astype(F32)], axis=0
    ).astype(BF)
    from_y = swap(via_y, 4)
    from_x = swap(via_x, 2)
    return pair(0, 0, rows) + from_x.astype(F32) + from_y.astype(F32)


def exchange(blocks, axes):
    return lax.all_to_all(blocks, axes, split_axis=0, concat_axis=0, tiled=True)


def shards(
    tokens,
    segment_ids,
    expert_ids,
    w_query,
    w_key_value,
    w_out,
    w_router,
    norm_attn,
    norm_moe,
    w_gate_up,
    w_down,
    grad_out,
):
    tok_rows = tokens.shape[0]
    members = lax.axis_size("expert")
    groups = lax.axis_size("dp")
    position = lax.axis_index("expert")
    devices = groups * members
    seq = tok_rows * members
    expert_total = EXP_DEV * members
    in_rows = w_query.shape[0]
    q_cols = GROUP * HEAD_DIM
    kv_cols = KV_HEADS * HEAD_DIM
    qkv_cols = q_cols + 2 * HEAD_DIM

    own = jnp.concatenate(
        [
            w_query.reshape(in_rows, members, q_cols),
            w_key_value[:, :kv_cols].reshape(in_rows, members, HEAD_DIM),
            w_key_value[:, kv_cols:].reshape(in_rows, members, HEAD_DIM),
            jnp.broadcast_to(
                jnp.concatenate(
                    [
                        w_router,
                        norm_attn[:, None],
                        norm_moe[:, None],
                        jnp.zeros((in_rows, 64 - expert_total - 2), BF),
                    ],
                    axis=1,
                )[:, None, :],
                (in_rows, members, 64),
            ),
        ],
        axis=2,
    )
    own = jnp.moveaxis(own, 1, 0)
    own = jnp.broadcast_to(own[None], (groups,) + own.shape).reshape(devices, in_rows, -1)
    weights = exchange(own, BOTH).reshape(D, -1)
    w_qkv = weights[:, :qkv_cols]
    full_router = weights[:, qkv_cols : qkv_cols + expert_total]
    gain_attn = weights[:, qkv_cols + expert_total].astype(F32)
    gain_moe = weights[:, qkv_cols + expert_total + 1].astype(F32)

    x_all = lax.all_gather(tokens, "expert", axis=0, tiled=True)
    ids_t = exchange(
        jnp.broadcast_to(expert_ids.T[None], (members, TOP, tok_rows)), "expert"
    )
    out_t = lax.all_gather(w_out.T, BOTH, axis=0, tiled=True)
    dy_all = lax.all_gather(grad_out, "expert", axis=0, tiled=True)

    token_pos = jnp.arange(seq, dtype=jnp.int32)
    start = jnp.sum(
        (segment_ids[:, None] < segment_ids[None, :]).astype(jnp.int32), axis=0, keepdims=True
    )
    first = start[0, ::BLK] // BLK
    frequency = ROPE_BASE ** (-(jnp.arange(HALF, dtype=F32) * 2.0 / HEAD_DIM))
    angles = frequency[:, None] * token_pos.astype(F32)[None, :]
    cosine, sine = jnp.cos(angles), jnp.sin(angles)

    normed = rms_scale(x_all.astype(F32), gain_attn).astype(BF)
    qkv_t = dot(w_qkv, normed, 0, 1)
    qk_t = rotate_t(qkv_t[: q_cols + HEAD_DIM], cosine, sine).astype(BF)
    q_t, k_t = qk_t[:q_cols], qk_t[q_cols:]
    v_t = qkv_t[q_cols + HEAD_DIM :].astype(BF)
    k, v = k_t.T, v_t.T
    a_t, o_t, lse = attn_forward(first, q_t, k, v_t, start)
    a_all = lax.all_gather(a_t, "expert", axis=0, tiled=True)

    after_attn = x_all.astype(F32) + RESIDUAL * dot(a_all, out_t, 0, 1)
    h2 = rms_scale(after_attn, gain_moe).astype(BF)
    logits = dot(full_router, h2, 0, 1)
    ids = jnp.moveaxis(ids_t.reshape(members, TOP, tok_rows), 1, 0).reshape(TOP, 1, seq)
    chosen = jnp.any(ids == jnp.arange(expert_total, dtype=jnp.int32)[None, :, None], axis=0)
    masked = jnp.where(chosen, logits, MASKED)
    power = jnp.where(chosen, jnp.exp(masked - jnp.max(masked, axis=0, keepdims=True)), 0.0)
    gates_t = power / jnp.sum(power, axis=0, keepdims=True)
    own_gates = RESIDUAL * lax.dynamic_slice_in_dim(gates_t, position * EXP_DEV, EXP_DEV, 0)

    parts, d_parts, up_wgrads, down_wgrads, gate_grads = [], [], [], [], []
    for e in range(EXP_DEV):
        gate = own_gates[e][:, None]
        gate_up = dot(h2, w_gate_up[e], 1, 0)
        back = dot(dy_all, w_down[e], 1, 1)
        g, u = gate_up[:, :FF], gate_up[:, FF:]
        sig = jax.nn.sigmoid(g)
        act = g * sig * u
        gate_grads.append(RESIDUAL * jnp.sum(act * back, axis=1))
        parts.append((gate * act).astype(BF))
        dact = gate * back
        dgu = jnp.concatenate(
            [dact * u * sig * (1.0 + g * (1.0 - sig)), dact * g * sig], axis=1
        ).astype(BF)
        d_parts.append(dgu)
        down_wgrads.append(dot(parts[e], dy_all, 0, 0).astype(BF))
        up_wgrads.append(dot(h2, dgu, 0, 0).astype(BF))
    out_part = dot(
        jnp.concatenate(parts, axis=1), w_down.reshape(EXP_DEV * FF, D), 1, 0
    ).astype(BF)
    dh2_part = sum(dot(d_parts[e], w_gate_up[e], 1, 1) for e in range(EXP_DEV)).astype(BF)

    down_share = lax.psum_scatter(
        jnp.stack(down_wgrads), "dp", scatter_dimension=2, tiled=True
    ).astype(F32)
    up_share = lax.psum_scatter(
        jnp.stack(up_wgrads), "dp", scatter_dimension=1, tiled=True
    ).astype(F32)

    gate_grads = jnp.moveaxis(
        jnp.stack(gate_grads).reshape(EXP_DEV, members, tok_rows), 1, 0
    )
    gate_grads_t = exchange(gate_grads, "expert").reshape(expert_total, tok_rows)
    dh2_moe = scatter_sum(dh2_part)
    combined = scatter_sum(out_part)

    row0 = position * tok_rows
    y1 = lax.dynamic_slice_in_dim(after_attn, row0, tok_rows, 0)
    h2_own = lax.dynamic_slice_in_dim(h2, row0, tok_rows, 0)
    gates_own = lax.dynamic_slice_in_dim(gates_t, row0, tok_rows, 1)
    result = (y1 + combined).astype(BF)

    mean_grad = jnp.sum(gates_own * gate_grads_t, axis=0, keepdims=True)
    dlogits_t = (gates_own * (gate_grads_t - mean_grad)).astype(BF)
    router_wgrad = dot(h2_own, dlogits_t, 0, 1)
    dh2 = dh2_moe + dot(dlogits_t, full_router, 0, 1)
    _, moe_pull = jax.vjp(rms_scale, y1, gain_moe)
    dy1_norm, moe_gain_grad = moe_pull(dh2)
    dy1 = grad_out.astype(F32) + dy1_norm
    db = (RESIDUAL * dy1).astype(BF)
    da_t = dot(out_t, db, 0, 1).astype(BF)
    da = exchange(da_t.reshape(members, q_cols, tok_rows), "expert")

    out_cols = w_out.shape[1]
    db_cols = exchange(
        jnp.moveaxis(db.reshape(tok_rows, groups, members, out_cols), 2, 0).reshape(
            members, tok_rows, groups * out_cols
        ),
        "expert",
    ).reshape(seq, groups * out_cols)
    out_wgrad = dot(db_cols, a_all, 0, 1).astype(BF).reshape(groups, out_cols, D)
    out_share = jnp.sum(exchange(out_wgrad, "dp").astype(F32), axis=0).T

    dq_t, dk_t, dv_t = attn_backward(first, q_t, da, o_t, lse, k, k_t, v, start)
    dqk_t = rotate_t(jnp.concatenate([dq_t, dk_t], axis=0), cosine, -sine)
    dqkv_t = jnp.concatenate([dqk_t, dv_t], axis=0).astype(BF)
    dh1_part = dot(dqkv_t, w_qkv, 0, 1).astype(BF)
    dh1 = scatter_sum(dh1_part)
    qkv_wgrad = dot(normed, dqkv_t, 0, 1).astype(BF)

    def split(values):
        high = values.astype(BF)
        return [high, (values - high.astype(F32)).astype(BF)]

    sent = jnp.concatenate(
        [qkv_wgrad]
        + split(router_wgrad)
        + split(moe_gain_grad[:, None])
        + [jnp.zeros((D, 64 - 2 * expert_total - 2), BF)],
        axis=1,
    )
    came = exchange(sent.reshape(devices, in_rows, -1), BOTH)
    came = jnp.sum(
        came.reshape(groups, members, in_rows, -1).astype(F32), axis=0
    )
    query_share = jnp.moveaxis(came[:, :, :q_cols], 0, 1).reshape(in_rows, members * q_cols)
    key_share = jnp.moveaxis(came[:, :, q_cols : q_cols + HEAD_DIM], 0, 1).reshape(in_rows, kv_cols)
    value_share = jnp.moveaxis(came[:, :, q_cols + HEAD_DIM : qkv_cols], 0, 1).reshape(
        in_rows, kv_cols
    )
    rest = jnp.sum(came[:, :, qkv_cols:], axis=0)
    router_share = rest[:, :expert_total] + rest[:, expert_total : 2 * expert_total]
    moe_gain_share = rest[:, 2 * expert_total] + rest[:, 2 * expert_total + 1]

    x_own = tokens.astype(F32)
    _, attn_pull = jax.vjp(rms_scale, x_own, gain_attn)
    dx_norm, attn_gain_grad = attn_pull(dh1)
    token_grad = (dy1 + dx_norm).astype(BF)
    gain_rows = jnp.pad(attn_gain_grad.reshape(devices, in_rows), ((0, 0), (0, 128 - in_rows)))
    attn_gain_share = jnp.sum(exchange(gain_rows, BOTH), axis=0)[:in_rows]

    return (
        result,
        token_grad,
        query_share,
        jnp.concatenate([key_share, value_share], axis=1),
        out_share,
        router_share,
        attn_gain_share,
        moe_gain_share,
        up_share,
        down_share,
    )


def solution(mesh):
    in_specs = (
        P(("dp", "expert"), None),
        P("dp"),
        P(("dp", "expert"), None),
        P(("dp", "expert"), None),
        P(("dp", "expert"), None),
        P(None, ("dp", "expert")),
        P(("dp", "expert"), None),
        P(("dp", "expert")),
        P(("dp", "expert")),
        P("expert", None, None),
        P("expert", None, None),
        P(("dp", "expert"), None),
    )
    out_specs = (
        P(("dp", "expert"), None),
        P(("dp", "expert"), None),
        P(("dp", "expert"), None),
        P(("dp", "expert"), None),
        P(None, ("dp", "expert")),
        P(("dp", "expert"), None),
        P(("dp", "expert")),
        P(("dp", "expert")),
        P("expert", "dp", None),
        P("expert", None, "dp"),
    )
    return jax.shard_map(shards, mesh=mesh, in_specs=in_specs, out_specs=out_specs, check_vma=False)
```

```python
import functools

import jax
import jax.numpy as jnp
from jax import lax
from jax.experimental import pallas as pl
from jax.experimental.pallas import tpu as pltpu
from jax.sharding import PartitionSpec as P

D = 1536
HEADS = 24
KV_HEADS = 8
HEAD_DIM = 64
FF = 512
TOP = 8
EXP_DEV = 2

RESIDUAL = 0.22
ATTN_SCALE = 0.015625
LOG2E = 1.4426950408889634
EPSILON = 1e-06
ROPE_BASE = 10000.0
MASKED = -1e30

GROUP = HEADS // KV_HEADS
HALF = HEAD_DIM // 2
BLK = 256
BF = jnp.bfloat16
F32 = jnp.float32
BOTH = ("dp", "expert")


def dot(a, b, ca, cb):
    return lax.dot_general(a, b, (((ca,), (cb,)), ((), ())), preferred_element_type=F32)


def rms_scale(values, gain_vec):
    return (
        values * lax.rsqrt(jnp.mean(values * values, axis=-1, keepdims=True) + EPSILON) * gain_vec
    )


def side_by_side(block):
    return jnp.concatenate(
        [block[h * HEAD_DIM : (h + 1) * HEAD_DIM] for h in range(GROUP)], axis=1
    )


def stacked(wide):
    width = wide.shape[1] // GROUP
    return jnp.concatenate([wide[:, h * width : (h + 1) * width] for h in range(GROUP)], axis=0)


def allowed_keys(start_ref, block, key_block):
    lane = lax.broadcasted_iota(jnp.int32, (1, BLK), 1) + block * BLK
    reach = lane - start_ref[...]
    lane3 = jnp.concatenate([lane] * GROUP, axis=1)
    reach3 = jnp.concatenate([reach] * GROUP, axis=1)
    key_pos = lax.broadcasted_iota(jnp.int32, (BLK, 1), 0) + key_block * BLK
    back = lane3 - key_pos
    return (back >= 0) & (back <= reach3)


def attn_fwd_kernel(first_ref, q_ref, k_ref, vt_ref, start_ref, a_ref, o_ref, lse_ref):
    block = pl.program_id(0)
    query = side_by_side(q_ref[...])
    width = GROUP * BLK

    def step(key_block, carry):
        largest, total, acc = carry
        keys = k_ref[pl.ds(pl.multiple_of(key_block * BLK, BLK), BLK), :]
        values = vt_ref[:, pl.ds(pl.multiple_of(key_block * BLK, BLK), BLK)]
        scores = dot(keys, query, 1, 0) * (ATTN_SCALE * LOG2E)
        scores = jnp.where(allowed_keys(start_ref, block, key_block), scores, MASKED)
        now = jnp.maximum(largest, jnp.max(scores, axis=0, keepdims=True))
        power = jnp.exp2(scores - now)
        fade = jnp.exp2(largest - now)
        total = total * fade + jnp.sum(power, axis=0, keepdims=True)
        acc = acc * fade + dot(values, power.astype(BF), 1, 0)
        return now, total, acc

    largest, total, acc = lax.fori_loop(
        first_ref[block],
        block + 1,
        step,
        (
            jnp.full((1, width), MASKED, F32),
            jnp.zeros((1, width), F32),
            jnp.zeros((HEAD_DIM, width), F32),
        ),
    )
    out = stacked(acc / total)
    o_ref[...] = out
    a_ref[...] = out.astype(BF)
    lse = largest + jnp.log2(total)
    lse_ref[...] = jnp.concatenate(
        [lse[:, h * BLK : (h + 1) * BLK] for h in range(GROUP)]
        + [jnp.zeros((8 - GROUP, BLK), F32)],
        axis=0,
    )


def attn_bwd_kernel(
    first_ref, q_ref, da_ref, o_ref, lse_ref, k_ref, kt_ref, v_ref, start_ref,
    dq_ref, dk_ref, dv_ref, dk_acc, dv_acc,
):
    block = pl.program_id(0)

    @pl.when(block == 0)
    def _():
        dk_acc[...] = jnp.zeros_like(dk_acc)
        dv_acc[...] = jnp.zeros_like(dv_acc)

    query_t = side_by_side(q_ref[...])
    query = query_t.astype(F32).T.astype(BF)
    grad_t = side_by_side(da_ref[0])
    grad_f = grad_t.astype(F32)
    grad = grad_f.T.astype(BF)
    delta = jnp.sum(side_by_side(o_ref[...]) * grad_f, axis=0, keepdims=True)
    lse = jnp.concatenate([lse_ref[h : h + 1, :] for h in range(GROUP)], axis=1)

    def step(key_block, dq):
        rows = pl.ds(pl.multiple_of(key_block * BLK, BLK), BLK)
        keys = k_ref[rows, :]
        scores = dot(keys, query_t, 1, 0) * (ATTN_SCALE * LOG2E)
        scores = jnp.where(allowed_keys(start_ref, block, key_block), scores, MASKED)
        prob = jnp.exp2(scores - lse)
        grad_prob = dot(v_ref[rows, :], grad_t, 1, 0)
        grad_score = (prob * (grad_prob - delta) * ATTN_SCALE).astype(BF)
        dv_acc[rows, :] += dot(prob.astype(BF), grad, 1, 0)
        dk_acc[rows, :] += dot(grad_score, query, 1, 0)
        return dq + dot(kt_ref[:, rows], grad_score, 1, 0)

    dq = lax.fori_loop(
        first_ref[block], block + 1, step, jnp.zeros((HEAD_DIM, GROUP * BLK), F32)
    )
    dq_ref[...] = stacked(dq)

    @pl.when(block == pl.num_programs(0) - 1)
    def _():
        dk_ref[...] = dk_acc[...].T
        dv_ref[...] = dv_acc[...].T


def attn_forward(first, q_t, k, v_t, start):
    seq = q_t.shape[1]
    rows = GROUP * HEAD_DIM
    column = lambda g, first: (0, g)
    whole = lambda g, first: (0, 0)
    return pl.pallas_call(
        attn_fwd_kernel,
        grid_spec=pltpu.PrefetchScalarGridSpec(
            num_scalar_prefetch=1,
            grid=(seq // BLK,),
            in_specs=[
                pl.BlockSpec((rows, BLK), column),
                pl.BlockSpec((seq, HEAD_DIM), whole),
                pl.BlockSpec((HEAD_DIM, seq), whole),
                pl.BlockSpec((1, BLK), column),
            ],
            out_specs=[
                pl.BlockSpec((rows, BLK), column),
                pl.BlockSpec((rows, BLK), column),
                pl.BlockSpec((8, BLK), column),
            ],
        ),
        out_shape=[
            jax.ShapeDtypeStruct((rows, seq), BF),
            jax.ShapeDtypeStruct((rows, seq), F32),
            jax.ShapeDtypeStruct((8, seq), F32),
        ],
        cost_estimate=pl.CostEstimate(
            flops=4 * rows * seq * seq, bytes_accessed=8 * rows * seq, transcendentals=GROUP * seq * seq
        ),
        name="attn_fwd",
    )(first, q_t, k, v_t, start)


def attn_backward(first, q_t, da, o_t, lse, k, k_t, v, start):
    seq = q_t.shape[1]
    rows = GROUP * HEAD_DIM
    column = lambda g, first: (0, g)
    whole = lambda g, first: (0, 0)
    return pl.pallas_call(
        attn_bwd_kernel,
        grid_spec=pltpu.PrefetchScalarGridSpec(
            num_scalar_prefetch=1,
            grid=(seq // BLK,),
            in_specs=[
                pl.BlockSpec((rows, BLK), column),
                pl.BlockSpec((1, rows, BLK), lambda g, first: (g, 0, 0)),
                pl.BlockSpec((rows, BLK), column),
                pl.BlockSpec((8, BLK), column),
                pl.BlockSpec((seq, HEAD_DIM), whole),
                pl.BlockSpec((HEAD_DIM, seq), whole),
                pl.BlockSpec((seq, HEAD_DIM), whole),
                pl.BlockSpec((1, BLK), column),
            ],
            out_specs=[
                pl.BlockSpec((rows, BLK), column),
                pl.BlockSpec((HEAD_DIM, seq), whole),
                pl.BlockSpec((HEAD_DIM, seq), whole),
            ],
            scratch_shapes=[
                pltpu.VMEM((seq, HEAD_DIM), F32),
                pltpu.VMEM((seq, HEAD_DIM), F32),
            ],
        ),
        out_shape=[
            jax.ShapeDtypeStruct((rows, seq), F32),
            jax.ShapeDtypeStruct((HEAD_DIM, seq), F32),
            jax.ShapeDtypeStruct((HEAD_DIM, seq), F32),
        ],
        cost_estimate=pl.CostEstimate(
            flops=10 * rows * seq * seq, bytes_accessed=12 * rows * seq, transcendentals=GROUP * seq * seq
        ),
        name="attn_bwd",
    )(first, q_t, da, o_t, lse, k, k_t, v, start)


PACK = 384
Q_COLS = GROUP * HEAD_DIM
QKV = Q_COLS + 2 * HEAD_DIM
ROUTE = QKV - 256


def spec(shape, index):
    return pl.BlockSpec(shape, index)


def resident(shape):
    return pl.BlockSpec(
        shape, lambda *_: (0,) * len(shape), pipeline_mode=pl.Buffered(1)
    )


def call(kernel, name, grid, in_specs, out_specs, out_shape, flops, moved, scratch=()):
    return pl.pallas_call(
        kernel,
        grid_spec=pltpu.PrefetchScalarGridSpec(
            num_scalar_prefetch=1,
            grid=grid,
            in_specs=in_specs,
            out_specs=out_specs,
            scratch_shapes=list(scratch),
        ),
        out_shape=out_shape,
        cost_estimate=pl.CostEstimate(flops=flops, bytes_accessed=moved, transcendentals=0),
        name=name,
    )


def shape(dims, kind):
    return jax.ShapeDtypeStruct(dims, kind)


def relative(step, half):
    return jnp.where(step < half, 2 * step + 1, 2 * (step - half))


def owner(step, half, pos):
    return relative(step, half) ^ pos[0]


def give_index(step, half):
    return jnp.minimum(step, half - 1)


def keep_index(step, half):
    return jnp.maximum(step - half, 0)


def turn_rows(rows_t, cosine, sine):
    out = []
    for h in range(rows_t.shape[0] // HEAD_DIM):
        a = rows_t[h * HEAD_DIM : h * HEAD_DIM + HALF]
        b = rows_t[h * HEAD_DIM + HALF : (h + 1) * HEAD_DIM]
        out += [a * cosine - b * sine, b * cosine + a * sine]
    return jnp.concatenate(out, axis=0)


def norm_of(values):
    return values * lax.rsqrt(jnp.mean(values * values, axis=1, keepdims=True) + EPSILON)


def qkv_kernel(count, pos_ref, *refs):
    pieces = refs[: count + 2]
    w_ref, gain_ref, cos_ref, sin_ref, q_ref, kt_ref, vt_ref, k_ref, v_ref = refs[count + 2 :]
    gain = gain_ref[...]
    for r in range(count):
        if r < count - 2:
            rows = pieces[r][...]
        else:
            at = count - 2 + 2 * (r - count + 2)
            rows = jnp.concatenate([pieces[at][...], pieces[at + 1][...]], axis=0)
        normed = (norm_of(rows.astype(F32)) * gain).astype(BF)
        both = dot(normed, w_ref[...], 1, 0)
        turned = both.T
        place = pl.multiple_of((pos_ref[0] ^ r) * BLK, BLK)
        columns = pl.ds(place, BLK)
        cosine, sine = cos_ref[:, columns], sin_ref[:, columns]
        qk = turn_rows(turned[: Q_COLS + HEAD_DIM], cosine, sine)
        q_ref[:, columns] = qk[:Q_COLS].astype(BF)
        kt_ref[:, columns] = qk[Q_COLS:].astype(BF)
        vt_ref[:, columns] = turned[Q_COLS + HEAD_DIM : QKV].astype(BF)
        k_ref[columns, :] = qk[Q_COLS:].T.astype(BF)
        v_ref[columns, :] = both[:, 256 : 256 + HEAD_DIM].astype(BF)


def qkv_forward(pos, pieces, weights, gain, cosine, sine):
    count = len(pieces) - 2
    seq = cosine.shape[1]
    full = lambda a: resident(a.shape)
    return call(
        functools.partial(qkv_kernel, count),
        "qkv",
        (1,),
        [full(a) for a in pieces] + [full(a) for a in (weights, gain, cosine, sine)],
        [resident(s) for s in ((Q_COLS, seq), (HEAD_DIM, seq), (HEAD_DIM, seq), (seq, HEAD_DIM), (seq, HEAD_DIM))],
        [
            shape((Q_COLS, seq), BF),
            shape((HEAD_DIM, seq), BF),
            shape((HEAD_DIM, seq), BF),
            shape((seq, HEAD_DIM), BF),
            shape((seq, HEAD_DIM), BF),
        ],
        2 * seq * D * PACK,
        2 * seq * D,
    )(pos, *pieces, weights, gain, cosine, sine)


def mix_kernel(count, pos_ref, *refs):
    pieces = refs[: count + 2]
    x_ref, w_ref, gain_ref, route_ref, ids_ref = refs[count + 2 : count + 7]
    h2_ref, gates_ref, y1_ref, h2_own_ref, gates_own_ref, heads = refs[count + 7 :]
    block = pl.program_id(0)
    pos = pos_ref[0]
    for r in range(count):
        base = (pos ^ r) * Q_COLS
        if r < count - 2:
            heads[pl.ds(pl.multiple_of(base, Q_COLS), Q_COLS), :] = pieces[r][...]
        else:
            half = Q_COLS // 2
            at = count - 2 + 2 * (r - count + 2)
            heads[pl.ds(pl.multiple_of(base, half), half), :] = pieces[at][...]
            heads[pl.ds(pl.multiple_of(base + half, half), half), :] = pieces[at + 1][...]
    y1 = x_ref[0].astype(F32) + RESIDUAL * dot(heads[...], w_ref[...], 0, 0)
    h2 = (norm_of(y1) * gain_ref[...]).astype(BF)
    logits = dot(h2, route_ref[...], 1, 0)
    lane = lax.broadcasted_iota(jnp.int32, logits.shape, 1) - ROUTE
    ids = ids_ref[...]
    chosen = lane == ids[:, 0:1]
    for k in range(1, TOP):
        chosen = chosen | (lane == ids[:, k : k + 1])
    masked = jnp.where(chosen, logits, MASKED)
    power = jnp.where(chosen, jnp.exp(masked - jnp.max(masked, axis=1, keepdims=True)), 0.0)
    gates = power / jnp.sum(power, axis=1, keepdims=True)
    h2_ref[...] = h2
    gates_ref[...] = gates

    @pl.when(block == pos)
    def _():
        y1_ref[...] = y1
        h2_own_ref[...] = h2
        gates_own_ref[...] = gates


def mix_forward(pos, pieces, x_rel, w_full, gain, weights, ids):
    count = len(pieces) - 2
    seq = ids.shape[0]
    row = lambda s, pos: (s, 0)
    return call(
        functools.partial(mix_kernel, count),
        "mix",
        (seq // BLK,),
        [spec((a.shape[0], BLK), lambda s, pos: (0, s)) for a in pieces]
        + [
            spec((1, BLK, D), lambda s, pos: (s ^ pos[0], 0, 0)),
            resident(w_full.shape),
            resident(gain.shape),
            pl.BlockSpec((D, 128), lambda s, pos: (0, 2), pipeline_mode=pl.Buffered(1)),
            spec((BLK, TOP), row),
        ],
        [
            spec((BLK, D), row),
            spec((BLK, 128), row),
            resident((BLK, D)),
            resident((BLK, D)),
            resident((BLK, 128)),
        ],
        [
            shape((seq, D), BF),
            shape((seq, 128), F32),
            shape((BLK, D), F32),
            shape((BLK, D), BF),
            shape((BLK, 128), F32),
        ],
        2 * seq * D * D,
        10 * seq * D,
        [pltpu.VMEM((HEADS * HEAD_DIM, BLK), BF)],
    )(pos, *pieces, x_rel, w_full, gain, weights, ids)


def expert_kernel(
    half, pos_ref, h2_ref, dy_ref, gates_ref, up_ref, down_ref,
    give_ref, keep_ref, ag_ref, dgu_ref, dg_ref,
):
    step = pl.program_id(0)
    h2, dy, gates = h2_ref[...], dy_ref[...], gates_ref[...]
    lane = lax.broadcasted_iota(jnp.int32, gates.shape, 1) - ROUTE - EXP_DEV * pos_ref[0]
    total = None
    gate_grads = jnp.zeros(gates.shape, F32)
    for e in range(EXP_DEV):
        gate = RESIDUAL * jnp.sum(jnp.where(lane == e, gates, 0.0), axis=1, keepdims=True)
        gu = dot(h2, up_ref[e], 1, 0)
        back = dot(dy, down_ref[e], 1, 1)
        g, u = gu[:, :FF], gu[:, FF:]
        sig = 1.0 / (1.0 + jnp.exp(-g))
        swish = g * sig
        act = swish * u
        gate_grad = RESIDUAL * jnp.sum(act * back, axis=1, keepdims=True)
        which = lax.broadcasted_iota(jnp.int32, gates.shape, 1)
        gate_grads = jnp.where(which == e, gate_grad, gate_grads)
        ag_ref[e] = (gate * act).astype(BF)
        dact = gate * back
        dgu = jnp.concatenate(
            [dact * u * (sig * (1.0 + g * (1.0 - sig))), dact * swish], axis=1
        ).astype(BF)
        dgu_ref[e] = dgu
        term = dot(dgu, up_ref[e], 1, 1)
        total = term if total is None else total + term
    dg_ref[0] = gate_grads.T[:8]

    @pl.when(step < half)
    def _():
        give_ref[0] = total.astype(BF)

    @pl.when(step >= half)
    def _():
        keep_ref[0] = total.astype(BF)


def expert_main(pos, h2, dy_all, gates, w_gate_up, w_down):
    seq = h2.shape[0]
    steps = seq // BLK
    half = steps // 2
    row = lambda s, pos: (owner(s, half, pos), 0)
    each = lambda s, pos: (0, owner(s, half, pos), 0)
    return call(
        functools.partial(expert_kernel, half),
        "experts",
        (steps,),
        [
            spec((BLK, D), row),
            spec((BLK, D), row),
            spec((BLK, 128), row),
            resident(w_gate_up.shape),
            resident(w_down.shape),
        ],
        [
            spec((1, BLK, D), lambda s, pos: (give_index(s, half), 0, 0)),
            spec((1, BLK, D), lambda s, pos: (keep_index(s, half), 0, 0)),
            spec((EXP_DEV, BLK, FF), each),
            spec((EXP_DEV, BLK, 2 * FF), each),
            spec((1, 8, BLK), lambda s, pos: (owner(s, half, pos), 0, 0)),
        ],
        [
            shape((half, BLK, D), BF),
            shape((half, BLK, D), BF),
            shape((EXP_DEV, seq, FF), BF),
            shape((EXP_DEV, seq, 2 * FF), BF),
            shape((steps, 8, BLK), F32),
        ],
        10 * EXP_DEV * seq * D * FF,
        20 * seq * D,
    )(pos, h2, dy_all, gates, w_gate_up, w_down)


def down_grad_kernel(pos_ref, ag_ref, dy_ref, out_ref):
    out_ref[0, 0] = dot(ag_ref[0], dy_ref[...], 0, 0).astype(BF)


def down_grad(pos, ag, dy_all, groups):
    seq = dy_all.shape[0]
    cols = D // groups
    wide = cols if cols % 128 == 0 else D
    out = call(
        down_grad_kernel,
        "down_grad",
        (EXP_DEV, D // wide),
        [
            spec((1, seq, FF), lambda e, s, pos: (e, 0, 0)),
            spec((seq, wide), lambda e, s, pos: (0, s)),
        ],
        spec((1, 1, FF, wide), lambda e, s, pos: (s, e, 0, 0)),
        shape((D // wide, EXP_DEV, FF, wide), BF),
        2 * EXP_DEV * seq * D * FF,
        8 * seq * D,
    )(pos, ag, dy_all)
    if wide == cols:
        return out
    return jnp.moveaxis(out[0].reshape(EXP_DEV, FF, groups, cols), 2, 0)


def up_grad_kernel(pos_ref, h2_ref, dgu_ref, out_ref):
    out_ref[0] = dot(h2_ref[...], dgu_ref[0], 0, 0).astype(BF)


def up_grad(pos, h2, dgu, groups):
    seq = h2.shape[0]
    rows = 384
    out = call(
        up_grad_kernel,
        "up_grad",
        (EXP_DEV, D // rows),
        [
            spec((seq, rows), lambda e, s, pos: (0, s)),
            spec((1, seq, 2 * FF), lambda e, s, pos: (e, 0, 0)),
        ],
        spec((1, rows, 2 * FF), lambda e, s, pos: (e, s, 0)),
        shape((EXP_DEV, D, 2 * FF), BF),
        4 * EXP_DEV * seq * D * FF,
        8 * seq * D,
    )(pos, h2, dgu)
    return out


def combine_kernel(half, pos_ref, ag_ref, down_ref, give_ref, keep_ref):
    step = pl.program_id(0)
    total = dot(ag_ref[0], down_ref[0], 1, 0)
    for e in range(1, EXP_DEV):
        total = total + dot(ag_ref[e], down_ref[e], 1, 0)

    @pl.when(step < half)
    def _():
        give_ref[0] = total.astype(BF)

    @pl.when(step >= half)
    def _():
        keep_ref[0] = total.astype(BF)


def combine(pos, ag, w_down):
    seq = ag.shape[1]
    steps = seq // BLK
    half = steps // 2
    return call(
        functools.partial(combine_kernel, half),
        "combine",
        (steps,),
        [
            spec((EXP_DEV, BLK, FF), lambda s, pos: (0, owner(s, half, pos), 0)),
            resident(w_down.shape),
        ],
        [
            spec((1, BLK, D), lambda s, pos: (give_index(s, half), 0, 0)),
            spec((1, BLK, D), lambda s, pos: (keep_index(s, half), 0, 0)),
        ],
        [shape((half, BLK, D), BF), shape((half, BLK, D), BF)],
        2 * EXP_DEV * seq * D * FF,
        4 * seq * D,
    )(pos, ag, w_down)


def norm_pull(values, gain, grad):
    scale = lax.rsqrt(jnp.mean(values * values, axis=1, keepdims=True) + EPSILON)
    unit = values * scale
    inner = grad * gain
    pulled = scale * (inner - unit * jnp.mean(inner * unit, axis=1, keepdims=True))
    return pulled, jnp.sum(grad * unit, axis=0, keepdims=True)


def middle_kernel(
    pos_ref, keep_ref, got_ref, fx_ref, fy_ref, y1_ref, h2_ref, gates_ref, dg_ref, dy_ref,
    route_ref, gain_ref, w_ref, dy1_ref, db_ref, da_ref, router_ref, gain_grad_ref,
):
    dh2 = (
        keep_ref[0].astype(F32)
        + got_ref[0].astype(F32)
        + fx_ref[...].astype(F32)
        + fy_ref[...].astype(F32)
    )
    gates, gate_grads = gates_ref[...], dg_ref[...]
    mean = jnp.sum(gates * gate_grads, axis=1, keepdims=True)
    dlogits = (gates * (gate_grads - mean)).astype(BF)
    dh2 = dh2 + dot(dlogits, route_ref[...], 1, 1)
    router_ref[...] = dot(h2_ref[...], dlogits, 0, 0)
    pulled, gain_grad = norm_pull(y1_ref[...], gain_ref[...], dh2)
    gain_grad_ref[...] = jnp.broadcast_to(gain_grad, gain_grad_ref.shape)
    dy1 = dy_ref[...].astype(F32) + pulled
    dy1_ref[...] = dy1
    db = (RESIDUAL * dy1).astype(BF)
    db_ref[...] = db
    da = dot(w_ref[...], db, 1, 1).astype(BF)
    for j in range(da_ref.shape[0]):
        da_ref[j] = da[j * Q_COLS : (j + 1) * Q_COLS]


def middle(pos, keep, got, fx, fy, y1, h2, gates, dg, dy, weights, gain, w_full):
    rows = y1.shape[0]
    full = lambda a: resident(a.shape)
    first = pl.BlockSpec((1, rows, D), lambda s, pos: (0, 0, 0), pipeline_mode=pl.Buffered(1))
    members = HEADS * HEAD_DIM // Q_COLS
    return call(
        middle_kernel,
        "middle",
        (1,),
        [first, first]
        + [full(a) for a in (fx, fy, y1, h2, gates, dg, dy)]
        + [
            pl.BlockSpec((D, 128), lambda s, pos: (0, 2), pipeline_mode=pl.Buffered(1)),
            full(gain),
            full(w_full),
        ],
        [
            resident((rows, D)),
            resident((rows, D)),
            resident((members, Q_COLS, rows)),
            resident((D, 128)),
            resident((8, D)),
        ],
        [
            shape((rows, D), F32),
            shape((rows, D), BF),
            shape((members, Q_COLS, rows), BF),
            shape((D, 128), F32),
            shape((8, D), F32),
        ],
        2 * rows * D * D,
        4 * D * D,
    )(pos, keep, got, fx, fy, y1, h2, gates, dg, dy, weights, gain, w_full)


def back_kernel(
    half, pos_ref, dq_ref, dk_ref, dv_ref, cos_ref, sin_ref, w_ref, give_ref, keep_ref, packed_ref
):
    step = pl.program_id(0)
    cosine, sine = cos_ref[...], -sin_ref[...]
    rows = jnp.concatenate(
        [
            turn_rows(dq_ref[...], cosine, sine),
            turn_rows(dk_ref[...], cosine, sine),
            dv_ref[...],
            jnp.zeros((PACK - QKV, BLK), F32),
        ],
        axis=0,
    ).astype(BF)
    packed_ref[...] = rows
    total = dot(rows, w_ref[...], 0, 1).astype(BF)

    @pl.when(step < half)
    def _():
        give_ref[0] = total

    @pl.when(step >= half)
    def _():
        keep_ref[0] = total


def back(pos, dq_t, dk_t, dv_t, cosine, sine, weights):
    seq = dq_t.shape[1]
    steps = seq // BLK
    half = steps // 2
    column = lambda s, pos: (0, owner(s, half, pos))
    return call(
        functools.partial(back_kernel, half),
        "back",
        (steps,),
        [
            spec((Q_COLS, BLK), column),
            spec((HEAD_DIM, BLK), column),
            spec((HEAD_DIM, BLK), column),
            spec((HALF, BLK), column),
            spec((HALF, BLK), column),
            resident(weights.shape),
        ],
        [
            spec((1, BLK, D), lambda s, pos: (give_index(s, half), 0, 0)),
            spec((1, BLK, D), lambda s, pos: (keep_index(s, half), 0, 0)),
            spec((PACK, BLK), column),
        ],
        [
            shape((half, BLK, D), BF),
            shape((half, BLK, D), BF),
            shape((PACK, seq), BF),
        ],
        2 * seq * D * PACK,
        4 * seq * D,
    )(pos, dq_t, dk_t, dv_t, cosine, sine, weights)


def low_pair(values):
    high = values.astype(BF).astype(F32)
    return high, values - high


def pack_kernel(pos_ref, packed_ref, x_ref, gain_ref, router_ref, moe_ref, out_ref, acc):
    step = pl.program_id(0)

    @pl.when(step == 0)
    def _():
        acc[...] = jnp.zeros_like(acc)

    normed = (norm_of(x_ref[0].astype(F32)) * gain_ref[...]).astype(BF)
    acc[...] += dot(packed_ref[...], normed, 1, 0)

    @pl.when(step == pl.num_programs(0) - 1)
    def _():
        out_ref[:, :256] = acc[:256].T.astype(BF)
        lane = lax.broadcasted_iota(jnp.int32, (D, 128), 1)
        high, low = low_pair(router_ref[...])
        gain_high, gain_low = low_pair(moe_ref[...].T)
        rest = acc[256:].T + high + pltpu.roll(low, 16, 1)
        rest = jnp.where(lane == ROUTE + 32, gain_high[:, :1], rest)
        rest = jnp.where(lane == ROUTE + 33, gain_low[:, :1], rest)
        out_ref[:, 256:] = rest.astype(BF)


def pack(pos, packed, x_rel, gain, router, moe):
    seq = packed.shape[1]
    return call(
        pack_kernel,
        "pack",
        (seq // BLK,),
        [
            spec((PACK, BLK), lambda s, pos: (0, s)),
            spec((1, BLK, D), lambda s, pos: (s ^ pos[0], 0, 0)),
            resident(gain.shape),
            resident(router.shape),
            resident(moe.shape),
        ],
        resident((D, PACK)),
        shape((D, PACK), BF),
        2 * seq * D * PACK,
        4 * seq * D,
        [pltpu.VMEM((PACK, D), F32)],
    )(pos, packed, x_rel, gain, router, moe)


def last_kernel(
    pos_ref, keep_ref, got_ref, fx_ref, fy_ref, x_ref, gain_ref, dy1_ref, out_ref, gain_grad_ref
):
    dh1 = (
        keep_ref[0].astype(F32)
        + got_ref[0].astype(F32)
        + fx_ref[...].astype(F32)
        + fy_ref[...].astype(F32)
    )
    pulled, gain_grad = norm_pull(x_ref[...].astype(F32), gain_ref[...], dh1)
    out_ref[...] = (dy1_ref[...] + pulled).astype(BF)
    gain_grad_ref[...] = jnp.broadcast_to(gain_grad, gain_grad_ref.shape)


def last(pos, keep, got, fx, fy, x, gain, dy1):
    rows = x.shape[0]
    full = lambda a: resident(a.shape)
    first = pl.BlockSpec((1, rows, D), lambda s, pos: (0, 0, 0), pipeline_mode=pl.Buffered(1))
    return call(
        last_kernel,
        "last",
        (1,),
        [first, first] + [full(a) for a in (fx, fy, x, gain, dy1)],
        [resident((rows, D)), resident((8, D))],
        [shape((rows, D), BF), shape((8, D), F32)],
        20 * rows * D,
        14 * rows * D,
    )(pos, keep, got, fx, fy, x, gain, dy1)


def out_grad_kernel(count, pos_ref, *refs):
    pieces = refs[: count + 2]
    db_ref, out_ref, heads = refs[count + 2 :]
    step = pl.program_id(0)
    pos = pos_ref[0]
    for r in range(count):
        base = (pos ^ r) * Q_COLS
        if r < count - 2:
            heads[pl.ds(pl.multiple_of(base, Q_COLS), Q_COLS), :] = pieces[r][...]
        else:
            half = Q_COLS // 2
            at = count - 2 + 2 * (r - count + 2)
            heads[pl.ds(pl.multiple_of(base, half), half), :] = pieces[at][...]
            heads[pl.ds(pl.multiple_of(base + half, half), half), :] = pieces[at + 1][...]
    term = dot(db_ref[...], heads[...], 0, 1)

    @pl.when(step == 0)
    def _():
        out_ref[...] = term

    @pl.when(step > 0)
    def _():
        out_ref[...] += term


def out_grad(pos, pieces, db_cols):
    count = len(pieces) - 2
    seq, cols = db_cols.shape
    return call(
        functools.partial(out_grad_kernel, count),
        "out_grad",
        (seq // BLK,),
        [spec((a.shape[0], BLK), lambda s, pos: (0, s)) for a in pieces]
        + [spec((BLK, cols), lambda s, pos: (s, 0))],
        resident((cols, HEADS * HEAD_DIM)),
        shape((cols, HEADS * HEAD_DIM), F32),
        2 * seq * D * cols,
        4 * seq * D,
        [pltpu.VMEM((HEADS * HEAD_DIM, BLK), BF)],
    )(pos, *pieces, db_cols).astype(BF)


def unpack_kernel(groups, members, pos_ref, came_ref, query_ref, pair_ref, rest_ref):
    total = None
    for j in range(members):
        here = came_ref[j].astype(F32)
        for i in range(1, groups):
            here = here + came_ref[i * members + j].astype(F32)
        query_ref[:, j * Q_COLS : (j + 1) * Q_COLS] = here[:, :Q_COLS]
        pair_ref[:, j * HEAD_DIM : (j + 1) * HEAD_DIM] = here[:, Q_COLS : Q_COLS + HEAD_DIM]
        at = (members + j) * HEAD_DIM
        pair_ref[:, at : at + HEAD_DIM] = here[:, Q_COLS + HEAD_DIM : QKV]
        rest = here[:, 256:]
        total = rest if total is None else total + rest
    rest_ref[...] = total


def unpack(pos, came, groups):
    devices, rows, _ = came.shape
    members = devices // groups
    return call(
        functools.partial(unpack_kernel, groups, members),
        "unpack",
        (1,),
        [resident(came.shape)],
        [resident((rows, D)), resident((rows, 2 * KV_HEADS * HEAD_DIM)), resident((rows, 128))],
        [
            shape((rows, D), F32),
            shape((rows, 2 * KV_HEADS * HEAD_DIM), F32),
            shape((rows, 128), F32),
        ],
        devices * rows * PACK,
        4 * devices * rows * PACK,
    )(pos, came)


def swap(values, bit):
    count = lax.axis_size("expert")
    return lax.ppermute(values, "expert", [(i, i ^ bit) for i in range(count)])


def gather_pieces(own):
    half = own.shape[0] // 2
    x, y = swap(own, 2), swap(own, 4)
    core = swap(own, 1)
    far_a, far_b = swap(x[:half], 4), swap(y[half:], 2)
    return [
        own, core, x, swap(x, 1), y, swap(y, 1),
        far_a, far_b, swap(far_a, 1), swap(far_b, 1),
    ]


def scatter_sum(give, keep):
    half = keep.shape[1] // 2
    got = swap(give, 1)

    def pair(which, low, high):
        return keep[which, low:high].astype(F32) + got[which, low:high].astype(F32)

    far_a = swap(pair(3, 0, half).astype(BF), 2)
    far_b = swap(pair(3, half, 2 * half).astype(BF), 4)
    via_y = jnp.concatenate(
        [pair(2, 0, half) + far_a.astype(F32), pair(2, half, 2 * half)], axis=0
    ).astype(BF)
    via_x = jnp.concatenate(
        [pair(1, 0, half), pair(1, half, 2 * half) + far_b.astype(F32)], axis=0
    ).astype(BF)
    return got, swap(via_x, 2), swap(via_y, 4)


def exchange(blocks, axes):
    return lax.all_to_all(blocks, axes, split_axis=0, concat_axis=0, tiled=True)


def shards(
    tokens,
    segment_ids,
    expert_ids,
    w_query,
    w_key_value,
    w_out,
    w_router,
    norm_attn,
    norm_moe,
    w_gate_up,
    w_down,
    grad_out,
):
    tok_rows = tokens.shape[0]
    members = lax.axis_size("expert")
    groups = lax.axis_size("dp")
    position = lax.axis_index("expert")
    pos = position.astype(jnp.int32).reshape(1)
    devices = groups * members
    seq = tok_rows * members
    expert_total = EXP_DEV * members
    in_rows = w_query.shape[0]
    out_cols = w_out.shape[1]
    kv_cols = KV_HEADS * HEAD_DIM

    x_pieces = gather_pieces(tokens)

    own = jnp.concatenate(
        [
            w_query.reshape(in_rows, members, Q_COLS),
            w_key_value[:, :kv_cols].reshape(in_rows, members, HEAD_DIM),
            w_key_value[:, kv_cols:].reshape(in_rows, members, HEAD_DIM),
            jnp.broadcast_to(
                jnp.concatenate(
                    [
                        w_router,
                        norm_attn[:, None],
                        norm_moe[:, None],
                        jnp.zeros((in_rows, PACK - QKV - expert_total - 2), BF),
                    ],
                    axis=1,
                )[:, None, :],
                (in_rows, members, PACK - QKV),
            ),
        ],
        axis=2,
    )
    own = jnp.moveaxis(own, 1, 0)
    own = jnp.broadcast_to(own[None], (groups,) + own.shape).reshape(devices, in_rows, PACK)
    weights = exchange(own, BOTH).reshape(D, PACK)
    gain_attn = weights[:, QKV + expert_total].astype(F32)[None]
    gain_moe = weights[:, QKV + expert_total + 1].astype(F32)[None]

    ids_t = exchange(
        jnp.broadcast_to(expert_ids.T[None], (members, TOP, tok_rows)), "expert"
    )
    ids = jnp.moveaxis(ids_t.reshape(members, TOP, tok_rows), 1, 2).reshape(seq, TOP)
    w_full = lax.all_gather(w_out.T, BOTH, axis=0, tiled=True).T
    dy_all = lax.all_gather(grad_out, "expert", axis=0, tiled=True)

    token_pos = jnp.arange(seq, dtype=jnp.int32)
    start = jnp.sum(
        (segment_ids[:, None] < segment_ids[None, :]).astype(jnp.int32), axis=0, keepdims=True
    )
    first = start[0, ::BLK] // BLK
    frequency = ROPE_BASE ** (-(jnp.arange(HALF, dtype=F32) * 2.0 / HEAD_DIM))
    angles = frequency[:, None] * token_pos.astype(F32)[None, :]
    cosine, sine = jnp.cos(angles), jnp.sin(angles)

    q_t, k_t, v_t, k, v = qkv_forward(pos, x_pieces, weights, gain_attn, cosine, sine)
    a_t, o_t, lse = attn_forward(first, q_t, k, v_t, start)
    a_pieces = gather_pieces(a_t)
    x_rel = jnp.concatenate(
        [piece for piece in x_pieces], axis=0
    ).reshape(members, tok_rows, D)

    h2, gates, y1, h2_own, gates_own = mix_forward(
        pos, a_pieces, x_rel, w_full, gain_moe, weights, ids
    )

    give, keep, ag, dgu, dg = expert_main(pos, h2, dy_all, gates, w_gate_up, w_down)
    dg = exchange(dg, "expert")[:, :EXP_DEV].reshape(expert_total, tok_rows).T
    dg = jnp.pad(dg, ((0, 0), (ROUTE, 128 - ROUTE - expert_total)))
    got, from_x, from_y = scatter_sum(give, keep)

    down_wgrad = down_grad(pos, ag, dy_all, groups)
    down_share = lax.psum_scatter(
        down_wgrad.reshape(groups * EXP_DEV * FF, -1), "dp", scatter_dimension=0, tiled=True
    ).astype(F32).reshape(EXP_DEV, FF, -1)
    up_wgrad = up_grad(pos, h2, dgu, groups)
    up_share = lax.psum_scatter(up_wgrad, "dp", scatter_dimension=1, tiled=True).astype(F32)

    out_give, out_keep = combine(pos, ag, w_down)
    out_got, out_x, out_y = scatter_sum(out_give, out_keep)
    result = (
        y1
        + out_keep[0].astype(F32)
        + out_got[0].astype(F32)
        + out_x.astype(F32)
        + out_y.astype(F32)
    ).astype(BF)

    dy1, db, da, router_wgrad, moe_gain_grad = middle(
        pos, keep, got, from_x, from_y, y1, h2_own, gates_own, dg, grad_out, weights, gain_moe, w_full
    )
    da = exchange(da, "expert")

    db_cols = exchange(
        jnp.moveaxis(db.reshape(tok_rows, groups, members, out_cols), 2, 0).reshape(
            members, tok_rows, groups * out_cols
        ),
        "expert",
    ).reshape(seq, groups * out_cols)
    out_wgrad = out_grad(pos, a_pieces, db_cols).reshape(groups, out_cols, D)
    out_share = jnp.sum(exchange(out_wgrad, "dp").astype(F32), axis=0).T

    dq_t, dk_t, dv_t = attn_backward(first, q_t, da, o_t, lse, k, k_t, v, start)
    give1, keep1, packed = back(pos, dq_t, dk_t, dv_t, cosine, sine, weights)
    got1, from_x1, from_y1 = scatter_sum(give1, keep1)

    sent = pack(pos, packed, x_rel, gain_attn, router_wgrad, moe_gain_grad)
    came = exchange(sent.reshape(devices, in_rows, PACK), BOTH)
    query_share, pair_share, rest = unpack(pos, came, groups)
    router_share = (
        rest[:, ROUTE : ROUTE + expert_total]
        + rest[:, ROUTE + expert_total : ROUTE + 2 * expert_total]
    )
    moe_gain_share = rest[:, ROUTE + 32] + rest[:, ROUTE + 33]

    token_grad, attn_gain_grad = last(pos, keep1, got1, from_x1, from_y1, tokens, gain_attn, dy1)
    gain_rows = jnp.pad(
        attn_gain_grad[0].reshape(devices, in_rows), ((0, 0), (0, 128 - in_rows))
    )
    attn_gain_share = jnp.sum(exchange(gain_rows, BOTH), axis=0)[:in_rows]

    return (
        result,
        token_grad,
        query_share,
        pair_share,
        out_share,
        router_share,
        attn_gain_share,
        moe_gain_share,
        up_share,
        down_share,
    )


def solution(mesh):
    in_specs = (
        P(("dp", "expert"), None),
        P("dp"),
        P(("dp", "expert"), None),
        P(("dp", "expert"), None),
        P(("dp", "expert"), None),
        P(None, ("dp", "expert")),
        P(("dp", "expert"), None),
        P(("dp", "expert")),
        P(("dp", "expert")),
        P("expert", None, None),
        P("expert", None, None),
        P(("dp", "expert"), None),
    )
    out_specs = (
        P(("dp", "expert"), None),
        P(("dp", "expert"), None),
        P(("dp", "expert"), None),
        P(("dp", "expert"), None),
        P(None, ("dp", "expert")),
        P(("dp", "expert"), None),
        P(("dp", "expert")),
        P(("dp", "expert")),
        P("expert", "dp", None),
        P("expert", None, "dp"),
    )
    return jax.shard_map(shards, mesh=mesh, in_specs=in_specs, out_specs=out_specs, check_vma=False)
```

```python
import functools

import jax
import jax.numpy as jnp
from jax import lax
from jax.experimental import pallas as pl
from jax.experimental.pallas import tpu as pltpu
from jax.sharding import PartitionSpec as P

D = 1536
HEADS = 24
KV_HEADS = 8
HEAD_DIM = 64
FF = 512
TOP = 8
EXP_DEV = 2

RESIDUAL = 0.22
ATTN_SCALE = 0.015625
LOG2E = 1.4426950408889634
EPSILON = 1e-06
ROPE_BASE = 10000.0
MASKED = -1e30

GROUP = HEADS // KV_HEADS
HALF = HEAD_DIM // 2
BLK = 256
BF = jnp.bfloat16
F32 = jnp.float32
BOTH = ("dp", "expert")


def cost(micros):
    return pl.CostEstimate(flops=micros * 10**9, bytes_accessed=10**4, transcendentals=0)


LONG, SHORT = cost(50), cost(0)


def dot(a, b, ca, cb):
    return lax.dot_general(a, b, (((ca,), (cb,)), ((), ())), preferred_element_type=F32)


def rms_scale(values, gain_vec):
    return (
        values * lax.rsqrt(jnp.mean(values * values, axis=-1, keepdims=True) + EPSILON) * gain_vec
    )


def side_by_side(block):
    return jnp.concatenate(
        [block[h * HEAD_DIM : (h + 1) * HEAD_DIM] for h in range(GROUP)], axis=1
    )


def stacked(wide):
    width = wide.shape[1] // GROUP
    return jnp.concatenate([wide[:, h * width : (h + 1) * width] for h in range(GROUP)], axis=0)


def allowed_keys(start_ref, block, key_block):
    lane = lax.broadcasted_iota(jnp.int32, (1, BLK), 1) + block * BLK
    reach = lane - start_ref[...]
    lane3 = jnp.concatenate([lane] * GROUP, axis=1)
    reach3 = jnp.concatenate([reach] * GROUP, axis=1)
    key_pos = lax.broadcasted_iota(jnp.int32, (BLK, 1), 0) + key_block * BLK
    back = lane3 - key_pos
    return (back >= 0) & (back <= reach3)


def attn_fwd_kernel(first_ref, q_ref, k_ref, vt_ref, start_ref, a_ref, o_ref, lse_ref):
    block = pl.program_id(0)
    query = side_by_side(q_ref[...])
    width = GROUP * BLK

    def step(key_block, carry):
        largest, total, acc = carry
        keys = k_ref[pl.ds(pl.multiple_of(key_block * BLK, BLK), BLK), :]
        values = vt_ref[:, pl.ds(pl.multiple_of(key_block * BLK, BLK), BLK)]
        scores = dot(keys, query, 1, 0) * (ATTN_SCALE * LOG2E)
        scores = jnp.where(allowed_keys(start_ref, block, key_block), scores, MASKED)
        now = jnp.maximum(largest, jnp.max(scores, axis=0, keepdims=True))
        power = jnp.exp2(scores - now)
        fade = jnp.exp2(largest - now)
        total = total * fade + jnp.sum(power, axis=0, keepdims=True)
        acc = acc * fade + dot(values, power.astype(BF), 1, 0)
        return now, total, acc

    largest, total, acc = lax.fori_loop(
        first_ref[block],
        block + 1,
        step,
        (
            jnp.full((1, width), MASKED, F32),
            jnp.zeros((1, width), F32),
            jnp.zeros((HEAD_DIM, width), F32),
        ),
    )
    out = stacked(acc / total)
    o_ref[...] = out
    a_ref[...] = out.astype(BF)
    lse = largest + jnp.log2(total)
    lse_ref[...] = jnp.concatenate(
        [lse[:, h * BLK : (h + 1) * BLK] for h in range(GROUP)]
        + [jnp.zeros((8 - GROUP, BLK), F32)],
        axis=0,
    )


def attn_bwd_kernel(
    first_ref, q_ref, da_ref, o_ref, lse_ref, k_ref, kt_ref, v_ref, start_ref,
    dq_ref, dk_ref, dv_ref, dk_acc, dv_acc,
):
    block = pl.program_id(0)

    @pl.when(block == 0)
    def _():
        dk_acc[...] = jnp.zeros_like(dk_acc)
        dv_acc[...] = jnp.zeros_like(dv_acc)

    query_t = side_by_side(q_ref[...])
    query = query_t.astype(F32).T.astype(BF)
    grad_t = side_by_side(da_ref[0])
    grad_f = grad_t.astype(F32)
    grad = grad_f.T.astype(BF)
    delta = jnp.sum(side_by_side(o_ref[...]) * grad_f, axis=0, keepdims=True)
    lse = jnp.concatenate([lse_ref[h : h + 1, :] for h in range(GROUP)], axis=1)

    def step(key_block, dq):
        rows = pl.ds(pl.multiple_of(key_block * BLK, BLK), BLK)
        keys = k_ref[rows, :]
        scores = dot(keys, query_t, 1, 0) * (ATTN_SCALE * LOG2E)
        scores = jnp.where(allowed_keys(start_ref, block, key_block), scores, MASKED)
        prob = jnp.exp2(scores - lse)
        grad_prob = dot(v_ref[rows, :], grad_t, 1, 0)
        grad_score = (prob * (grad_prob - delta) * ATTN_SCALE).astype(BF)
        dv_acc[rows, :] += dot(prob.astype(BF), grad, 1, 0)
        dk_acc[rows, :] += dot(grad_score, query, 1, 0)
        return dq + dot(kt_ref[:, rows], grad_score, 1, 0)

    dq = lax.fori_loop(
        first_ref[block], block + 1, step, jnp.zeros((HEAD_DIM, GROUP * BLK), F32)
    )
    dq_ref[...] = stacked(dq)

    @pl.when(block == pl.num_programs(0) - 1)
    def _():
        dk_ref[...] = dk_acc[...].T
        dv_ref[...] = dv_acc[...].T


def attn_forward(first, q_t, k, v_t, start):
    seq = q_t.shape[1]
    rows = GROUP * HEAD_DIM
    column = lambda g, first: (0, g)
    whole = lambda g, first: (0, 0)
    return pl.pallas_call(
        attn_fwd_kernel,
        grid_spec=pltpu.PrefetchScalarGridSpec(
            num_scalar_prefetch=1,
            grid=(seq // BLK,),
            in_specs=[
                pl.BlockSpec((rows, BLK), column),
                pl.BlockSpec((seq, HEAD_DIM), whole),
                pl.BlockSpec((HEAD_DIM, seq), whole),
                pl.BlockSpec((1, BLK), column),
            ],
            out_specs=[
                pl.BlockSpec((rows, BLK), column),
                pl.BlockSpec((rows, BLK), column),
                pl.BlockSpec((8, BLK), column),
            ],
        ),
        out_shape=[
            jax.ShapeDtypeStruct((rows, seq), BF),
            jax.ShapeDtypeStruct((rows, seq), F32),
            jax.ShapeDtypeStruct((8, seq), F32),
        ],
        cost_estimate=LONG,
        name="attn_fwd",
    )(first, q_t, k, v_t, start)


def attn_backward(first, q_t, da, o_t, lse, k, k_t, v, start):
    seq = q_t.shape[1]
    rows = GROUP * HEAD_DIM
    column = lambda g, first: (0, g)
    whole = lambda g, first: (0, 0)
    return pl.pallas_call(
        attn_bwd_kernel,
        grid_spec=pltpu.PrefetchScalarGridSpec(
            num_scalar_prefetch=1,
            grid=(seq // BLK,),
            in_specs=[
                pl.BlockSpec((rows, BLK), column),
                pl.BlockSpec((1, rows, BLK), lambda g, first: (g, 0, 0)),
                pl.BlockSpec((rows, BLK), column),
                pl.BlockSpec((8, BLK), column),
                pl.BlockSpec((seq, HEAD_DIM), whole),
                pl.BlockSpec((HEAD_DIM, seq), whole),
                pl.BlockSpec((seq, HEAD_DIM), whole),
                pl.BlockSpec((1, BLK), column),
            ],
            out_specs=[
                pl.BlockSpec((rows, BLK), column),
                pl.BlockSpec((HEAD_DIM, seq), whole),
                pl.BlockSpec((HEAD_DIM, seq), whole),
            ],
            scratch_shapes=[
                pltpu.VMEM((seq, HEAD_DIM), F32),
                pltpu.VMEM((seq, HEAD_DIM), F32),
            ],
        ),
        out_shape=[
            jax.ShapeDtypeStruct((rows, seq), F32),
            jax.ShapeDtypeStruct((HEAD_DIM, seq), F32),
            jax.ShapeDtypeStruct((HEAD_DIM, seq), F32),
        ],
        cost_estimate=cost(20),
        name="attn_bwd",
    )(first, q_t, da, o_t, lse, k, k_t, v, start)


PACK = 384
Q_COLS = GROUP * HEAD_DIM
QKV = Q_COLS + 2 * HEAD_DIM
ROUTE = QKV - 256


def spec(shape, index):
    return pl.BlockSpec(shape, index)


def resident(shape):
    return pl.BlockSpec(
        shape, lambda *_: (0,) * len(shape), pipeline_mode=pl.Buffered(1)
    )


def call(kernel, name, grid, in_specs, out_specs, out_shape, estimate, scratch=()):
    return pl.pallas_call(
        kernel,
        grid_spec=pltpu.PrefetchScalarGridSpec(
            num_scalar_prefetch=1,
            grid=grid,
            in_specs=in_specs,
            out_specs=out_specs,
            scratch_shapes=list(scratch),
        ),
        out_shape=out_shape,
        cost_estimate=estimate,
        name=name,
    )


def shape(dims, kind):
    return jax.ShapeDtypeStruct(dims, kind)


def relative(step, half):
    return jnp.where(step < half, 2 * step + 1, 2 * (step - half))


def owner(step, half, pos):
    return relative(step, half) ^ pos[0]


def give_index(step, half):
    return jnp.minimum(step, half - 1)


def keep_index(step, half):
    return jnp.maximum(step - half, 0)


def turn_rows(rows_t, cosine, sine):
    out = []
    for h in range(rows_t.shape[0] // HEAD_DIM):
        a = rows_t[h * HEAD_DIM : h * HEAD_DIM + HALF]
        b = rows_t[h * HEAD_DIM + HALF : (h + 1) * HEAD_DIM]
        out += [a * cosine - b * sine, b * cosine + a * sine]
    return jnp.concatenate(out, axis=0)


def norm_of(values):
    return values * lax.rsqrt(jnp.mean(values * values, axis=1, keepdims=True) + EPSILON)


def qkv_kernel(count, pos_ref, *refs):
    pieces = refs[: count + 2]
    w_ref, gain_ref, cos_ref, sin_ref, q_ref, kt_ref, vt_ref, k_ref, v_ref = refs[count + 2 :]
    gain = gain_ref[...]
    for r in range(count):
        if r < count - 2:
            rows = pieces[r][...]
        else:
            at = count - 2 + 2 * (r - count + 2)
            rows = jnp.concatenate([pieces[at][...], pieces[at + 1][...]], axis=0)
        normed = (norm_of(rows.astype(F32)) * gain).astype(BF)
        both = dot(normed, w_ref[...], 1, 0)
        turned = both.T
        place = pl.multiple_of((pos_ref[0] ^ r) * BLK, BLK)
        columns = pl.ds(place, BLK)
        cosine, sine = cos_ref[:, columns], sin_ref[:, columns]
        qk = turn_rows(turned[: Q_COLS + HEAD_DIM], cosine, sine)
        q_ref[:, columns] = qk[:Q_COLS].astype(BF)
        kt_ref[:, columns] = qk[Q_COLS:].astype(BF)
        vt_ref[:, columns] = turned[Q_COLS + HEAD_DIM : QKV].astype(BF)
        k_ref[columns, :] = qk[Q_COLS:].T.astype(BF)
        v_ref[columns, :] = both[:, 256 : 256 + HEAD_DIM].astype(BF)


def qkv_forward(pos, pieces, weights, gain, cosine, sine):
    count = len(pieces) - 2
    seq = cosine.shape[1]
    full = lambda a: resident(a.shape)
    return call(
        functools.partial(qkv_kernel, count),
        "qkv",
        (1,),
        [full(a) for a in pieces] + [full(a) for a in (weights, gain, cosine, sine)],
        [resident(s) for s in ((Q_COLS, seq), (HEAD_DIM, seq), (HEAD_DIM, seq), (seq, HEAD_DIM), (seq, HEAD_DIM))],
        [
            shape((Q_COLS, seq), BF),
            shape((HEAD_DIM, seq), BF),
            shape((HEAD_DIM, seq), BF),
            shape((seq, HEAD_DIM), BF),
            shape((seq, HEAD_DIM), BF),
        ],
        cost(400),
    )(pos, *pieces, weights, gain, cosine, sine)


def send_weights_kernel(groups, members, pos_ref, q_ref, kv_ref, rest_ref, out_ref):
    query, pair, rest = q_ref[...], kv_ref[...], rest_ref[...]
    for j in range(members):
        block = jnp.concatenate(
            [query[:, j * Q_COLS : (j + 1) * Q_COLS]]
            + [pair[:, n * HEAD_DIM : (n + 1) * HEAD_DIM] for n in (j, members + j)]
            + [rest],
            axis=1,
        )
        for i in range(groups):
            out_ref[i * members + j] = block


def send_weights(pos, w_query, w_key_value, rest, groups, members):
    rows = w_query.shape[0]
    full = lambda a: resident(a.shape)
    return call(
        functools.partial(send_weights_kernel, groups, members),
        "send_weights",
        (1,),
        [full(a) for a in (w_query, w_key_value, rest)],
        resident((groups * members, rows, PACK)),
        shape((groups * members, rows, PACK), BF),
        SHORT,
    )(pos, w_query, w_key_value, rest)


def mix_kernel(count, pos_ref, *refs):
    pieces = refs[: count + 2]
    x_ref, w_ref, gain_ref, route_ref, ids_ref = refs[count + 2 : count + 7]
    h2_ref, gates_ref, y1_ref, h2_own_ref, gates_own_ref, heads = refs[count + 7 :]
    block = pl.program_id(0)
    pos = pos_ref[0]
    for r in range(count):
        base = (pos ^ r) * Q_COLS
        if r < count - 2:
            heads[pl.ds(pl.multiple_of(base, Q_COLS), Q_COLS), :] = pieces[r][...]
        else:
            half = Q_COLS // 2
            at = count - 2 + 2 * (r - count + 2)
            heads[pl.ds(pl.multiple_of(base, half), half), :] = pieces[at][...]
            heads[pl.ds(pl.multiple_of(base + half, half), half), :] = pieces[at + 1][...]
    y1 = x_ref[0].astype(F32) + RESIDUAL * dot(heads[...], w_ref[...], 0, 0)
    h2 = (norm_of(y1) * gain_ref[...]).astype(BF)
    logits = dot(h2, route_ref[...], 1, 0)
    lane = lax.broadcasted_iota(jnp.int32, logits.shape, 1) - ROUTE
    ids = ids_ref[0].T
    chosen = lane == ids[:, 0:1]
    for k in range(1, TOP):
        chosen = chosen | (lane == ids[:, k : k + 1])
    masked = jnp.where(chosen, logits, MASKED)
    power = jnp.where(chosen, jnp.exp(masked - jnp.max(masked, axis=1, keepdims=True)), 0.0)
    gates = power / jnp.sum(power, axis=1, keepdims=True)
    h2_ref[...] = h2
    gates_ref[...] = gates

    @pl.when(block == pos)
    def _():
        y1_ref[...] = y1
        h2_own_ref[...] = h2
        gates_own_ref[...] = gates


def mix_forward(pos, pieces, x_rel, w_full, gain, weights, ids):
    count = len(pieces) - 2
    seq = ids.shape[0] * BLK
    row = lambda s, pos: (s, 0)
    return call(
        functools.partial(mix_kernel, count),
        "mix",
        (seq // BLK,),
        [spec((a.shape[0], BLK), lambda s, pos: (0, s)) for a in pieces]
        + [
            spec((1, BLK, D), lambda s, pos: (s ^ pos[0], 0, 0)),
            resident(w_full.shape),
            resident(gain.shape),
            pl.BlockSpec((D, 128), lambda s, pos: (0, 2), pipeline_mode=pl.Buffered(1)),
            spec((1, TOP, BLK), lambda s, pos: (s ^ pos[0], 0, 0)),
        ],
        [
            spec((BLK, D), row),
            spec((BLK, 128), row),
            resident((BLK, D)),
            resident((BLK, D)),
            resident((BLK, 128)),
        ],
        [
            shape((seq, D), BF),
            shape((seq, 128), F32),
            shape((BLK, D), F32),
            shape((BLK, D), BF),
            shape((BLK, 128), F32),
        ],
        LONG,
        [pltpu.VMEM((HEADS * HEAD_DIM, BLK), BF)],
    )(pos, *pieces, x_rel, w_full, gain, weights, ids)


def expert_kernel(
    half, pos_ref, h2_ref, dy_ref, gates_ref, up_ref, down_ref,
    give_ref, keep_ref, ag_ref, dgu_ref, dg_ref,
):
    step = pl.program_id(0)
    h2, dy, gates = h2_ref[...], dy_ref[...], gates_ref[...]
    lane = lax.broadcasted_iota(jnp.int32, gates.shape, 1) - ROUTE - EXP_DEV * pos_ref[0]
    total = None
    gate_grads = jnp.zeros(gates.shape, F32)
    for e in range(EXP_DEV):
        gate = RESIDUAL * jnp.sum(jnp.where(lane == e, gates, 0.0), axis=1, keepdims=True)
        gu = dot(h2, up_ref[e], 1, 0)
        back = dot(dy, down_ref[e], 1, 1)
        g, u = gu[:, :FF], gu[:, FF:]
        sig = 1.0 / (1.0 + jnp.exp(-g))
        swish = g * sig
        act = swish * u
        gate_grad = RESIDUAL * jnp.sum(act * back, axis=1, keepdims=True)
        which = lax.broadcasted_iota(jnp.int32, gates.shape, 1)
        gate_grads = jnp.where(which == e, gate_grad, gate_grads)
        ag_ref[e] = (gate * act).astype(BF)
        dact = gate * back
        dgu = jnp.concatenate(
            [dact * u * (sig * (1.0 + g * (1.0 - sig))), dact * swish], axis=1
        ).astype(BF)
        dgu_ref[e] = dgu
        term = dot(dgu, up_ref[e], 1, 1)
        total = term if total is None else total + term
    dg_ref[0] = gate_grads.T[:8]

    @pl.when(step < half)
    def _():
        give_ref[0] = total.astype(BF)

    @pl.when(step >= half)
    def _():
        keep_ref[0] = total.astype(BF)


def expert_main(pos, h2, dy_all, gates, w_gate_up, w_down):
    seq = h2.shape[0]
    steps = seq // BLK
    half = steps // 2
    row = lambda s, pos: (owner(s, half, pos), 0)
    each = lambda s, pos: (0, owner(s, half, pos), 0)
    return call(
        functools.partial(expert_kernel, half),
        "experts",
        (steps,),
        [
            spec((BLK, D), row),
            spec((BLK, D), row),
            spec((BLK, 128), row),
            resident(w_gate_up.shape),
            resident(w_down.shape),
        ],
        [
            spec((1, BLK, D), lambda s, pos: (give_index(s, half), 0, 0)),
            spec((1, BLK, D), lambda s, pos: (keep_index(s, half), 0, 0)),
            spec((EXP_DEV, BLK, FF), each),
            spec((EXP_DEV, BLK, 2 * FF), each),
            spec((1, 8, BLK), lambda s, pos: (owner(s, half, pos), 0, 0)),
        ],
        [
            shape((half, BLK, D), BF),
            shape((half, BLK, D), BF),
            shape((EXP_DEV, seq, FF), BF),
            shape((EXP_DEV, seq, 2 * FF), BF),
            shape((steps, 8, BLK), F32),
        ],
        LONG,
    )(pos, h2, dy_all, gates, w_gate_up, w_down)


def down_grad_kernel(pos_ref, ag_ref, dy_ref, out_ref):
    out_ref[0, 0] = dot(ag_ref[0], dy_ref[...], 0, 0).astype(BF)


def down_grad(pos, ag, dy_all, groups):
    seq = dy_all.shape[0]
    cols = D // groups
    wide = cols if cols % 128 == 0 else D
    out = call(
        down_grad_kernel,
        "down_grad",
        (EXP_DEV, D // wide),
        [
            spec((1, seq, FF), lambda e, s, pos: (e, 0, 0)),
            spec((seq, wide), lambda e, s, pos: (0, s)),
        ],
        spec((1, 1, FF, wide), lambda e, s, pos: (s, e, 0, 0)),
        shape((D // wide, EXP_DEV, FF, wide), BF),
        SHORT,
    )(pos, ag, dy_all)
    if wide == cols:
        return out
    return jnp.moveaxis(out[0].reshape(EXP_DEV, FF, groups, cols), 2, 0)


def up_grad_kernel(pos_ref, h2_ref, dgu_ref, out_ref):
    out_ref[0] = dot(h2_ref[...], dgu_ref[0], 0, 0).astype(BF)


def up_grad(pos, h2, dgu, groups):
    seq = h2.shape[0]
    rows = 384
    out = call(
        up_grad_kernel,
        "up_grad",
        (EXP_DEV, D // rows),
        [
            spec((seq, rows), lambda e, s, pos: (0, s)),
            spec((1, seq, 2 * FF), lambda e, s, pos: (e, 0, 0)),
        ],
        spec((1, rows, 2 * FF), lambda e, s, pos: (e, s, 0)),
        shape((EXP_DEV, D, 2 * FF), BF),
        SHORT,
    )(pos, h2, dgu)
    return out


def combine_kernel(half, pos_ref, ag_ref, down_ref, give_ref, keep_ref):
    step = pl.program_id(0)
    total = dot(ag_ref[0], down_ref[0], 1, 0)
    for e in range(1, EXP_DEV):
        total = total + dot(ag_ref[e], down_ref[e], 1, 0)

    @pl.when(step < half)
    def _():
        give_ref[0] = total.astype(BF)

    @pl.when(step >= half)
    def _():
        keep_ref[0] = total.astype(BF)


def combine(pos, ag, w_down):
    seq = ag.shape[1]
    steps = seq // BLK
    half = steps // 2
    return call(
        functools.partial(combine_kernel, half),
        "combine",
        (steps,),
        [
            spec((EXP_DEV, BLK, FF), lambda s, pos: (0, owner(s, half, pos), 0)),
            resident(w_down.shape),
        ],
        [
            spec((1, BLK, D), lambda s, pos: (give_index(s, half), 0, 0)),
            spec((1, BLK, D), lambda s, pos: (keep_index(s, half), 0, 0)),
        ],
        [shape((half, BLK, D), BF), shape((half, BLK, D), BF)],
        SHORT,
    )(pos, ag, w_down)


def norm_pull(values, gain, grad):
    scale = lax.rsqrt(jnp.mean(values * values, axis=1, keepdims=True) + EPSILON)
    unit = values * scale
    inner = grad * gain
    pulled = scale * (inner - unit * jnp.mean(inner * unit, axis=1, keepdims=True))
    return pulled, jnp.sum(grad * unit, axis=0, keepdims=True)


def middle_kernel(
    members, groups, wide, pos_ref, keep_ref, got_ref, fx_ref, fy_ref, fd_ref, y1_ref, h2_ref, gates_ref, dg_ref, dy_ref,
    route_ref, gain_ref, w_ref, dy1_ref, db_ref, da_ref, router_ref, gain_grad_ref,
):
    dh2 = (
        keep_ref[0].astype(F32)
        + got_ref[0].astype(F32)
        + fx_ref[...].astype(F32)
        + fy_ref[...].astype(F32)
        + fd_ref[...].astype(F32)
    )
    gates, gate_grads = gates_ref[...], dg_ref[...]
    mean = jnp.sum(gates * gate_grads, axis=1, keepdims=True)
    dlogits = (gates * (gate_grads - mean)).astype(BF)
    dh2 = dh2 + dot(dlogits, route_ref[...], 1, 1)
    router_ref[...] = dot(h2_ref[...], dlogits, 0, 0)
    pulled, gain_grad = norm_pull(y1_ref[...], gain_ref[...], dh2)
    gain_grad_ref[...] = jnp.broadcast_to(gain_grad, gain_grad_ref.shape)
    dy1 = dy_ref[...].astype(F32) + pulled
    dy1_ref[...] = dy1
    db = (RESIDUAL * dy1).astype(BF)
    db_ref[...] = db
    da = dot(w_ref[...], db, 1, 1).astype(BF)
    for j in range(members):
        da_ref[j, :Q_COLS] = da[j * Q_COLS : (j + 1) * Q_COLS]
    if wide:
        cols = Q_COLS // groups
        db_t = (RESIDUAL * dy1).T.astype(BF)
        for j in range(members):
            for i in range(groups):
                at, to = (i * members + j) * cols, Q_COLS + i * cols
                da_ref[j, to : to + cols] = db_t[at : at + cols]


def middle(groups, pos, keep, got, sums, y1, h2, gates, dg, dy, weights, gain, w_full):
    rows = y1.shape[0]
    full = lambda a: resident(a.shape)
    first = pl.BlockSpec((1, rows, D), lambda s, pos: (0, 0, 0), pipeline_mode=pl.Buffered(1))
    members = HEADS * HEAD_DIM // Q_COLS
    wide = Q_COLS // groups % 16 == 0
    both = 2 * Q_COLS if wide else Q_COLS
    dy1, db, sent, router, gain_grad = call(
        functools.partial(middle_kernel, members, groups, wide),
        "middle",
        (1,),
        [first, first]
        + [full(a) for a in (*sums, y1, h2, gates, dg, dy)]
        + [
            pl.BlockSpec((D, 128), lambda s, pos: (0, 2), pipeline_mode=pl.Buffered(1)),
            full(gain),
            full(w_full),
        ],
        [
            resident((rows, D)),
            resident((rows, D)),
            resident((members, both, rows)),
            resident((D, 128)),
            resident((8, D)),
        ],
        [
            shape((rows, D), F32),
            shape((rows, D), BF),
            shape((members, both, rows), BF),
            shape((D, 128), F32),
            shape((8, D), F32),
        ],
        cost(100),
    )(pos, keep, got, *sums, y1, h2, gates, dg, dy, weights, gain, w_full)
    if not wide:
        cols = Q_COLS // groups
        db_t = jnp.moveaxis(db.T.reshape(groups, members, cols, rows), 1, 0)
        sent = jnp.concatenate([sent, db_t.reshape(members, Q_COLS, rows)], axis=1)
    return dy1, sent, router, gain_grad


def back_kernel(
    half, pos_ref, dq_ref, dk_ref, dv_ref, cos_ref, sin_ref, w_ref, give_ref, keep_ref, packed_ref
):
    step = pl.program_id(0)
    cosine, sine = cos_ref[...], -sin_ref[...]
    rows = jnp.concatenate(
        [
            turn_rows(dq_ref[...], cosine, sine),
            turn_rows(dk_ref[...], cosine, sine),
            dv_ref[...],
            jnp.zeros((PACK - QKV, BLK), F32),
        ],
        axis=0,
    ).astype(BF)
    packed_ref[...] = rows
    total = dot(rows, w_ref[...], 0, 1).astype(BF)

    @pl.when(step < half)
    def _():
        give_ref[0] = total

    @pl.when(step >= half)
    def _():
        keep_ref[0] = total


def back(pos, dq_t, dk_t, dv_t, cosine, sine, weights):
    seq = dq_t.shape[1]
    steps = seq // BLK
    half = steps // 2
    column = lambda s, pos: (0, owner(s, half, pos))
    return call(
        functools.partial(back_kernel, half),
        "back",
        (steps,),
        [
            spec((Q_COLS, BLK), column),
            spec((HEAD_DIM, BLK), column),
            spec((HEAD_DIM, BLK), column),
            spec((HALF, BLK), column),
            spec((HALF, BLK), column),
            resident(weights.shape),
        ],
        [
            spec((1, BLK, D), lambda s, pos: (give_index(s, half), 0, 0)),
            spec((1, BLK, D), lambda s, pos: (keep_index(s, half), 0, 0)),
            spec((PACK, BLK), column),
        ],
        [
            shape((half, BLK, D), BF),
            shape((half, BLK, D), BF),
            shape((PACK, seq), BF),
        ],
        cost(10),
    )(pos, dq_t, dk_t, dv_t, cosine, sine, weights)


def low_pair(values):
    high = values.astype(BF).astype(F32)
    return high, values - high


def pack_kernel(pos_ref, packed_ref, x_ref, gain_ref, w_ref, router_ref, moe_ref, out_ref, acc):
    step = pl.program_id(0)

    @pl.when(step == 0)
    def _():
        acc[...] = jnp.zeros_like(acc)

    normed = (norm_of(x_ref[0].astype(F32)) * gain_ref[...]).astype(BF)
    acc[...] += dot(packed_ref[...], normed, 1, 0)

    @pl.when(step == pl.num_programs(0) - 1)
    def _():
        main, rest = acc[:256].T, acc[256:].T
        w_main, w_rest = w_ref[:, :256].astype(F32), w_ref[:, 256:].astype(F32)
        lane = lax.broadcasted_iota(jnp.int32, (D, 128), 1)
        gain_attn = (
            jnp.sum(main * w_main, axis=1, keepdims=True)
            + jnp.sum(rest * w_rest, axis=1, keepdims=True)
        ) / w_rest[:, ROUTE + 16 : ROUTE + 17]
        high, low = low_pair(router_ref[...])
        moe_high, moe_low = low_pair(moe_ref[...].T)
        attn_high, attn_low = low_pair(gain_attn)
        rest = rest + high + pltpu.roll(low, 16, 1)
        for at, column in enumerate((moe_high[:, :1], moe_low[:, :1], attn_high, attn_low)):
            rest = jnp.where(lane == ROUTE + 32 + at, column, rest)
        out_ref[:, :256] = main.astype(BF)
        out_ref[:, 256:] = rest.astype(BF)


def pack(pos, packed, x_rel, gain, weights, router, moe):
    seq = packed.shape[1]
    return call(
        pack_kernel,
        "pack",
        (seq // BLK,),
        [
            spec((PACK, BLK), lambda s, pos: (0, s)),
            spec((1, BLK, D), lambda s, pos: (s ^ pos[0], 0, 0)),
            resident(gain.shape),
            resident(weights.shape),
            resident(router.shape),
            resident(moe.shape),
        ],
        resident((D, PACK)),
        shape((D, PACK), BF),
        SHORT,
        [pltpu.VMEM((PACK, D), F32)],
    )(pos, packed, x_rel, gain, weights, router, moe)


def last_kernel(
    pos_ref, keep_ref, got_ref, fx_ref, fy_ref, fd_ref, x_ref, gain_ref, dy1_ref, out_ref
):
    dh1 = (
        keep_ref[0].astype(F32)
        + got_ref[0].astype(F32)
        + fx_ref[...].astype(F32)
        + fy_ref[...].astype(F32)
        + fd_ref[...].astype(F32)
    )
    pulled, _ = norm_pull(x_ref[...].astype(F32), gain_ref[...], dh1)
    out_ref[...] = (dy1_ref[...] + pulled).astype(BF)


def last(pos, keep, got, sums, x, gain, dy1):
    rows = x.shape[0]
    full = lambda a: resident(a.shape)
    first = pl.BlockSpec((1, rows, D), lambda s, pos: (0, 0, 0), pipeline_mode=pl.Buffered(1))
    return call(
        last_kernel,
        "last",
        (1,),
        [first, first] + [full(a) for a in (*sums, x, gain, dy1)],
        resident((rows, D)),
        shape((rows, D), BF),
        cost(50),
    )(pos, keep, got, *sums, x, gain, dy1)


def out_grad_kernel(count, pos_ref, *refs):
    pieces = refs[: count + 2]
    db_ref, out_ref, heads = refs[count + 2 :]
    step = pl.program_id(0)
    pos = pos_ref[0]
    for r in range(count):
        base = (pos ^ r) * Q_COLS
        if r < count - 2:
            heads[pl.ds(pl.multiple_of(base, Q_COLS), Q_COLS), :] = pieces[r][...]
        else:
            half = Q_COLS // 2
            at = count - 2 + 2 * (r - count + 2)
            heads[pl.ds(pl.multiple_of(base, half), half), :] = pieces[at][...]
            heads[pl.ds(pl.multiple_of(base + half, half), half), :] = pieces[at + 1][...]
    term = dot(db_ref[0], heads[...], 1, 1)

    @pl.when(step == 0)
    def _():
        out_ref[...] = term

    @pl.when(step > 0)
    def _():
        out_ref[...] += term


def out_grad(pos, pieces, came):
    count = len(pieces) - 2
    seq, cols = came.shape[0] * BLK, Q_COLS
    return call(
        functools.partial(out_grad_kernel, count),
        "out_grad",
        (seq // BLK,),
        [spec((a.shape[0], BLK), lambda s, pos: (0, s)) for a in pieces]
        + [spec((1, cols, BLK), lambda s, pos: (s, 1, 0))],
        resident((cols, HEADS * HEAD_DIM)),
        shape((cols, HEADS * HEAD_DIM), F32),
        SHORT,
        [pltpu.VMEM((HEADS * HEAD_DIM, BLK), BF)],
    )(pos, *pieces, came).astype(BF)


def unpack_kernel(groups, members, pos_ref, came_ref, query_ref, pair_ref, rest_ref):
    total = None
    for j in range(members):
        here = came_ref[j].astype(F32)
        for i in range(1, groups):
            here = here + came_ref[i * members + j].astype(F32)
        query_ref[:, j * Q_COLS : (j + 1) * Q_COLS] = here[:, :Q_COLS]
        pair_ref[:, j * HEAD_DIM : (j + 1) * HEAD_DIM] = here[:, Q_COLS : Q_COLS + HEAD_DIM]
        at = (members + j) * HEAD_DIM
        pair_ref[:, at : at + HEAD_DIM] = here[:, Q_COLS + HEAD_DIM : QKV]
        rest = here[:, 256:]
        total = rest if total is None else total + rest
    rest_ref[...] = total


def unpack(pos, came, groups):
    devices, rows, _ = came.shape
    members = devices // groups
    return call(
        functools.partial(unpack_kernel, groups, members),
        "unpack",
        (1,),
        [resident(came.shape)],
        [resident((rows, D)), resident((rows, 2 * KV_HEADS * HEAD_DIM)), resident((rows, 128))],
        [
            shape((rows, D), F32),
            shape((rows, 2 * KV_HEADS * HEAD_DIM), F32),
            shape((rows, 128), F32),
        ],
        SHORT,
    )(pos, came)


def swap(values, bit):
    count = lax.axis_size("expert")
    return lax.ppermute(values, "expert", [(i, i ^ bit) for i in range(count)])


def gather_pieces(own, before_last):
    half = own.shape[0] // 2
    x, y = swap(own, 2), swap(own, 4)
    core = swap(own, 1)
    far_a, far_b = tie((swap(x[:half], 4), swap(y[half:], 2)), before_last)
    return [
        own, core, x, swap(x, 1), y, swap(y, 1),
        far_a, far_b, swap(far_a, 1), swap(far_b, 1),
    ]


def gather_direct(own):
    near = [own, swap(own, 2), swap(own, 4), swap(own, 6)]
    return [piece for value in near for piece in (value, swap(value, 1))]


def tie(values, *after):
    return lax.optimization_barrier((values, after))[0]


def pair_sums(keep, got):
    return [(keep[r].astype(F32) + got[r].astype(F32)).astype(BF) for r in (1, 2, 3)]


def send_sums(sums):
    return [swap(sums[0], 2), swap(sums[1], 4), swap(sums[2], 6)]


def send_to_groups(blocks):
    count = lax.axis_size("dp")
    me = lax.axis_index("dp")
    terms = [lax.dynamic_index_in_dim(blocks, me, 0, False)]
    for k in range(1, count):
        sent = lax.dynamic_index_in_dim(blocks, (me + k) % count, 0, False)
        terms.append(lax.ppermute(sent, "dp", [(i, (i + k) % count) for i in range(count)]))
    return terms


def exchange(blocks, axes):
    return lax.all_to_all(blocks, axes, split_axis=0, concat_axis=0, tiled=True)


def shards(
    tokens,
    segment_ids,
    expert_ids,
    w_query,
    w_key_value,
    w_out,
    w_router,
    norm_attn,
    norm_moe,
    w_gate_up,
    w_down,
    grad_out,
):
    tok_rows = tokens.shape[0]
    members = lax.axis_size("expert")
    groups = lax.axis_size("dp")
    position = lax.axis_index("expert")
    pos = position.astype(jnp.int32).reshape(1)
    devices = groups * members
    seq = tok_rows * members
    expert_total = EXP_DEV * members
    in_rows = w_query.shape[0]
    out_cols = w_out.shape[1]
    kv_cols = KV_HEADS * HEAD_DIM

    x_pieces = gather_pieces(tokens, ())

    rest = jnp.concatenate(
        [
            w_router,
            norm_attn[:, None],
            norm_moe[:, None],
            jnp.zeros((in_rows, PACK - QKV - expert_total - 2), BF),
        ],
        axis=1,
    )
    own = send_weights(pos, w_query, w_key_value, rest, groups, members)
    weights = exchange(own, BOTH).reshape(D, PACK)
    gain_attn = weights[:, QKV + expert_total].astype(F32)[None]
    gain_moe = weights[:, QKV + expert_total + 1].astype(F32)[None]

    token_pos = jnp.arange(seq, dtype=jnp.int32)
    start = jnp.sum(
        (segment_ids[:, None] < segment_ids[None, :]).astype(jnp.int32), axis=0, keepdims=True
    )
    first = start[0, ::BLK] // BLK
    frequency = ROPE_BASE ** (-(jnp.arange(HALF, dtype=F32) * 2.0 / HEAD_DIM))
    angles = frequency[:, None] * token_pos.astype(F32)[None, :]
    cosine, sine = jnp.cos(angles), jnp.sin(angles)

    q_t, k_t, v_t, k, v = qkv_forward(
        pos, x_pieces, tie(weights, start, first), gain_attn, cosine, sine
    )
    w_full = lax.all_gather(tie(w_out.T, q_t), BOTH, axis=0, tiled=True)
    dy_all = lax.all_gather(tie(grad_out, q_t), "expert", axis=0, tiled=True)
    w_full = w_full.T
    a_t, o_t, lse = attn_forward(first, q_t, k, v_t, start)
    ids = jnp.concatenate(gather_direct(tie(expert_ids, q_t).T), axis=0)
    ids = ids.reshape(members, TOP, tok_rows)
    a_pieces = gather_pieces(a_t, (w_full, ids))
    x_rel = jnp.concatenate(tie(x_pieces, a_t), axis=0).reshape(members, tok_rows, D)

    h2, gates, y1, h2_own, gates_own = mix_forward(
        pos, a_pieces, x_rel, w_full, gain_moe, weights, ids
    )

    give, keep, ag, dgu, dg = expert_main(pos, h2, dy_all, gates, w_gate_up, w_down)
    got = swap(give, 1)
    down_wgrad = down_grad(pos, ag, dy_all, groups)
    down_share = lax.psum_scatter(
        down_wgrad.reshape(groups * EXP_DEV * FF, -1), "dp", scatter_dimension=0, tiled=True
    ).astype(F32).reshape(EXP_DEV, FF, -1)
    sums = pair_sums(keep, tie(got, down_wgrad))
    came_sums = send_sums(sums)
    dg = exchange(tie(dg, sums), "expert")[:, :EXP_DEV].reshape(expert_total, tok_rows).T
    dg = jnp.pad(dg, ((0, 0), (ROUTE, 128 - ROUTE - expert_total)))
    up_wgrad = up_grad(pos, *tie((h2, dgu), sums), groups)
    up_share = lax.psum_scatter(up_wgrad, "dp", scatter_dimension=1, tiled=True).astype(F32)
    out_give, out_keep = combine(pos, tie(ag, up_wgrad), w_down)
    out_got = swap(out_give, 1)

    dy1, da, router_wgrad, moe_gain_grad = middle(
        groups, pos, tie(keep, out_keep), got, came_sums, y1, h2_own, gates_own, dg, grad_out,
        weights, gain_moe, w_full,
    )
    da = exchange(da, "expert")
    out_sums = pair_sums(out_keep, tie(out_got, dy1))
    out_came = send_sums(out_sums)

    dq_t, dk_t, dv_t = attn_backward(first, q_t, tie(da, out_sums), o_t, lse, k, k_t, v, start)
    result = y1 + out_keep[0].astype(F32) + out_got[0].astype(F32)
    for term in out_came:
        result = result + term.astype(F32)
    result = result.astype(BF)
    give1, keep1, packed = back(pos, tie(dq_t, result), dk_t, dv_t, cosine, sine, weights)
    got1 = swap(give1, 1)
    sent = pack(pos, packed, x_rel, gain_attn, weights, router_wgrad, moe_gain_grad)
    sums1 = pair_sums(keep1, tie(got1, sent))
    came_sums1 = send_sums(sums1)
    sent = tie(sent, sums1)
    out_wgrad = out_grad(pos, a_pieces, tie(da, sums1)).reshape(groups, out_cols, D)
    out_terms = send_to_groups(out_wgrad)
    came = exchange(sent.reshape(devices, in_rows, PACK), BOTH)
    query_share, pair_share, rest = unpack(pos, came, groups)
    router_share = (
        rest[:, ROUTE : ROUTE + expert_total]
        + rest[:, ROUTE + expert_total : ROUTE + 2 * expert_total]
    )
    moe_gain_share = rest[:, ROUTE + 32] + rest[:, ROUTE + 33]

    attn_gain_share = rest[:, ROUTE + 34] + rest[:, ROUTE + 35]
    token_grad = last(pos, keep1, got1, came_sums1, tie(tokens, rest), gain_attn, dy1)
    out_share = sum(term.astype(F32) for term in tie(out_terms, token_grad)).T

    return (
        result,
        token_grad,
        query_share,
        pair_share,
        out_share,
        router_share,
        attn_gain_share,
        moe_gain_share,
        up_share,
        down_share,
    )


def solution(mesh):
    in_specs = (
        P(("dp", "expert"), None),
        P("dp"),
        P(("dp", "expert"), None),
        P(("dp", "expert"), None),
        P(("dp", "expert"), None),
        P(None, ("dp", "expert")),
        P(("dp", "expert"), None),
        P(("dp", "expert")),
        P(("dp", "expert")),
        P("expert", None, None),
        P("expert", None, None),
        P(("dp", "expert"), None),
    )
    out_specs = (
        P(("dp", "expert"), None),
        P(("dp", "expert"), None),
        P(("dp", "expert"), None),
        P(("dp", "expert"), None),
        P(None, ("dp", "expert")),
        P(("dp", "expert"), None),
        P(("dp", "expert")),
        P(("dp", "expert")),
        P("expert", "dp", None),
        P("expert", None, "dp"),
    )
    return jax.shard_map(shards, mesh=mesh, in_specs=in_specs, out_specs=out_specs, check_vma=False)
```

```python
import functools

import jax
import jax.numpy as jnp
from jax import lax
from jax.experimental import pallas as pl
from jax.experimental.pallas import tpu as pltpu
from jax.sharding import PartitionSpec as P

D = 1536
HEADS = 24
KV_HEADS = 8
HEAD_DIM = 64
FF = 512
TOP = 8
EXP_DEV = 2

RESIDUAL = 0.22
ATTN_SCALE = 0.015625
LOG2E = 1.4426950408889634
EPSILON = 1e-06
ROPE_BASE = 10000.0
MASKED = -1e30

GROUP = HEADS // KV_HEADS
HALF = HEAD_DIM // 2
BLK = 256
BF = jnp.bfloat16
F32 = jnp.float32
BOTH = ("dp", "expert")


def cost(micros):
    return pl.CostEstimate(flops=micros * 10**9, bytes_accessed=10**4, transcendentals=0)


LONG, SHORT = cost(50), cost(0)


def dot(a, b, ca, cb):
    return lax.dot_general(a, b, (((ca,), (cb,)), ((), ())), preferred_element_type=F32)


def rms_scale(values, gain_vec):
    return (
        values * lax.rsqrt(jnp.mean(values * values, axis=-1, keepdims=True) + EPSILON) * gain_vec
    )


def side_by_side(block):
    return jnp.concatenate(
        [block[h * HEAD_DIM : (h + 1) * HEAD_DIM] for h in range(GROUP)], axis=1
    )


def stacked(wide):
    width = wide.shape[1] // GROUP
    return jnp.concatenate([wide[:, h * width : (h + 1) * width] for h in range(GROUP)], axis=0)


def allowed_keys(start_ref, block, key_block):
    lane = lax.broadcasted_iota(jnp.int32, (1, BLK), 1) + block * BLK
    reach = lane - start_ref[...]
    lane3 = jnp.concatenate([lane] * GROUP, axis=1)
    reach3 = jnp.concatenate([reach] * GROUP, axis=1)
    key_pos = lax.broadcasted_iota(jnp.int32, (BLK, 1), 0) + key_block * BLK
    back = lane3 - key_pos
    return (back >= 0) & (back <= reach3)


def attn_fwd_kernel(first_ref, q_ref, k_ref, vt_ref, start_ref, a_ref, o_ref, lse_ref):
    block = pl.program_id(0)
    query = side_by_side(q_ref[...])
    width = GROUP * BLK

    def step(key_block, carry):
        largest, total, acc = carry
        keys = k_ref[pl.ds(pl.multiple_of(key_block * BLK, BLK), BLK), :]
        values = vt_ref[:, pl.ds(pl.multiple_of(key_block * BLK, BLK), BLK)]
        scores = dot(keys, query, 1, 0) * (ATTN_SCALE * LOG2E)
        scores = jnp.where(allowed_keys(start_ref, block, key_block), scores, MASKED)
        now = jnp.maximum(largest, jnp.max(scores, axis=0, keepdims=True))
        power = jnp.exp2(scores - now)
        fade = jnp.exp2(largest - now)
        total = total * fade + jnp.sum(power, axis=0, keepdims=True)
        acc = acc * fade + dot(values, power.astype(BF), 1, 0)
        return now, total, acc

    largest, total, acc = lax.fori_loop(
        first_ref[block],
        block + 1,
        step,
        (
            jnp.full((1, width), MASKED, F32),
            jnp.zeros((1, width), F32),
            jnp.zeros((HEAD_DIM, width), F32),
        ),
    )
    out = stacked(acc / total)
    o_ref[...] = out
    a_ref[...] = out.astype(BF)
    lse = largest + jnp.log2(total)
    lse_ref[...] = jnp.concatenate(
        [lse[:, h * BLK : (h + 1) * BLK] for h in range(GROUP)]
        + [jnp.zeros((8 - GROUP, BLK), F32)],
        axis=0,
    )


def attn_bwd_kernel(
    first_ref, q_ref, da_ref, o_ref, lse_ref, k_ref, kt_ref, v_ref, start_ref,
    dq_ref, dk_ref, dv_ref, dk_acc, dv_acc,
):
    block = pl.program_id(0)

    @pl.when(block == 0)
    def _():
        dk_acc[...] = jnp.zeros_like(dk_acc)
        dv_acc[...] = jnp.zeros_like(dv_acc)

    query_t = side_by_side(q_ref[...])
    query = query_t.astype(F32).T.astype(BF)
    grad_t = side_by_side(da_ref[0])
    grad_f = grad_t.astype(F32)
    grad = grad_f.T.astype(BF)
    delta = jnp.sum(side_by_side(o_ref[...]) * grad_f, axis=0, keepdims=True)
    lse = jnp.concatenate([lse_ref[h : h + 1, :] for h in range(GROUP)], axis=1)

    def step(key_block, dq):
        rows = pl.ds(pl.multiple_of(key_block * BLK, BLK), BLK)
        keys = k_ref[rows, :]
        scores = dot(keys, query_t, 1, 0) * (ATTN_SCALE * LOG2E)
        scores = jnp.where(allowed_keys(start_ref, block, key_block), scores, MASKED)
        prob = jnp.exp2(scores - lse)
        grad_prob = dot(v_ref[rows, :], grad_t, 1, 0)
        grad_score = (prob * (grad_prob - delta) * ATTN_SCALE).astype(BF)
        dv_acc[rows, :] += dot(prob.astype(BF), grad, 1, 0)
        dk_acc[rows, :] += dot(grad_score, query, 1, 0)
        return dq + dot(kt_ref[:, rows], grad_score, 1, 0)

    dq = lax.fori_loop(
        first_ref[block], block + 1, step, jnp.zeros((HEAD_DIM, GROUP * BLK), F32)
    )
    dq_ref[...] = stacked(dq)

    @pl.when(block == pl.num_programs(0) - 1)
    def _():
        dk_ref[...] = dk_acc[...].T
        dv_ref[...] = dv_acc[...].T


def attn_forward(first, q_t, k, v_t, start):
    seq = q_t.shape[1]
    rows = GROUP * HEAD_DIM
    column = lambda g, first: (0, g)
    whole = lambda g, first: (0, 0)
    return pl.pallas_call(
        attn_fwd_kernel,
        grid_spec=pltpu.PrefetchScalarGridSpec(
            num_scalar_prefetch=1,
            grid=(seq // BLK,),
            in_specs=[
                pl.BlockSpec((rows, BLK), column),
                pl.BlockSpec((seq, HEAD_DIM), whole),
                pl.BlockSpec((HEAD_DIM, seq), whole),
                pl.BlockSpec((1, BLK), column),
            ],
            out_specs=[
                pl.BlockSpec((rows, BLK), column),
                pl.BlockSpec((rows, BLK), column),
                pl.BlockSpec((8, BLK), column),
            ],
        ),
        out_shape=[
            jax.ShapeDtypeStruct((rows, seq), BF),
            jax.ShapeDtypeStruct((rows, seq), F32),
            jax.ShapeDtypeStruct((8, seq), F32),
        ],
        cost_estimate=LONG,
        name="attn_fwd",
    )(first, q_t, k, v_t, start)


def attn_backward(first, q_t, da, o_t, lse, k, k_t, v, start):
    seq = q_t.shape[1]
    rows = GROUP * HEAD_DIM
    column = lambda g, first: (0, g)
    whole = lambda g, first: (0, 0)
    return pl.pallas_call(
        attn_bwd_kernel,
        grid_spec=pltpu.PrefetchScalarGridSpec(
            num_scalar_prefetch=1,
            grid=(seq // BLK,),
            in_specs=[
                pl.BlockSpec((rows, BLK), column),
                pl.BlockSpec((1, rows, BLK), lambda g, first: (g, 0, 0)),
                pl.BlockSpec((rows, BLK), column),
                pl.BlockSpec((8, BLK), column),
                pl.BlockSpec((seq, HEAD_DIM), whole),
                pl.BlockSpec((HEAD_DIM, seq), whole),
                pl.BlockSpec((seq, HEAD_DIM), whole),
                pl.BlockSpec((1, BLK), column),
            ],
            out_specs=[
                pl.BlockSpec((rows, BLK), column),
                pl.BlockSpec((HEAD_DIM, seq), whole),
                pl.BlockSpec((HEAD_DIM, seq), whole),
            ],
            scratch_shapes=[
                pltpu.VMEM((seq, HEAD_DIM), F32),
                pltpu.VMEM((seq, HEAD_DIM), F32),
            ],
        ),
        out_shape=[
            jax.ShapeDtypeStruct((rows, seq), F32),
            jax.ShapeDtypeStruct((HEAD_DIM, seq), F32),
            jax.ShapeDtypeStruct((HEAD_DIM, seq), F32),
        ],
        cost_estimate=cost(20),
        name="attn_bwd",
    )(first, q_t, da, o_t, lse, k, k_t, v, start)


PACK = 384
Q_COLS = GROUP * HEAD_DIM
QKV = Q_COLS + 2 * HEAD_DIM
ROUTE = QKV - 256


def spec(shape, index):
    return pl.BlockSpec(shape, index)


def resident(shape):
    return pl.BlockSpec(
        shape, lambda *_: (0,) * len(shape), pipeline_mode=pl.Buffered(1)
    )


def call(kernel, name, grid, in_specs, out_specs, out_shape, estimate, scratch=()):
    return pl.pallas_call(
        kernel,
        grid_spec=pltpu.PrefetchScalarGridSpec(
            num_scalar_prefetch=1,
            grid=grid,
            in_specs=in_specs,
            out_specs=out_specs,
            scratch_shapes=list(scratch),
        ),
        out_shape=out_shape,
        cost_estimate=estimate,
        name=name,
    )


def shape(dims, kind):
    return jax.ShapeDtypeStruct(dims, kind)


PAIR = 2 * BLK


def far_pair(step, pos):
    return step ^ (pos[0] // 2)


def halves(pos):
    core = pos[0] % 2
    return [pl.ds(pl.multiple_of(start * BLK, BLK), BLK) for start in (1 - core, core)]


def turn_rows(rows_t, cosine, sine):
    out = []
    for h in range(rows_t.shape[0] // HEAD_DIM):
        a = rows_t[h * HEAD_DIM : h * HEAD_DIM + HALF]
        b = rows_t[h * HEAD_DIM + HALF : (h + 1) * HEAD_DIM]
        out += [a * cosine - b * sine, b * cosine + a * sine]
    return jnp.concatenate(out, axis=0)


def norm_of(values):
    return values * lax.rsqrt(jnp.mean(values * values, axis=1, keepdims=True) + EPSILON)


def qkv_kernel(count, pos_ref, *refs):
    pieces = refs[: count + 2]
    w_ref, gain_ref, cos_ref, sin_ref, q_ref, kt_ref, vt_ref, k_ref, v_ref = refs[count + 2 :]
    gain = gain_ref[...]
    for r in range(count):
        if r < count - 2:
            rows = pieces[r][...]
        else:
            at = count - 2 + 2 * (r - count + 2)
            rows = jnp.concatenate([pieces[at][...], pieces[at + 1][...]], axis=0)
        normed = (norm_of(rows.astype(F32)) * gain).astype(BF)
        both = dot(normed, w_ref[...], 1, 0)
        turned = both.T
        place = pl.multiple_of((pos_ref[0] ^ r) * BLK, BLK)
        columns = pl.ds(place, BLK)
        cosine, sine = cos_ref[:, columns], sin_ref[:, columns]
        qk = turn_rows(turned[: Q_COLS + HEAD_DIM], cosine, sine)
        q_ref[:, columns] = qk[:Q_COLS].astype(BF)
        kt_ref[:, columns] = qk[Q_COLS:].astype(BF)
        vt_ref[:, columns] = turned[Q_COLS + HEAD_DIM : QKV].astype(BF)
        k_ref[columns, :] = qk[Q_COLS:].T.astype(BF)
        v_ref[columns, :] = both[:, 256 : 256 + HEAD_DIM].astype(BF)


def qkv_forward(pos, pieces, weights, gain, cosine, sine):
    count = len(pieces) - 2
    seq = cosine.shape[1]
    full = lambda a: resident(a.shape)
    return call(
        functools.partial(qkv_kernel, count),
        "qkv",
        (1,),
        [full(a) for a in pieces] + [full(a) for a in (weights, gain, cosine, sine)],
        [resident(s) for s in ((Q_COLS, seq), (HEAD_DIM, seq), (HEAD_DIM, seq), (seq, HEAD_DIM), (seq, HEAD_DIM))],
        [
            shape((Q_COLS, seq), BF),
            shape((HEAD_DIM, seq), BF),
            shape((HEAD_DIM, seq), BF),
            shape((seq, HEAD_DIM), BF),
            shape((seq, HEAD_DIM), BF),
        ],
        cost(400),
    )(pos, *pieces, weights, gain, cosine, sine)


def send_weights_kernel(groups, members, pos_ref, q_ref, kv_ref, rest_ref, out_ref):
    query, pair, rest = q_ref[...], kv_ref[...], rest_ref[...]
    for j in range(members):
        block = jnp.concatenate(
            [query[:, j * Q_COLS : (j + 1) * Q_COLS]]
            + [pair[:, n * HEAD_DIM : (n + 1) * HEAD_DIM] for n in (j, members + j)]
            + [rest],
            axis=1,
        )
        for i in range(groups):
            out_ref[i * members + j] = block


def send_weights(pos, w_query, w_key_value, rest, groups, members):
    rows = w_query.shape[0]
    full = lambda a: resident(a.shape)
    return call(
        functools.partial(send_weights_kernel, groups, members),
        "send_weights",
        (1,),
        [full(a) for a in (w_query, w_key_value, rest)],
        resident((groups * members, rows, PACK)),
        shape((groups * members, rows, PACK), BF),
        SHORT,
    )(pos, w_query, w_key_value, rest)


def mix_kernel(count, pos_ref, *refs):
    pieces = refs[: count + 2]
    x_ref, w_ref, gain_ref, route_ref, ids_ref = refs[count + 2 : count + 7]
    h2_ref, gates_ref, y1_ref, h2_own_ref, gates_own_ref, heads, y1_all = refs[count + 7 :]
    block = pl.program_id(0)
    pos = pos_ref[0]
    for r in range(count):
        base = (pos ^ r) * Q_COLS
        if r < count - 2:
            heads[pl.ds(pl.multiple_of(base, Q_COLS), Q_COLS), :] = pieces[r][...]
        else:
            half = Q_COLS // 2
            at = count - 2 + 2 * (r - count + 2)
            heads[pl.ds(pl.multiple_of(base, half), half), :] = pieces[at][...]
            heads[pl.ds(pl.multiple_of(base + half, half), half), :] = pieces[at + 1][...]
    route, gain = route_ref[...], gain_ref[...]
    for h in range(2):
        rows = slice(h * BLK, (h + 1) * BLK)
        mixed = dot(heads[:, rows], w_ref[...], 0, 0)
        y1 = x_ref[h ^ (pos % 2)].astype(F32) + RESIDUAL * mixed
        h2 = (norm_of(y1) * gain).astype(BF)
        logits = dot(h2, route, 1, 0)
        lane = lax.broadcasted_iota(jnp.int32, logits.shape, 1) - ROUTE
        ids = ids_ref[h ^ (pos % 2)].T
        chosen = lane == ids[:, 0:1]
        for k in range(1, TOP):
            chosen = chosen | (lane == ids[:, k : k + 1])
        masked = jnp.where(chosen, logits, MASKED)
        power = jnp.where(chosen, jnp.exp(masked - jnp.max(masked, axis=1, keepdims=True)), 0.0)
        gates = power / jnp.sum(power, axis=1, keepdims=True)
        h2_ref[rows] = h2
        gates_ref[rows] = gates
        y1_all[rows] = y1

    @pl.when(block == pos // 2)
    def _():
        mine = halves(pos_ref)[1]
        y1_ref[...] = y1_all[mine]
        h2_own_ref[...] = h2_ref[mine]
        gates_own_ref[...] = gates_ref[mine]


def mix_forward(pos, pieces, x_rel, w_full, gain, weights, ids):
    count = len(pieces) - 2
    seq = ids.shape[0] * BLK
    row = lambda s, pos: (s, 0)
    return call(
        functools.partial(mix_kernel, count),
        "mix",
        (seq // PAIR,),
        [spec((a.shape[0], PAIR), lambda s, pos: (0, s)) for a in pieces]
        + [
            spec((2, BLK, D), lambda s, pos: (far_pair(s, pos), 0, 0)),
            resident(w_full.shape),
            resident(gain.shape),
            pl.BlockSpec((D, 128), lambda s, pos: (0, 2), pipeline_mode=pl.Buffered(1)),
            spec((2, TOP, BLK), lambda s, pos: (far_pair(s, pos), 0, 0)),
        ],
        [
            spec((PAIR, D), row),
            spec((PAIR, 128), row),
            resident((BLK, D)),
            resident((BLK, D)),
            resident((BLK, 128)),
        ],
        [
            shape((seq, D), BF),
            shape((seq, 128), F32),
            shape((BLK, D), F32),
            shape((BLK, D), BF),
            shape((BLK, 128), F32),
        ],
        LONG,
        [pltpu.VMEM((HEADS * HEAD_DIM, PAIR), BF), pltpu.VMEM((PAIR, D), F32)],
    )(pos, *pieces, x_rel, w_full, gain, weights, ids)


def expert_kernel(e, pos_ref, h2_ref, dy_ref, gates_ref, up_ref, down_ref, *refs):
    if e == 0:
        ag_ref, dgu_ref, sum_ref, dg_ref = refs
    else:
        sum_ref, dg_in_ref, ag_ref, dgu_ref, give_ref, keep_ref, dg_ref = refs
    for h, rows in enumerate(halves(pos_ref)):
        h2, dy, gates = h2_ref[rows], dy_ref[rows], gates_ref[rows]
        which = lax.broadcasted_iota(jnp.int32, gates.shape, 1)
        here = which == ROUTE + EXP_DEV * pos_ref[0] + e
        gate = RESIDUAL * jnp.sum(jnp.where(here, gates, 0.0), axis=1, keepdims=True)
        gu = dot(h2, up_ref[0], 1, 0)
        back = dot(dy, down_ref[0], 1, 1)
        g, u = gu[:, :FF], gu[:, FF:]
        sig = 1.0 / (1.0 + jnp.exp(-g))
        swish = g * sig
        act = swish * u
        gate_grad = RESIDUAL * jnp.sum(act * back, axis=1, keepdims=True)
        gate_grad = jnp.where(which == e, gate_grad, 0.0).T[:8]
        ag_ref[rows] = (gate * act).astype(BF)
        dact = gate * back
        dgu = jnp.concatenate(
            [dact * u * (sig * (1.0 + g * (1.0 - sig))), dact * swish], axis=1
        ).astype(BF)
        dgu_ref[rows] = dgu
        total = dot(dgu, up_ref[0], 1, 1)
        place = pos_ref[0] % 2 if h else 1 - pos_ref[0] % 2
        if e == 0:
            sum_ref[rows] = total
            dg_ref[place] = gate_grad
        else:
            (keep_ref if h else give_ref)[0] = (sum_ref[rows] + total).astype(BF)
            dg_ref[place] = dg_in_ref[place] + gate_grad


def expert_pass(e, pos, h2, dy_all, gates, w_gate_up, w_down, carried=()):
    seq = h2.shape[0]
    row = lambda s, pos: (s, 0)
    blocks = lambda s, pos: (s, 0, 0)
    pair = lambda s, pos: (far_pair(s, pos), 0, 0)
    half = seq // PAIR
    one = lambda a: pl.BlockSpec(
        (1,) + a.shape[1:], lambda s, pos: (e, 0, 0), pipeline_mode=pl.Buffered(1)
    )
    sums = (spec((PAIR, D), row), shape((seq, D), F32))
    gate_grads = (spec((2, 8, BLK), blocks), shape((2 * half, 8, BLK), F32))
    outs = [
        (spec((PAIR, FF), row), shape((seq, FF), BF)),
        (spec((PAIR, 2 * FF), row), shape((seq, 2 * FF), BF)),
    ]
    if e == 0:
        outs += [sums, gate_grads]
    else:
        outs += 2 * [(spec((1, BLK, D), pair), shape((half, BLK, D), BF))] + [gate_grads]
    return call(
        functools.partial(expert_kernel, e),
        "expert_%d" % e,
        (half,),
        [spec((PAIR, D), row), spec((PAIR, D), row), spec((PAIR, 128), row)]
        + [one(w_gate_up), one(w_down)]
        + ([sums[0], gate_grads[0]] if carried else []),
        [o[0] for o in outs],
        [o[1] for o in outs],
        cost(5),
    )(pos, h2, dy_all, gates, w_gate_up, w_down, *carried)


def down_grad_kernel(pos_ref, ag_ref, dy_ref, out_ref):
    out_ref[0] = dot(ag_ref[...], dy_ref[...], 0, 0).astype(BF)


def down_grad(pos, ag, dy_all, groups):
    seq = dy_all.shape[0]
    cols = D // groups
    wide = cols if cols % 128 == 0 else D // 4
    out = call(
        down_grad_kernel,
        "down_grad",
        (D // wide,),
        [resident(ag.shape), spec((seq, wide), lambda s, pos: (0, s))],
        spec((1, FF, wide), lambda s, pos: (s, 0, 0)),
        shape((D // wide, FF, wide), BF),
        SHORT,
    )(pos, ag, dy_all)
    if wide == cols:
        return out
    out = jnp.moveaxis(out, 0, 1).reshape(FF, groups, cols)
    return jnp.moveaxis(out, 1, 0)


def up_grad_kernel(pos_ref, h2_ref, dgu_ref, out_ref):
    out_ref[...] = dot(h2_ref[...], dgu_ref[...], 0, 0).astype(BF)


def up_grad(pos, h2, dgu):
    seq = h2.shape[0]
    rows = 384
    return call(
        up_grad_kernel,
        "up_grad",
        (D // rows,),
        [spec((seq, rows), lambda s, pos: (0, s)), resident(dgu.shape)],
        spec((rows, 2 * FF), lambda s, pos: (s, 0)),
        shape((D, 2 * FF), BF),
        SHORT,
    )(pos, h2, dgu)


def combine_kernel(pos_ref, *refs):
    ags = refs[:EXP_DEV]
    down_ref, give_ref, keep_ref = refs[EXP_DEV:]
    for h, rows in enumerate(halves(pos_ref)):
        total = dot(ags[0][rows], down_ref[0], 1, 0)
        for e in range(1, EXP_DEV):
            total = total + dot(ags[e][rows], down_ref[e], 1, 0)
        (keep_ref if h else give_ref)[0] = total.astype(BF)


def combine(pos, ags, w_down):
    seq = ags[0].shape[0]
    half = seq // PAIR
    pair = lambda s, pos: (far_pair(s, pos), 0, 0)
    return call(
        combine_kernel,
        "combine",
        (half,),
        [spec((PAIR, FF), lambda s, pos: (s, 0)) for _ in ags] + [resident(w_down.shape)],
        [spec((1, BLK, D), pair), spec((1, BLK, D), pair)],
        [shape((half, BLK, D), BF), shape((half, BLK, D), BF)],
        SHORT,
    )(pos, *ags, w_down)


def norm_pull(values, gain, grad):
    scale = lax.rsqrt(jnp.mean(values * values, axis=1, keepdims=True) + EPSILON)
    unit = values * scale
    inner = grad * gain
    pulled = scale * (inner - unit * jnp.mean(inner * unit, axis=1, keepdims=True))
    return pulled, jnp.sum(grad * unit, axis=0, keepdims=True)


def middle_kernel(
    members, groups, wide, pos_ref, keep_ref, got_ref, fx_ref, fy_ref, fd_ref, y1_ref, h2_ref, gates_ref, dg_ref, dy_ref,
    route_ref, gain_ref, w_ref, dy1_ref, db_ref, da_ref, router_ref, gain_grad_ref,
):
    dh2 = (
        keep_ref[0].astype(F32)
        + got_ref[0].astype(F32)
        + fx_ref[...].astype(F32)
        + fy_ref[...].astype(F32)
        + fd_ref[...].astype(F32)
    )
    gates, gate_grads = gates_ref[...], dg_ref[...]
    mean = jnp.sum(gates * gate_grads, axis=1, keepdims=True)
    dlogits = (gates * (gate_grads - mean)).astype(BF)
    dh2 = dh2 + dot(dlogits, route_ref[...], 1, 1)
    router_ref[...] = dot(h2_ref[...], dlogits, 0, 0)
    pulled, gain_grad = norm_pull(y1_ref[...], gain_ref[...], dh2)
    gain_grad_ref[...] = jnp.broadcast_to(gain_grad, gain_grad_ref.shape)
    dy1 = dy_ref[...].astype(F32) + pulled
    dy1_ref[...] = dy1
    db = (RESIDUAL * dy1).astype(BF)
    db_ref[...] = db
    da = dot(w_ref[...], db, 1, 1).astype(BF)
    for j in range(members):
        da_ref[j, :Q_COLS] = da[j * Q_COLS : (j + 1) * Q_COLS]
    if wide:
        cols = Q_COLS // groups
        db_t = (RESIDUAL * dy1).T.astype(BF)
        for j in range(members):
            for i in range(groups):
                at, to = (i * members + j) * cols, Q_COLS + i * cols
                da_ref[j, to : to + cols] = db_t[at : at + cols]


def middle(groups, pos, keep, got, sums, y1, h2, gates, dg, dy, weights, gain, w_full):
    rows = y1.shape[0]
    full = lambda a: resident(a.shape)
    first = pl.BlockSpec((1, rows, D), lambda s, pos: (0, 0, 0), pipeline_mode=pl.Buffered(1))
    members = HEADS * HEAD_DIM // Q_COLS
    wide = Q_COLS // groups % 16 == 0
    both = 2 * Q_COLS if wide else Q_COLS
    dy1, db, sent, router, gain_grad = call(
        functools.partial(middle_kernel, members, groups, wide),
        "middle",
        (1,),
        [first, first]
        + [full(a) for a in (*sums, y1, h2, gates, dg, dy)]
        + [
            pl.BlockSpec((D, 128), lambda s, pos: (0, 2), pipeline_mode=pl.Buffered(1)),
            full(gain),
            full(w_full),
        ],
        [
            resident((rows, D)),
            resident((rows, D)),
            resident((members, both, rows)),
            resident((D, 128)),
            resident((8, D)),
        ],
        [
            shape((rows, D), F32),
            shape((rows, D), BF),
            shape((members, both, rows), BF),
            shape((D, 128), F32),
            shape((8, D), F32),
        ],
        cost(100),
    )(pos, keep, got, *sums, y1, h2, gates, dg, dy, weights, gain, w_full)
    if not wide:
        cols = Q_COLS // groups
        db_t = jnp.moveaxis(db.T.reshape(groups, members, cols, rows), 1, 0)
        sent = jnp.concatenate([sent, db_t.reshape(members, Q_COLS, rows)], axis=1)
    return dy1, sent, router, gain_grad


def back_kernel(
    pos_ref, dq_ref, dk_ref, dv_ref, cos_ref, sin_ref, w_ref, give_ref, keep_ref, packed_ref
):
    cosine, sine = cos_ref[...], -sin_ref[...]
    rows_t = jnp.concatenate(
        [
            turn_rows(dq_ref[...], cosine, sine),
            turn_rows(dk_ref[...], cosine, sine),
            dv_ref[...],
            jnp.zeros((PACK - QKV, PAIR), F32),
        ],
        axis=0,
    ).astype(BF)
    packed_ref[...] = rows_t
    for h, rows in enumerate(halves(pos_ref)):
        total = dot(packed_ref[:, rows], w_ref[...], 0, 1).astype(BF)
        (keep_ref if h else give_ref)[0] = total


def back(pos, dq_t, dk_t, dv_t, cosine, sine, weights):
    seq = dq_t.shape[1]
    half = seq // PAIR
    column = lambda s, pos: (0, s)
    pair = lambda s, pos: (far_pair(s, pos), 0, 0)
    return call(
        back_kernel,
        "back",
        (half,),
        [
            spec((Q_COLS, PAIR), column),
            spec((HEAD_DIM, PAIR), column),
            spec((HEAD_DIM, PAIR), column),
            spec((HALF, PAIR), column),
            spec((HALF, PAIR), column),
            resident(weights.shape),
        ],
        [spec((1, BLK, D), pair), spec((1, BLK, D), pair), spec((PACK, PAIR), column)],
        [
            shape((half, BLK, D), BF),
            shape((half, BLK, D), BF),
            shape((PACK, seq), BF),
        ],
        SHORT,
    )(pos, dq_t, dk_t, dv_t, cosine, sine, weights)


def low_pair(values):
    high = values.astype(BF).astype(F32)
    return high, values - high


def pack_kernel(pos_ref, packed_ref, x_ref, gain_ref, w_ref, router_ref, moe_ref, out_ref, acc):
    step = pl.program_id(0)

    @pl.when(step == 0)
    def _():
        acc[...] = jnp.zeros_like(acc)

    term = None
    for h in range(2):
        here = x_ref[h ^ (pos_ref[0] % 2)].astype(F32)
        normed = (norm_of(here) * gain_ref[...]).astype(BF)
        part = dot(packed_ref[:, h * BLK : (h + 1) * BLK], normed, 1, 0)
        term = part if term is None else term + part
    acc[...] += term

    @pl.when(step == pl.num_programs(0) - 1)
    def _():
        main, rest = acc[:256].T, acc[256:].T
        w_main, w_rest = w_ref[:, :256].astype(F32), w_ref[:, 256:].astype(F32)
        lane = lax.broadcasted_iota(jnp.int32, (D, 128), 1)
        gain_attn = (
            jnp.sum(main * w_main, axis=1, keepdims=True)
            + jnp.sum(rest * w_rest, axis=1, keepdims=True)
        ) / w_rest[:, ROUTE + 16 : ROUTE + 17]
        high, low = low_pair(router_ref[...])
        moe_high, moe_low = low_pair(moe_ref[...].T)
        attn_high, attn_low = low_pair(gain_attn)
        rest = rest + high + pltpu.roll(low, 16, 1)
        for at, column in enumerate((moe_high[:, :1], moe_low[:, :1], attn_high, attn_low)):
            rest = jnp.where(lane == ROUTE + 32 + at, column, rest)
        out_ref[:, :256] = main.astype(BF)
        out_ref[:, 256:] = rest.astype(BF)


def pack(pos, packed, x_rel, gain, weights, router, moe):
    seq = packed.shape[1]
    return call(
        pack_kernel,
        "pack",
        (seq // PAIR,),
        [
            spec((PACK, PAIR), lambda s, pos: (0, s)),
            spec((2, BLK, D), lambda s, pos: (far_pair(s, pos), 0, 0)),
            resident(gain.shape),
            resident(weights.shape),
            resident(router.shape),
            resident(moe.shape),
        ],
        resident((D, PACK)),
        shape((D, PACK), BF),
        cost(50),
        [pltpu.VMEM((PACK, D), F32)],
    )(pos, packed, x_rel, gain, weights, router, moe)


def last_kernel(
    pos_ref, keep_ref, got_ref, fx_ref, fy_ref, fd_ref, x_ref, gain_ref, dy1_ref, out_ref
):
    dh1 = (
        keep_ref[0].astype(F32)
        + got_ref[0].astype(F32)
        + fx_ref[...].astype(F32)
        + fy_ref[...].astype(F32)
        + fd_ref[...].astype(F32)
    )
    pulled, _ = norm_pull(x_ref[...].astype(F32), gain_ref[...], dh1)
    out_ref[...] = (dy1_ref[...] + pulled).astype(BF)


def last(pos, keep, got, sums, x, gain, dy1):
    rows = x.shape[0]
    full = lambda a: resident(a.shape)
    first = pl.BlockSpec((1, rows, D), lambda s, pos: (0, 0, 0), pipeline_mode=pl.Buffered(1))
    return call(
        last_kernel,
        "last",
        (1,),
        [first, first] + [full(a) for a in (*sums, x, gain, dy1)],
        resident((rows, D)),
        shape((rows, D), BF),
        cost(50),
    )(pos, keep, got, *sums, x, gain, dy1)


def out_grad_kernel(count, pos_ref, *refs):
    pieces = refs[: count + 2]
    db_ref, out_ref, heads = refs[count + 2 :]
    step = pl.program_id(0)
    pos = pos_ref[0]
    for r in range(count):
        base = (pos ^ r) * Q_COLS
        if r < count - 2:
            heads[pl.ds(pl.multiple_of(base, Q_COLS), Q_COLS), :] = pieces[r][...]
        else:
            half = Q_COLS // 2
            at = count - 2 + 2 * (r - count + 2)
            heads[pl.ds(pl.multiple_of(base, half), half), :] = pieces[at][...]
            heads[pl.ds(pl.multiple_of(base + half, half), half), :] = pieces[at + 1][...]
    term = dot(db_ref[0], heads[...], 1, 1)

    @pl.when(step == 0)
    def _():
        out_ref[...] = term

    @pl.when(step > 0)
    def _():
        out_ref[...] += term


def out_grad(pos, pieces, came):
    count = len(pieces) - 2
    seq, cols = came.shape[0] * BLK, Q_COLS
    return call(
        functools.partial(out_grad_kernel, count),
        "out_grad",
        (seq // BLK,),
        [spec((a.shape[0], BLK), lambda s, pos: (0, s)) for a in pieces]
        + [spec((1, cols, BLK), lambda s, pos: (s, 1, 0))],
        resident((cols, HEADS * HEAD_DIM)),
        shape((cols, HEADS * HEAD_DIM), F32),
        SHORT,
        [pltpu.VMEM((HEADS * HEAD_DIM, BLK), BF)],
    )(pos, *pieces, came).astype(BF)


def unpack_kernel(groups, members, pos_ref, came_ref, query_ref, pair_ref, rest_ref):
    total = None
    for j in range(members):
        here = came_ref[j].astype(F32)
        for i in range(1, groups):
            here = here + came_ref[i * members + j].astype(F32)
        query_ref[:, j * Q_COLS : (j + 1) * Q_COLS] = here[:, :Q_COLS]
        pair_ref[:, j * HEAD_DIM : (j + 1) * HEAD_DIM] = here[:, Q_COLS : Q_COLS + HEAD_DIM]
        at = (members + j) * HEAD_DIM
        pair_ref[:, at : at + HEAD_DIM] = here[:, Q_COLS + HEAD_DIM : QKV]
        rest = here[:, 256:]
        total = rest if total is None else total + rest
    rest_ref[...] = total


def unpack(pos, came, groups):
    devices, rows, _ = came.shape
    members = devices // groups
    return call(
        functools.partial(unpack_kernel, groups, members),
        "unpack",
        (1,),
        [resident(came.shape)],
        [resident((rows, D)), resident((rows, 2 * KV_HEADS * HEAD_DIM)), resident((rows, 128))],
        [
            shape((rows, D), F32),
            shape((rows, 2 * KV_HEADS * HEAD_DIM), F32),
            shape((rows, 128), F32),
        ],
        SHORT,
    )(pos, came)


def swap(values, bit):
    count = lax.axis_size("expert")
    return lax.ppermute(values, "expert", [(i, i ^ bit) for i in range(count)])


def gather_pieces(own, before_last):
    half = own.shape[0] // 2
    x, y = swap(own, 2), swap(own, 4)
    core = swap(own, 1)
    far_a, far_b = tie((swap(x[:half], 4), swap(y[half:], 2)), before_last)
    return [
        own, core, x, swap(x, 1), y, swap(y, 1),
        far_a, far_b, swap(far_a, 1), swap(far_b, 1),
    ]


def gather_direct(own):
    near = [own, swap(own, 2), swap(own, 4), swap(own, 6)]
    return [piece for value in near for piece in (value, swap(value, 1))]


def tie(values, *after):
    return lax.optimization_barrier((values, after))[0]


def pair_sums(keep, got):
    return [(keep[r].astype(F32) + got[r].astype(F32)).astype(BF) for r in (1, 2, 3)]


def send_sums(sums):
    return [swap(sums[0], 2), swap(sums[1], 4), swap(sums[2], 6)]


def send_to_groups(blocks):
    count = lax.axis_size("dp")
    me = lax.axis_index("dp")
    terms = [lax.dynamic_index_in_dim(blocks, me, 0, False)]
    for k in range(1, count):
        sent = lax.dynamic_index_in_dim(blocks, (me + k) % count, 0, False)
        terms.append(lax.ppermute(sent, "dp", [(i, (i + k) % count) for i in range(count)]))
    return terms


def exchange(blocks, axes):
    return lax.all_to_all(blocks, axes, split_axis=0, concat_axis=0, tiled=True)


def shards(
    tokens,
    segment_ids,
    expert_ids,
    w_query,
    w_key_value,
    w_out,
    w_router,
    norm_attn,
    norm_moe,
    w_gate_up,
    w_down,
    grad_out,
):
    tok_rows = tokens.shape[0]
    members = lax.axis_size("expert")
    groups = lax.axis_size("dp")
    position = lax.axis_index("expert")
    pos = position.astype(jnp.int32).reshape(1)
    devices = groups * members
    seq = tok_rows * members
    expert_total = EXP_DEV * members
    in_rows = w_query.shape[0]
    out_cols = w_out.shape[1]
    kv_cols = KV_HEADS * HEAD_DIM

    x_pieces = gather_pieces(tokens, ())

    rest = jnp.concatenate(
        [
            w_router,
            norm_attn[:, None],
            norm_moe[:, None],
            jnp.zeros((in_rows, PACK - QKV - expert_total - 2), BF),
        ],
        axis=1,
    )
    own = send_weights(pos, w_query, w_key_value, rest, groups, members)
    weights = exchange(own, BOTH).reshape(D, PACK)
    gain_attn = weights[:, QKV + expert_total].astype(F32)[None]
    gain_moe = weights[:, QKV + expert_total + 1].astype(F32)[None]

    token_pos = jnp.arange(seq, dtype=jnp.int32)
    start = jnp.sum(
        (segment_ids[:, None] < segment_ids[None, :]).astype(jnp.int32), axis=0, keepdims=True
    )
    first = start[0, ::BLK] // BLK
    frequency = ROPE_BASE ** (-(jnp.arange(HALF, dtype=F32) * 2.0 / HEAD_DIM))
    angles = frequency[:, None] * token_pos.astype(F32)[None, :]
    cosine, sine = jnp.cos(angles), jnp.sin(angles)

    q_t, k_t, v_t, k, v = qkv_forward(
        pos, x_pieces, tie(weights, start, first), gain_attn, cosine, sine
    )
    w_full = lax.all_gather(tie(w_out.T, own), BOTH, axis=0, tiled=True)
    dy_all = lax.all_gather(tie(grad_out, own), "expert", axis=0, tiled=True)
    w_full = w_full.T
    a_t, o_t, lse = attn_forward(first, q_t, k, v_t, start)
    ids = jnp.concatenate(gather_direct(tie(expert_ids, q_t).T), axis=0)
    ids = ids.reshape(members, TOP, tok_rows)
    a_pieces = gather_pieces(a_t, (w_full, ids))
    x_rel = jnp.concatenate(tie(x_pieces, a_t), axis=0).reshape(members, tok_rows, D)

    h2, gates, y1, h2_own, gates_own = mix_forward(
        pos, a_pieces, x_rel, w_full, gain_moe, weights, ids
    )

    ag0, dgu0, *carried = expert_pass(0, pos, h2, dy_all, gates, w_gate_up, w_down)
    down0 = down_grad(pos, ag0, dy_all, groups)
    ag1, dgu1, give, keep, dg = expert_pass(
        1, pos, tie(h2, down0), dy_all, gates, w_gate_up, w_down, carried
    )
    got = swap(give, 1)
    down1 = down_grad(pos, ag1, dy_all, groups)
    sums = pair_sums(keep, tie(got, down1))
    came_sums = send_sums(sums)
    dg = exchange(tie(dg, sums), "expert")[:, :EXP_DEV].reshape(expert_total, tok_rows).T
    dg = jnp.pad(dg, ((0, 0), (ROUTE, 128 - ROUTE - expert_total)))
    up0 = up_grad(pos, *tie((h2, dgu0), sums))
    up1 = up_grad(pos, *tie((h2, dgu1), up0))
    out_give, out_keep = combine(pos, tie((ag0, ag1), up1), w_down)
    spread = functools.partial(lax.psum_scatter, axis_name="dp", scatter_dimension=0, tiled=True)
    down_share = [spread(d.reshape(groups * FF, -1)) for d in (down0, down1)]
    up_share = [spread(d) for d in (up0, up1)]
    keep, down_share[0] = lax.optimization_barrier((keep, down_share[0]))
    out_got = swap(out_give, 1)

    dy1, da, router_wgrad, moe_gain_grad = middle(
        groups, pos, tie(keep, out_keep), got, came_sums, y1, h2_own, gates_own, dg, grad_out,
        weights, gain_moe, w_full,
    )
    da = exchange(da, "expert")
    out_sums = pair_sums(out_keep, tie(out_got, dy1))
    out_came = send_sums(out_sums)

    dq_t, dk_t, dv_t = attn_backward(first, q_t, tie(da, out_sums), o_t, lse, k, k_t, v, start)
    result = y1 + out_keep[0].astype(F32) + out_got[0].astype(F32)
    for term in out_came:
        result = result + term.astype(F32)
    result = result.astype(BF)
    give1, keep1, packed = back(pos, dq_t, dk_t, dv_t, cosine, sine, weights)
    got1 = swap(give1, 1)
    sent = pack(pos, tie(packed, result), x_rel, gain_attn, weights, router_wgrad, moe_gain_grad)
    sums1 = pair_sums(keep1, tie(got1, sent))
    came_sums1 = send_sums(sums1)
    sent = tie(sent, sums1)
    out_wgrad = out_grad(pos, a_pieces, tie(da, sums1)).reshape(groups, out_cols, D)
    out_terms = send_to_groups(out_wgrad)
    came = exchange(sent.reshape(devices, in_rows, PACK), BOTH)
    query_share, pair_share, rest = unpack(pos, came, groups)
    router_share = (
        rest[:, ROUTE : ROUTE + expert_total]
        + rest[:, ROUTE + expert_total : ROUTE + 2 * expert_total]
    )
    moe_gain_share = rest[:, ROUTE + 32] + rest[:, ROUTE + 33]

    attn_gain_share = rest[:, ROUTE + 34] + rest[:, ROUTE + 35]
    token_grad = last(pos, keep1, got1, came_sums1, tie(tokens, rest), gain_attn, dy1)
    out_share = sum(term.astype(F32) for term in tie(out_terms, token_grad)).T

    return (
        result,
        token_grad,
        query_share,
        pair_share,
        out_share,
        router_share,
        attn_gain_share,
        moe_gain_share,
        jnp.stack(up_share).astype(F32),
        jnp.stack(down_share).astype(F32),
    )


def solution(mesh):
    in_specs = (
        P(("dp", "expert"), None),
        P("dp"),
        P(("dp", "expert"), None),
        P(("dp", "expert"), None),
        P(("dp", "expert"), None),
        P(None, ("dp", "expert")),
        P(("dp", "expert"), None),
        P(("dp", "expert")),
        P(("dp", "expert")),
        P("expert", None, None),
        P("expert", None, None),
        P(("dp", "expert"), None),
    )
    out_specs = (
        P(("dp", "expert"), None),
        P(("dp", "expert"), None),
        P(("dp", "expert"), None),
        P(("dp", "expert"), None),
        P(None, ("dp", "expert")),
        P(("dp", "expert"), None),
        P(("dp", "expert")),
        P(("dp", "expert")),
        P("expert", "dp", None),
        P("expert", None, "dp"),
    )
    return jax.shard_map(shards, mesh=mesh, in_specs=in_specs, out_specs=out_specs, check_vma=False)
```

```python
import functools

import jax
import jax.numpy as jnp
from jax import lax
from jax.experimental import pallas as pl
from jax.experimental.pallas import tpu as pltpu
from jax.sharding import PartitionSpec as P

D = 1536
HEADS = 24
KV_HEADS = 8
HEAD_DIM = 64
FF = 512
TOP = 8
EXP_DEV = 2

RESIDUAL = 0.22
ATTN_SCALE = 0.015625
LOG2E = 1.4426950408889634
EPSILON = 1e-06
ROPE_BASE = 10000.0
MASKED = -1e30

GROUP = HEADS // KV_HEADS
HALF = HEAD_DIM // 2
BLK = 256
BF = jnp.bfloat16
F32 = jnp.float32
BOTH = ("dp", "expert")


def cost(micros):
    return pl.CostEstimate(flops=micros * 10**9, bytes_accessed=10**4, transcendentals=0)


LONG, SHORT = cost(50), cost(0)


def dot(a, b, ca, cb):
    return lax.dot_general(a, b, (((ca,), (cb,)), ((), ())), preferred_element_type=F32)


def rms_scale(values, gain_vec):
    return (
        values * lax.rsqrt(jnp.mean(values * values, axis=-1, keepdims=True) + EPSILON) * gain_vec
    )


def side_by_side(block):
    return jnp.concatenate(
        [block[h * HEAD_DIM : (h + 1) * HEAD_DIM] for h in range(GROUP)], axis=1
    )


def stacked(wide):
    width = wide.shape[1] // GROUP
    return jnp.concatenate([wide[:, h * width : (h + 1) * width] for h in range(GROUP)], axis=0)


def allowed_keys(start_ref, block, key_block):
    lane = lax.broadcasted_iota(jnp.int32, (1, BLK), 1) + block * BLK
    reach = lane - start_ref[...]
    lane3 = jnp.concatenate([lane] * GROUP, axis=1)
    reach3 = jnp.concatenate([reach] * GROUP, axis=1)
    key_pos = lax.broadcasted_iota(jnp.int32, (BLK, 1), 0) + key_block * BLK
    back = lane3 - key_pos
    return (back >= 0) & (back <= reach3)


def over_keys(first_ref, block, step, carry):
    clear = jnp.minimum(first_ref[1, block], block)
    carry = lax.fori_loop(first_ref[0, block], clear, functools.partial(step, True), carry)
    pairs = (block - clear) // 2
    carry = lax.fori_loop(
        0, pairs, lambda n, carry: step(False, clear + 2 * n, carry, 2), carry
    )
    carry = lax.fori_loop(clear + 2 * pairs, block, functools.partial(step, False), carry)
    return step(True, block, carry)


def attn_fwd_kernel(first_ref, q_ref, k_ref, vt_ref, start_ref, a_ref, o_ref, lse_ref):
    block = pl.program_id(0)
    query = side_by_side(q_ref[...])
    width = GROUP * BLK

    def step(masked, key_block, carry, count=1):
        largest, total, acc = carry
        rows = pl.ds(pl.multiple_of(key_block * BLK, BLK), count * BLK)
        keys, values = k_ref[rows, :], vt_ref[:, rows]
        scores = dot(keys, query, 1, 0) * (ATTN_SCALE * LOG2E)
        if masked:
            scores = jnp.where(allowed_keys(start_ref, block, key_block), scores, MASKED)
        now = jnp.maximum(largest, jnp.max(scores, axis=0, keepdims=True))
        power = jnp.exp2(scores - now)
        fade = jnp.exp2(largest - now)
        total = total * fade + jnp.sum(power, axis=0, keepdims=True)
        acc = acc * fade + dot(values, power.astype(BF), 1, 0)
        return now, total, acc

    largest, total, acc = over_keys(
        first_ref,
        block,
        step,
        (
            jnp.full((1, width), MASKED, F32),
            jnp.zeros((1, width), F32),
            jnp.zeros((HEAD_DIM, width), F32),
        ),
    )
    out = stacked(acc / total)
    o_ref[...] = out
    a_ref[...] = out.astype(BF)
    lse = largest + jnp.log2(total)
    lse_ref[...] = jnp.concatenate(
        [lse[:, h * BLK : (h + 1) * BLK] for h in range(GROUP)]
        + [jnp.zeros((8 - GROUP, BLK), F32)],
        axis=0,
    )


def attn_bwd_kernel(
    first_ref, q_ref, da_ref, o_ref, lse_ref, k_ref, kt_ref, v_ref, start_ref,
    dq_ref, dk_ref, dv_ref, dk_acc, dv_acc,
):
    block = pl.program_id(0)

    @pl.when(block == 0)
    def _():
        dk_acc[...] = jnp.zeros_like(dk_acc)
        dv_acc[...] = jnp.zeros_like(dv_acc)

    query_t = side_by_side(q_ref[...])
    query = query_t.astype(F32).T.astype(BF)
    grad_t = side_by_side(da_ref[0])
    grad_f = grad_t.astype(F32)
    grad = grad_f.T.astype(BF)
    delta = jnp.sum(side_by_side(o_ref[...]) * grad_f, axis=0, keepdims=True)
    lse = jnp.concatenate([lse_ref[h : h + 1, :] for h in range(GROUP)], axis=1)

    def step(masked, key_block, dq, count=1):
        rows = pl.ds(pl.multiple_of(key_block * BLK, BLK), count * BLK)
        keys = k_ref[rows, :]
        scores = dot(keys, query_t, 1, 0) * (ATTN_SCALE * LOG2E)
        if masked:
            scores = jnp.where(allowed_keys(start_ref, block, key_block), scores, MASKED)
        prob = jnp.exp2(scores - lse)
        grad_prob = dot(v_ref[rows, :], grad_t, 1, 0)
        grad_score = (prob * (grad_prob - delta) * ATTN_SCALE).astype(BF)
        dv_acc[rows, :] += dot(prob.astype(BF), grad, 1, 0)
        dk_acc[rows, :] += dot(grad_score, query, 1, 0)
        return dq + dot(kt_ref[:, rows], grad_score, 1, 0)

    dq = over_keys(first_ref, block, step, jnp.zeros((HEAD_DIM, GROUP * BLK), F32))
    dq_ref[...] = stacked(dq)

    @pl.when(block == pl.num_programs(0) - 1)
    def _():
        dk_ref[...] = dk_acc[...].T
        dv_ref[...] = dv_acc[...].T


def attn_forward(first, q_t, k, v_t, start):
    seq = q_t.shape[1]
    rows = GROUP * HEAD_DIM
    column = lambda g, first: (0, g)
    whole = lambda g, first: (0, 0)
    return pl.pallas_call(
        attn_fwd_kernel,
        grid_spec=pltpu.PrefetchScalarGridSpec(
            num_scalar_prefetch=1,
            grid=(seq // BLK,),
            in_specs=[
                pl.BlockSpec((rows, BLK), column),
                pl.BlockSpec((seq, HEAD_DIM), whole),
                pl.BlockSpec((HEAD_DIM, seq), whole),
                pl.BlockSpec((1, BLK), column),
            ],
            out_specs=[
                pl.BlockSpec((rows, BLK), column),
                pl.BlockSpec((rows, BLK), column),
                pl.BlockSpec((8, BLK), column),
            ],
        ),
        out_shape=[
            jax.ShapeDtypeStruct((rows, seq), BF),
            jax.ShapeDtypeStruct((rows, seq), F32),
            jax.ShapeDtypeStruct((8, seq), F32),
        ],
        cost_estimate=LONG,
        name="attn_fwd",
    )(first, q_t, k, v_t, start)


def attn_backward(first, q_t, da, o_t, lse, k, k_t, v, start):
    seq = q_t.shape[1]
    rows = GROUP * HEAD_DIM
    column = lambda g, first: (0, g)
    whole = lambda g, first: (0, 0)
    return pl.pallas_call(
        attn_bwd_kernel,
        grid_spec=pltpu.PrefetchScalarGridSpec(
            num_scalar_prefetch=1,
            grid=(seq // BLK,),
            in_specs=[
                pl.BlockSpec((rows, BLK), column),
                pl.BlockSpec((1, rows, BLK), lambda g, first: (g, 0, 0)),
                pl.BlockSpec((rows, BLK), column),
                pl.BlockSpec((8, BLK), column),
                pl.BlockSpec((seq, HEAD_DIM), whole),
                pl.BlockSpec((HEAD_DIM, seq), whole),
                pl.BlockSpec((seq, HEAD_DIM), whole),
                pl.BlockSpec((1, BLK), column),
            ],
            out_specs=[
                pl.BlockSpec((rows, BLK), column),
                pl.BlockSpec((HEAD_DIM, seq), whole),
                pl.BlockSpec((HEAD_DIM, seq), whole),
            ],
            scratch_shapes=[
                pltpu.VMEM((seq, HEAD_DIM), F32),
                pltpu.VMEM((seq, HEAD_DIM), F32),
            ],
        ),
        out_shape=[
            jax.ShapeDtypeStruct((rows, seq), F32),
            jax.ShapeDtypeStruct((HEAD_DIM, seq), F32),
            jax.ShapeDtypeStruct((HEAD_DIM, seq), F32),
        ],
        cost_estimate=cost(20),
        name="attn_bwd",
    )(first, q_t, da, o_t, lse, k, k_t, v, start)


PACK = 384
Q_COLS = GROUP * HEAD_DIM
QKV = Q_COLS + 2 * HEAD_DIM
ROUTE = QKV - 256


def spec(shape, index):
    return pl.BlockSpec(shape, index)


def resident(shape):
    return pl.BlockSpec(
        shape, lambda *_: (0,) * len(shape), pipeline_mode=pl.Buffered(1)
    )


def call(kernel, name, grid, in_specs, out_specs, out_shape, estimate, scratch=()):
    return pl.pallas_call(
        kernel,
        grid_spec=pltpu.PrefetchScalarGridSpec(
            num_scalar_prefetch=1,
            grid=grid,
            in_specs=in_specs,
            out_specs=out_specs,
            scratch_shapes=list(scratch),
        ),
        out_shape=out_shape,
        cost_estimate=estimate,
        name=name,
    )


def shape(dims, kind):
    return jax.ShapeDtypeStruct(dims, kind)


PAIR = 2 * BLK


def far_pair(step, pos):
    return step ^ (pos[0] // 2)


def halves(pos):
    core = pos[0] % 2
    return [pl.ds(pl.multiple_of(start * BLK, BLK), BLK) for start in (1 - core, core)]


def turn_rows(rows_t, cosine, sine):
    out = []
    for h in range(rows_t.shape[0] // HEAD_DIM):
        a = rows_t[h * HEAD_DIM : h * HEAD_DIM + HALF]
        b = rows_t[h * HEAD_DIM + HALF : (h + 1) * HEAD_DIM]
        out += [a * cosine - b * sine, b * cosine + a * sine]
    return jnp.concatenate(out, axis=0)


def norm_of(values):
    return values * lax.rsqrt(jnp.mean(values * values, axis=1, keepdims=True) + EPSILON)


def qkv_kernel(count, pos_ref, *refs):
    pieces = refs[: count + 2]
    w_ref, gain_ref, cos_ref, sin_ref, q_ref, kt_ref, vt_ref, k_ref, v_ref = refs[count + 2 :]
    gain = gain_ref[...]
    for r in range(count):
        if r < count - 2:
            rows = pieces[r][...]
        else:
            at = count - 2 + 2 * (r - count + 2)
            rows = jnp.concatenate([pieces[at][...], pieces[at + 1][...]], axis=0)
        normed = (norm_of(rows.astype(F32)) * gain).astype(BF)
        both = dot(normed, w_ref[...], 1, 0)
        turned = both.T
        place = pl.multiple_of((pos_ref[0] ^ r) * BLK, BLK)
        columns = pl.ds(place, BLK)
        cosine, sine = cos_ref[:, columns], sin_ref[:, columns]
        qk = turn_rows(turned[: Q_COLS + HEAD_DIM], cosine, sine)
        q_ref[:, columns] = qk[:Q_COLS].astype(BF)
        kt_ref[:, columns] = qk[Q_COLS:].astype(BF)
        vt_ref[:, columns] = turned[Q_COLS + HEAD_DIM : QKV].astype(BF)
        k_ref[columns, :] = qk[Q_COLS:].T.astype(BF)
        v_ref[columns, :] = both[:, 256 : 256 + HEAD_DIM].astype(BF)


def qkv_forward(pos, pieces, weights, gain, cosine, sine):
    count = len(pieces) - 2
    seq = cosine.shape[1]
    full = lambda a: resident(a.shape)
    return call(
        functools.partial(qkv_kernel, count),
        "qkv",
        (1,),
        [full(a) for a in pieces] + [full(a) for a in (weights, gain, cosine, sine)],
        [resident(s) for s in ((Q_COLS, seq), (HEAD_DIM, seq), (HEAD_DIM, seq), (seq, HEAD_DIM), (seq, HEAD_DIM))],
        [
            shape((Q_COLS, seq), BF),
            shape((HEAD_DIM, seq), BF),
            shape((HEAD_DIM, seq), BF),
            shape((seq, HEAD_DIM), BF),
            shape((seq, HEAD_DIM), BF),
        ],
        cost(400),
    )(pos, *pieces, weights, gain, cosine, sine)


def send_weights_kernel(groups, members, pos_ref, q_ref, kv_ref, rest_ref, out_ref):
    query, pair, rest = q_ref[...], kv_ref[...], rest_ref[...]
    for j in range(members):
        block = jnp.concatenate(
            [query[:, j * Q_COLS : (j + 1) * Q_COLS]]
            + [pair[:, n * HEAD_DIM : (n + 1) * HEAD_DIM] for n in (j, members + j)]
            + [rest],
            axis=1,
        )
        for i in range(groups):
            out_ref[i * members + j] = block


def send_weights(pos, w_query, w_key_value, rest, groups, members):
    rows = w_query.shape[0]
    full = lambda a: resident(a.shape)
    return call(
        functools.partial(send_weights_kernel, groups, members),
        "send_weights",
        (1,),
        [full(a) for a in (w_query, w_key_value, rest)],
        resident((groups * members, rows, PACK)),
        shape((groups * members, rows, PACK), BF),
        SHORT,
    )(pos, w_query, w_key_value, rest)


def mix_kernel(count, pos_ref, *refs):
    pieces = refs[: count + 2]
    x_ref, w_ref, gain_ref, route_ref, ids_ref = refs[count + 2 : count + 7]
    h2_ref, gates_ref, y1_ref, h2_own_ref, gates_own_ref, heads, y1_all = refs[count + 7 :]
    block = pl.program_id(0)
    pos = pos_ref[0]
    for r in range(count):
        base = (pos ^ r) * Q_COLS
        if r < count - 2:
            heads[pl.ds(pl.multiple_of(base, Q_COLS), Q_COLS), :] = pieces[r][...]
        else:
            half = Q_COLS // 2
            at = count - 2 + 2 * (r - count + 2)
            heads[pl.ds(pl.multiple_of(base, half), half), :] = pieces[at][...]
            heads[pl.ds(pl.multiple_of(base + half, half), half), :] = pieces[at + 1][...]
    route, gain = route_ref[...], gain_ref[...]
    for h in range(2):
        rows = slice(h * BLK, (h + 1) * BLK)
        mixed = dot(heads[:, rows], w_ref[...], 0, 0)
        y1 = x_ref[h ^ (pos % 2)].astype(F32) + RESIDUAL * mixed
        h2 = (norm_of(y1) * gain).astype(BF)
        logits = dot(h2, route, 1, 0)
        lane = lax.broadcasted_iota(jnp.int32, logits.shape, 1) - ROUTE
        ids = ids_ref[h ^ (pos % 2)].T
        chosen = lane == ids[:, 0:1]
        for k in range(1, TOP):
            chosen = chosen | (lane == ids[:, k : k + 1])
        masked = jnp.where(chosen, logits, MASKED)
        power = jnp.where(chosen, jnp.exp(masked - jnp.max(masked, axis=1, keepdims=True)), 0.0)
        gates = power / jnp.sum(power, axis=1, keepdims=True)
        h2_ref[rows] = h2
        gates_ref[rows] = gates
        y1_all[rows] = y1

    @pl.when(block == pos // 2)
    def _():
        mine = halves(pos_ref)[1]
        y1_ref[...] = y1_all[mine]
        h2_own_ref[...] = h2_ref[mine]
        gates_own_ref[...] = gates_ref[mine]


def mix_forward(pos, pieces, x_rel, w_full, gain, weights, ids):
    count = len(pieces) - 2
    seq = ids.shape[0] * BLK
    row = lambda s, pos: (s, 0)
    return call(
        functools.partial(mix_kernel, count),
        "mix",
        (seq // PAIR,),
        [spec((a.shape[0], PAIR), lambda s, pos: (0, s)) for a in pieces]
        + [
            spec((2, BLK, D), lambda s, pos: (far_pair(s, pos), 0, 0)),
            resident(w_full.shape),
            resident(gain.shape),
            pl.BlockSpec((D, 128), lambda s, pos: (0, 2), pipeline_mode=pl.Buffered(1)),
            spec((2, TOP, BLK), lambda s, pos: (far_pair(s, pos), 0, 0)),
        ],
        [
            spec((PAIR, D), row),
            spec((PAIR, 128), row),
            resident((BLK, D)),
            resident((BLK, D)),
            resident((BLK, 128)),
        ],
        [
            shape((seq, D), BF),
            shape((seq, 128), F32),
            shape((BLK, D), F32),
            shape((BLK, D), BF),
            shape((BLK, 128), F32),
        ],
        LONG,
        [pltpu.VMEM((HEADS * HEAD_DIM, PAIR), BF), pltpu.VMEM((PAIR, D), F32)],
    )(pos, *pieces, x_rel, w_full, gain, weights, ids)


def expert_kernel(e, pos_ref, h2_ref, dy_ref, gates_ref, up_ref, down_ref, *refs):
    if e == 0:
        ag_ref, dgu_ref, sum_ref, dg_ref, grad_ref, grad_acc = refs

        @pl.when(pl.program_id(0) == 0)
        def _():
            grad_acc[...] = jnp.zeros_like(grad_acc)

    else:
        sum_ref, dg_in_ref, ag_ref, dgu_ref, give_ref, keep_ref, dg_ref = refs
    for h, rows in enumerate(halves(pos_ref)):
        h2, dy, gates = h2_ref[rows], dy_ref[rows], gates_ref[rows]
        which = lax.broadcasted_iota(jnp.int32, gates.shape, 1)
        here = which == ROUTE + EXP_DEV * pos_ref[0] + e
        gate = RESIDUAL * jnp.sum(jnp.where(here, gates, 0.0), axis=1, keepdims=True)
        gu = dot(h2, up_ref[0], 1, 0)
        back = dot(dy, down_ref[0], 1, 1)
        g, u = gu[:, :FF], gu[:, FF:]
        sig = 1.0 / (1.0 + jnp.exp(-g))
        swish = g * sig
        act = swish * u
        gate_grad = RESIDUAL * jnp.sum(act * back, axis=1, keepdims=True)
        gate_grad = jnp.where(which == e, gate_grad, 0.0).T[:8]
        ag_ref[rows] = (gate * act).astype(BF)
        dact = gate * back
        dgu = jnp.concatenate(
            [dact * u * (sig * (1.0 + g * (1.0 - sig))), dact * swish], axis=1
        ).astype(BF)
        dgu_ref[rows] = dgu
        total = dot(dgu, up_ref[0], 1, 1)
        place = pos_ref[0] % 2 if h else 1 - pos_ref[0] % 2
        if e == 0:
            sum_ref[rows] = total
            dg_ref[place] = gate_grad
        else:
            (keep_ref if h else give_ref)[0] = (sum_ref[rows] + total).astype(BF)
            dg_ref[place] = dg_in_ref[place] + gate_grad
    if e == 0:
        grad_acc[...] += dot(ag_ref[...], dy_ref[...], 0, 0)

        @pl.when(pl.program_id(0) == pl.num_programs(0) - 1)
        def _():
            put_shares(grad_ref, grad_acc)


def expert_pass(e, pos, h2, dy_all, gates, w_gate_up, w_down, carried=()):
    seq = h2.shape[0]
    row = lambda s, pos: (s, 0)
    blocks = lambda s, pos: (s, 0, 0)
    pair = lambda s, pos: (far_pair(s, pos), 0, 0)
    half = seq // PAIR
    one = lambda a: pl.BlockSpec(
        (1,) + a.shape[1:], lambda s, pos: (e, 0, 0), pipeline_mode=pl.Buffered(1)
    )
    sums = (spec((PAIR, D), row), shape((seq, D), F32))
    gate_grads = (spec((2, 8, BLK), blocks), shape((2 * half, 8, BLK), F32))
    outs = [
        (spec((PAIR, FF), row), shape((seq, FF), BF)),
        (spec((PAIR, 2 * FF), row), shape((seq, 2 * FF), BF)),
    ]
    if e == 0:
        shares = (D // SHARE, FF, SHARE)
        outs += [sums, gate_grads, (resident(shares), shape(shares, BF))]
    else:
        outs += 2 * [(spec((1, BLK, D), pair), shape((half, BLK, D), BF))] + [gate_grads]
    return call(
        functools.partial(expert_kernel, e),
        "expert_%d" % e,
        (half,),
        [spec((PAIR, D), row), spec((PAIR, D), row), spec((PAIR, 128), row)]
        + [one(w_gate_up), one(w_down)]
        + ([sums[0], gate_grads[0]] if carried else []),
        [o[0] for o in outs],
        [o[1] for o in outs],
        cost(5),
        [] if e else [pltpu.VMEM((FF, D), F32)],
    )(pos, h2, dy_all, gates, w_gate_up, w_down, *carried)


SHARE = 384


def put_shares(out_ref, total):
    for n in range(out_ref.shape[0]):
        out_ref[n] = total[:, n * SHARE : (n + 1) * SHARE].astype(BF)


def by_group(shares, groups):
    cols = D // groups
    if cols == SHARE:
        return shares
    whole = jnp.moveaxis(shares, 0, 1).reshape(FF, groups, cols)
    return jnp.moveaxis(whole, 1, 0)


def down_grad_kernel(pos_ref, ag_ref, dy_ref, out_ref):
    put_shares(out_ref, dot(ag_ref[...], dy_ref[...], 0, 0))


def down_grad(pos, ag, dy_all, groups):
    seq = dy_all.shape[0]
    out = call(
        down_grad_kernel,
        "down_grad",
        (D // (2 * SHARE),),
        [resident(ag.shape), spec((seq, 2 * SHARE), lambda s, pos: (0, s))],
        spec((2, FF, SHARE), lambda s, pos: (s, 0, 0)),
        shape((D // SHARE, FF, SHARE), BF),
        SHORT,
    )(pos, ag, dy_all)
    return by_group(out, groups)


def up_grad_kernel(pos_ref, h2_ref, dgu_ref, out_ref):
    out_ref[...] = dot(h2_ref[...], dgu_ref[...], 0, 0).astype(BF)


def up_grad(pos, h2, dgu):
    seq = h2.shape[0]
    rows = 384
    return call(
        up_grad_kernel,
        "up_grad",
        (D // rows,),
        [spec((seq, rows), lambda s, pos: (0, s)), resident(dgu.shape)],
        spec((rows, 2 * FF), lambda s, pos: (s, 0)),
        shape((D, 2 * FF), BF),
        SHORT,
    )(pos, h2, dgu)


def combine_kernel(pos_ref, *refs):
    ags = refs[:EXP_DEV]
    down_ref, give_ref, keep_ref = refs[EXP_DEV:]
    for h, rows in enumerate(halves(pos_ref)):
        total = dot(ags[0][rows], down_ref[0], 1, 0)
        for e in range(1, EXP_DEV):
            total = total + dot(ags[e][rows], down_ref[e], 1, 0)
        (keep_ref if h else give_ref)[0] = total.astype(BF)


def combine(pos, ags, w_down):
    seq = ags[0].shape[0]
    half = seq // PAIR
    pair = lambda s, pos: (far_pair(s, pos), 0, 0)
    return call(
        combine_kernel,
        "combine",
        (half,),
        [spec((PAIR, FF), lambda s, pos: (s, 0)) for _ in ags] + [resident(w_down.shape)],
        [spec((1, BLK, D), pair), spec((1, BLK, D), pair)],
        [shape((half, BLK, D), BF), shape((half, BLK, D), BF)],
        SHORT,
    )(pos, *ags, w_down)


def norm_pull(values, gain, grad):
    scale = lax.rsqrt(jnp.mean(values * values, axis=1, keepdims=True) + EPSILON)
    unit = values * scale
    inner = grad * gain
    pulled = scale * (inner - unit * jnp.mean(inner * unit, axis=1, keepdims=True))
    return pulled, jnp.sum(grad * unit, axis=0, keepdims=True)


def middle_kernel(
    members, groups, wide, pos_ref, keep_ref, got_ref, fx_ref, fy_ref, fd_ref, y1_ref, h2_ref, gates_ref, dg_ref, dy_ref,
    route_ref, gain_ref, w_ref, dy1_ref, db_ref, da_ref, router_ref, gain_grad_ref,
):
    dh2 = (
        keep_ref[0].astype(F32)
        + got_ref[0].astype(F32)
        + fx_ref[...].astype(F32)
        + fy_ref[...].astype(F32)
        + fd_ref[...].astype(F32)
    )
    gates, gate_grads = gates_ref[...], dg_ref[...]
    mean = jnp.sum(gates * gate_grads, axis=1, keepdims=True)
    dlogits = (gates * (gate_grads - mean)).astype(BF)
    dh2 = dh2 + dot(dlogits, route_ref[...], 1, 1)
    router_ref[...] = dot(h2_ref[...], dlogits, 0, 0)
    pulled, gain_grad = norm_pull(y1_ref[...], gain_ref[...], dh2)
    gain_grad_ref[...] = jnp.broadcast_to(gain_grad, gain_grad_ref.shape)
    dy1 = dy_ref[...].astype(F32) + pulled
    dy1_ref[...] = dy1
    db = (RESIDUAL * dy1).astype(BF)
    db_ref[...] = db
    da = dot(w_ref[...], db, 1, 1).astype(BF)
    for j in range(members):
        da_ref[j, :Q_COLS] = da[j * Q_COLS : (j + 1) * Q_COLS]
    if wide:
        cols = Q_COLS // groups
        db_t = (RESIDUAL * dy1).T.astype(BF)
        for j in range(members):
            for i in range(groups):
                at, to = (i * members + j) * cols, Q_COLS + i * cols
                da_ref[j, to : to + cols] = db_t[at : at + cols]


def middle(groups, pos, keep, got, sums, y1, h2, gates, dg, dy, weights, gain, w_full):
    rows = y1.shape[0]
    full = lambda a: resident(a.shape)
    first = pl.BlockSpec((1, rows, D), lambda s, pos: (0, 0, 0), pipeline_mode=pl.Buffered(1))
    members = HEADS * HEAD_DIM // Q_COLS
    wide = Q_COLS // groups % 16 == 0
    both = 2 * Q_COLS if wide else Q_COLS
    dy1, db, sent, router, gain_grad = call(
        functools.partial(middle_kernel, members, groups, wide),
        "middle",
        (1,),
        [first, first]
        + [full(a) for a in (*sums, y1, h2, gates, dg, dy)]
        + [
            pl.BlockSpec((D, 128), lambda s, pos: (0, 2), pipeline_mode=pl.Buffered(1)),
            full(gain),
            full(w_full),
        ],
        [
            resident((rows, D)),
            resident((rows, D)),
            resident((members, both, rows)),
            resident((D, 128)),
            resident((8, D)),
        ],
        [
            shape((rows, D), F32),
            shape((rows, D), BF),
            shape((members, both, rows), BF),
            shape((D, 128), F32),
            shape((8, D), F32),
        ],
        cost(100),
    )(pos, keep, got, *sums, y1, h2, gates, dg, dy, weights, gain, w_full)
    if not wide:
        cols = Q_COLS // groups
        db_t = jnp.moveaxis(db.T.reshape(groups, members, cols, rows), 1, 0)
        sent = jnp.concatenate([sent, db_t.reshape(members, Q_COLS, rows)], axis=1)
    return dy1, sent, router, gain_grad


def back_kernel(
    pos_ref, dq_ref, dk_ref, dv_ref, cos_ref, sin_ref, w_ref, give_ref, keep_ref, packed_ref
):
    cosine, sine = cos_ref[...], -sin_ref[...]
    rows_t = jnp.concatenate(
        [
            turn_rows(dq_ref[...], cosine, sine),
            turn_rows(dk_ref[...], cosine, sine),
            dv_ref[...],
            jnp.zeros((PACK - QKV, PAIR), F32),
        ],
        axis=0,
    ).astype(BF)
    packed_ref[...] = rows_t
    for h, rows in enumerate(halves(pos_ref)):
        total = dot(packed_ref[:, rows], w_ref[...], 0, 1).astype(BF)
        (keep_ref if h else give_ref)[0] = total


def back(pos, dq_t, dk_t, dv_t, cosine, sine, weights):
    seq = dq_t.shape[1]
    half = seq // PAIR
    column = lambda s, pos: (0, s)
    pair = lambda s, pos: (far_pair(s, pos), 0, 0)
    return call(
        back_kernel,
        "back",
        (half,),
        [
            spec((Q_COLS, PAIR), column),
            spec((HEAD_DIM, PAIR), column),
            spec((HEAD_DIM, PAIR), column),
            spec((HALF, PAIR), column),
            spec((HALF, PAIR), column),
            resident(weights.shape),
        ],
        [spec((1, BLK, D), pair), spec((1, BLK, D), pair), spec((PACK, PAIR), column)],
        [
            shape((half, BLK, D), BF),
            shape((half, BLK, D), BF),
            shape((PACK, seq), BF),
        ],
        SHORT,
    )(pos, dq_t, dk_t, dv_t, cosine, sine, weights)


def low_pair(values):
    high = values.astype(BF).astype(F32)
    return high, values - high


def pack_kernel(pos_ref, packed_ref, x_ref, gain_ref, w_ref, router_ref, moe_ref, out_ref, acc):
    step = pl.program_id(0)

    @pl.when(step == 0)
    def _():
        acc[...] = jnp.zeros_like(acc)

    term = None
    for h in range(2):
        here = x_ref[h ^ (pos_ref[0] % 2)].astype(F32)
        normed = (norm_of(here) * gain_ref[...]).astype(BF)
        part = dot(packed_ref[:, h * BLK : (h + 1) * BLK], normed, 1, 0)
        term = part if term is None else term + part
    acc[...] += term

    @pl.when(step == pl.num_programs(0) - 1)
    def _():
        main, rest = acc[:256].T, acc[256:].T
        w_main, w_rest = w_ref[:, :256].astype(F32), w_ref[:, 256:].astype(F32)
        lane = lax.broadcasted_iota(jnp.int32, (D, 128), 1)
        gain_attn = (
            jnp.sum(main * w_main, axis=1, keepdims=True)
            + jnp.sum(rest * w_rest, axis=1, keepdims=True)
        ) / w_rest[:, ROUTE + 16 : ROUTE + 17]
        high, low = low_pair(router_ref[...])
        moe_high, moe_low = low_pair(moe_ref[...].T)
        attn_high, attn_low = low_pair(gain_attn)
        rest = rest + high + pltpu.roll(low, 16, 1)
        for at, column in enumerate((moe_high[:, :1], moe_low[:, :1], attn_high, attn_low)):
            rest = jnp.where(lane == ROUTE + 32 + at, column, rest)
        out_ref[:, :256] = main.astype(BF)
        out_ref[:, 256:] = rest.astype(BF)


def pack(pos, packed, x_rel, gain, weights, router, moe):
    seq = packed.shape[1]
    return call(
        pack_kernel,
        "pack",
        (seq // PAIR,),
        [
            spec((PACK, PAIR), lambda s, pos: (0, s)),
            spec((2, BLK, D), lambda s, pos: (far_pair(s, pos), 0, 0)),
            resident(gain.shape),
            resident(weights.shape),
            resident(router.shape),
            resident(moe.shape),
        ],
        resident((D, PACK)),
        shape((D, PACK), BF),
        cost(50),
        [pltpu.VMEM((PACK, D), F32)],
    )(pos, packed, x_rel, gain, weights, router, moe)


def last_kernel(
    pos_ref, keep_ref, got_ref, fx_ref, fy_ref, fd_ref, x_ref, gain_ref, dy1_ref, out_ref
):
    dh1 = (
        keep_ref[0].astype(F32)
        + got_ref[0].astype(F32)
        + fx_ref[...].astype(F32)
        + fy_ref[...].astype(F32)
        + fd_ref[...].astype(F32)
    )
    pulled, _ = norm_pull(x_ref[...].astype(F32), gain_ref[...], dh1)
    out_ref[...] = (dy1_ref[...] + pulled).astype(BF)


def last(pos, keep, got, sums, x, gain, dy1):
    rows = x.shape[0]
    full = lambda a: resident(a.shape)
    first = pl.BlockSpec((1, rows, D), lambda s, pos: (0, 0, 0), pipeline_mode=pl.Buffered(1))
    return call(
        last_kernel,
        "last",
        (1,),
        [first, first] + [full(a) for a in (*sums, x, gain, dy1)],
        resident((rows, D)),
        shape((rows, D), BF),
        cost(50),
    )(pos, keep, got, *sums, x, gain, dy1)


def out_grad_kernel(count, pos_ref, *refs):
    pieces = refs[: count + 2]
    db_ref, out_ref, heads = refs[count + 2 :]
    step = pl.program_id(0)
    pos = pos_ref[0]
    for r in range(count):
        base = (pos ^ r) * Q_COLS
        if r < count - 2:
            heads[pl.ds(pl.multiple_of(base, Q_COLS), Q_COLS), :] = pieces[r][...]
        else:
            half = Q_COLS // 2
            at = count - 2 + 2 * (r - count + 2)
            heads[pl.ds(pl.multiple_of(base, half), half), :] = pieces[at][...]
            heads[pl.ds(pl.multiple_of(base + half, half), half), :] = pieces[at + 1][...]
    term = dot(db_ref[0], heads[...], 1, 1)

    @pl.when(step == 0)
    def _():
        out_ref[...] = term

    @pl.when(step > 0)
    def _():
        out_ref[...] += term


def out_grad(pos, pieces, came):
    count = len(pieces) - 2
    seq, cols = came.shape[0] * BLK, Q_COLS
    return call(
        functools.partial(out_grad_kernel, count),
        "out_grad",
        (seq // BLK,),
        [spec((a.shape[0], BLK), lambda s, pos: (0, s)) for a in pieces]
        + [spec((1, cols, BLK), lambda s, pos: (s, 1, 0))],
        resident((cols, HEADS * HEAD_DIM)),
        shape((cols, HEADS * HEAD_DIM), F32),
        SHORT,
        [pltpu.VMEM((HEADS * HEAD_DIM, BLK), BF)],
    )(pos, *pieces, came).astype(BF)


def unpack_kernel(groups, members, pos_ref, came_ref, query_ref, pair_ref, rest_ref):
    total = None
    for j in range(members):
        here = came_ref[j].astype(F32)
        for i in range(1, groups):
            here = here + came_ref[i * members + j].astype(F32)
        query_ref[:, j * Q_COLS : (j + 1) * Q_COLS] = here[:, :Q_COLS]
        pair_ref[:, j * HEAD_DIM : (j + 1) * HEAD_DIM] = here[:, Q_COLS : Q_COLS + HEAD_DIM]
        at = (members + j) * HEAD_DIM
        pair_ref[:, at : at + HEAD_DIM] = here[:, Q_COLS + HEAD_DIM : QKV]
        rest = here[:, 256:]
        total = rest if total is None else total + rest
    rest_ref[...] = total


def unpack(pos, came, groups):
    devices, rows, _ = came.shape
    members = devices // groups
    return call(
        functools.partial(unpack_kernel, groups, members),
        "unpack",
        (1,),
        [resident(came.shape)],
        [resident((rows, D)), resident((rows, 2 * KV_HEADS * HEAD_DIM)), resident((rows, 128))],
        [
            shape((rows, D), F32),
            shape((rows, 2 * KV_HEADS * HEAD_DIM), F32),
            shape((rows, 128), F32),
        ],
        SHORT,
    )(pos, came)


def swap(values, bit):
    count = lax.axis_size("expert")
    return lax.ppermute(values, "expert", [(i, i ^ bit) for i in range(count)])


def gather_pieces(own, before_last):
    half = own.shape[0] // 2
    x, y = swap(own, 2), swap(own, 4)
    core = swap(own, 1)
    far_a, far_b = tie((swap(x[:half], 4), swap(y[half:], 2)), before_last)
    return [
        own, core, x, swap(x, 1), y, swap(y, 1),
        far_a, far_b, swap(far_a, 1), swap(far_b, 1),
    ]


def gather_direct(own):
    near = [own, swap(own, 2), swap(own, 4), swap(own, 6)]
    return [piece for value in near for piece in (value, swap(value, 1))]


def tie(values, *after):
    return lax.optimization_barrier((values, after))[0]


def pair_sums(keep, got):
    return [(keep[r].astype(F32) + got[r].astype(F32)).astype(BF) for r in (1, 2, 3)]


def send_sums(sums):
    return [swap(sums[0], 2), swap(sums[1], 4), swap(sums[2], 6)]


def send_to_groups(blocks):
    count = lax.axis_size("dp")
    me = lax.axis_index("dp")
    terms = [lax.dynamic_index_in_dim(blocks, me, 0, False)]
    for k in range(1, count):
        sent = lax.dynamic_index_in_dim(blocks, (me + k) % count, 0, False)
        terms.append(lax.ppermute(sent, "dp", [(i, (i + k) % count) for i in range(count)]))
    return terms


def exchange(blocks, axes):
    return lax.all_to_all(blocks, axes, split_axis=0, concat_axis=0, tiled=True)


def shards(
    tokens,
    segment_ids,
    expert_ids,
    w_query,
    w_key_value,
    w_out,
    w_router,
    norm_attn,
    norm_moe,
    w_gate_up,
    w_down,
    grad_out,
):
    tok_rows = tokens.shape[0]
    members = lax.axis_size("expert")
    groups = lax.axis_size("dp")
    position = lax.axis_index("expert")
    pos = position.astype(jnp.int32).reshape(1)
    devices = groups * members
    seq = tok_rows * members
    expert_total = EXP_DEV * members
    in_rows = w_query.shape[0]
    out_cols = w_out.shape[1]
    kv_cols = KV_HEADS * HEAD_DIM

    start = jnp.sum(
        (segment_ids[:, None] < segment_ids[None, :]).astype(jnp.int32), axis=0, keepdims=True
    )
    first = jnp.stack([start[0, ::BLK] // BLK, (start[0, BLK - 1 :: BLK] + BLK - 1) // BLK])
    x_pieces = gather_pieces(tokens, (start, first))

    rest = jnp.concatenate(
        [
            w_router,
            norm_attn[:, None],
            norm_moe[:, None],
            jnp.zeros((in_rows, PACK - QKV - expert_total - 2), BF),
        ],
        axis=1,
    )
    own = send_weights(pos, w_query, w_key_value, rest, groups, members)
    weights = exchange(own, BOTH).reshape(D, PACK)
    gain_attn = weights[:, QKV + expert_total].astype(F32)[None]
    gain_moe = weights[:, QKV + expert_total + 1].astype(F32)[None]

    token_pos = jnp.arange(seq, dtype=jnp.int32)
    frequency = ROPE_BASE ** (-(jnp.arange(HALF, dtype=F32) * 2.0 / HEAD_DIM))
    angles = frequency[:, None] * token_pos.astype(F32)[None, :]
    cosine, sine = jnp.cos(angles), jnp.sin(angles)

    q_t, k_t, v_t, k, v = qkv_forward(
        pos, x_pieces, weights, gain_attn, cosine, sine
    )
    w_full = lax.all_gather(tie(w_out.T, own), BOTH, axis=0, tiled=True)
    dy_all = lax.all_gather(tie(grad_out, own), "expert", axis=0, tiled=True)
    w_full = w_full.T
    a_t, o_t, lse = attn_forward(first, q_t, k, v_t, start)
    ids = jnp.concatenate(gather_direct(tie(expert_ids, q_t).T), axis=0)
    ids = ids.reshape(members, TOP, tok_rows)
    a_pieces = gather_pieces(a_t, (w_full, ids))
    x_rel = jnp.concatenate(tie(x_pieces, a_t), axis=0).reshape(members, tok_rows, D)

    h2, gates, y1, h2_own, gates_own = mix_forward(
        pos, a_pieces, x_rel, w_full, gain_moe, weights, ids
    )

    ag0, dgu0, *carried, down0 = expert_pass(0, pos, h2, dy_all, gates, w_gate_up, w_down)
    down0 = by_group(down0, groups)
    ag1, dgu1, give, keep, dg = expert_pass(
        1, pos, h2, dy_all, gates, w_gate_up, w_down, carried
    )
    got = swap(give, 1)
    down1 = down_grad(pos, ag1, dy_all, groups)
    sums = pair_sums(keep, tie(got, down1))
    came_sums = send_sums(sums)
    dg = exchange(tie(dg, sums), "expert")[:, :EXP_DEV].reshape(expert_total, tok_rows).T
    dg = jnp.pad(dg, ((0, 0), (ROUTE, 128 - ROUTE - expert_total)))
    up0 = up_grad(pos, *tie((h2, dgu0), sums))
    up1 = up_grad(pos, *tie((h2, dgu1), up0))
    out_give, out_keep = combine(pos, tie((ag0, ag1), up1), w_down)
    spread = functools.partial(lax.psum_scatter, axis_name="dp", scatter_dimension=0, tiled=True)
    down_share = [spread(d.reshape(groups * FF, -1)) for d in (down0, down1)]
    up_share = [spread(d) for d in (up0, up1)]
    keep, down_share[0] = lax.optimization_barrier((keep, down_share[0]))
    out_got = swap(out_give, 1)

    dy1, da, router_wgrad, moe_gain_grad = middle(
        groups, pos, tie(keep, out_keep), got, came_sums, y1, h2_own, gates_own, dg, grad_out,
        weights, gain_moe, w_full,
    )
    da = exchange(da, "expert")
    out_sums = pair_sums(out_keep, tie(out_got, dy1))
    out_came = send_sums(out_sums)

    dq_t, dk_t, dv_t = attn_backward(first, q_t, tie(da, out_sums), o_t, lse, k, k_t, v, start)
    give1, keep1, packed = back(pos, dq_t, dk_t, dv_t, cosine, sine, weights)
    got1 = swap(give1, 1)
    sent = pack(pos, packed, x_rel, gain_attn, weights, router_wgrad, moe_gain_grad)
    sums1 = pair_sums(keep1, tie(got1, sent))
    came_sums1 = send_sums(sums1)
    result = y1 + out_keep[0].astype(F32) + out_got[0].astype(F32)
    for term in tie(out_came, sums1):
        result = result + term.astype(F32)
    result = result.astype(BF)
    out_wgrad = out_grad(pos, a_pieces, tie(da, result)).reshape(groups, out_cols, D)
    out_terms = send_to_groups(out_wgrad)
    came = exchange(sent.reshape(devices, in_rows, PACK), BOTH)
    token_grad = last(pos, keep1, got1, came_sums1, tokens, gain_attn, dy1)
    query_share, pair_share, rest = unpack(pos, tie(came, token_grad), groups)
    router_share = (
        rest[:, ROUTE : ROUTE + expert_total]
        + rest[:, ROUTE + expert_total : ROUTE + 2 * expert_total]
    )
    moe_gain_share = rest[:, ROUTE + 32] + rest[:, ROUTE + 33]

    attn_gain_share = rest[:, ROUTE + 34] + rest[:, ROUTE + 35]
    out_share = sum(term.astype(F32) for term in tie(out_terms, token_grad)).T

    return (
        result,
        token_grad,
        query_share,
        pair_share,
        out_share,
        router_share,
        attn_gain_share,
        moe_gain_share,
        jnp.stack(tie(up_share, rest, out_share)).astype(F32),
        jnp.stack(down_share).astype(F32),
    )


def solution(mesh):
    in_specs = (
        P(("dp", "expert"), None),
        P("dp"),
        P(("dp", "expert"), None),
        P(("dp", "expert"), None),
        P(("dp", "expert"), None),
        P(None, ("dp", "expert")),
        P(("dp", "expert"), None),
        P(("dp", "expert")),
        P(("dp", "expert")),
        P("expert", None, None),
        P("expert", None, None),
        P(("dp", "expert"), None),
    )
    out_specs = (
        P(("dp", "expert"), None),
        P(("dp", "expert"), None),
        P(("dp", "expert"), None),
        P(("dp", "expert"), None),
        P(None, ("dp", "expert")),
        P(("dp", "expert"), None),
        P(("dp", "expert")),
        P(("dp", "expert")),
        P("expert", "dp", None),
        P("expert", None, "dp"),
    )
    return jax.shard_map(shards, mesh=mesh, in_specs=in_specs, out_specs=out_specs, check_vma=False)
```

```python
import functools

import jax
import jax.numpy as jnp
from jax import lax
from jax.experimental import pallas as pl
from jax.experimental.pallas import tpu as pltpu
from jax.sharding import PartitionSpec as P

D = 1536
HEADS = 24
KV_HEADS = 8
HEAD_DIM = 64
FF = 512
TOP = 8
EXP_DEV = 2

RESIDUAL = 0.22
ATTN_SCALE = 0.015625
LOG2E = 1.4426950408889634
EPSILON = 1e-06
ROPE_BASE = 10000.0
MASKED = -1e30

GROUP = HEADS // KV_HEADS
HALF = HEAD_DIM // 2
BLK = 256
BF = jnp.bfloat16
F32 = jnp.float32
BOTH = ("dp", "expert")


ROOM = {
    "attn_fwd": 8,
    "qkv": 24,
    "back": 12,
    "pack": 20,
    "last": 16,
    "out_grad": 16,
    "unpack": 12,
}


def room(name):
    return pltpu.CompilerParams(vmem_limit_bytes=ROOM[name] << 20 if name in ROOM else None)


def cost(micros):
    return pl.CostEstimate(flops=micros * 10**9, bytes_accessed=10**4, transcendentals=0)


LONG, SHORT = cost(50), cost(0)


def dot(a, b, ca, cb):
    return lax.dot_general(a, b, (((ca,), (cb,)), ((), ())), preferred_element_type=F32)


def rms_scale(values, gain_vec):
    return (
        values * lax.rsqrt(jnp.mean(values * values, axis=-1, keepdims=True) + EPSILON) * gain_vec
    )


def side_by_side(block):
    return jnp.concatenate(
        [block[h * HEAD_DIM : (h + 1) * HEAD_DIM] for h in range(GROUP)], axis=1
    )


def stacked(wide):
    width = wide.shape[1] // GROUP
    return jnp.concatenate([wide[:, h * width : (h + 1) * width] for h in range(GROUP)], axis=0)


def allowed_keys(start_ref, block, key_block):
    lane = lax.broadcasted_iota(jnp.int32, (1, BLK), 1) + block * BLK
    reach = lane - start_ref[...]
    lane3 = jnp.concatenate([lane] * GROUP, axis=1)
    reach3 = jnp.concatenate([reach] * GROUP, axis=1)
    key_pos = lax.broadcasted_iota(jnp.int32, (BLK, 1), 0) + key_block * BLK
    back = lane3 - key_pos
    return (back >= 0) & (back <= reach3)


def over_keys(first_ref, block, step, carry):
    clear = jnp.minimum(first_ref[1, block], block)
    carry = lax.fori_loop(first_ref[0, block], clear, functools.partial(step, True), carry)
    pairs = (block - clear) // 2
    carry = lax.fori_loop(
        0, pairs, lambda n, carry: step(False, clear + 2 * n, carry, 2), carry
    )
    carry = lax.fori_loop(clear + 2 * pairs, block, functools.partial(step, False), carry)
    return step(True, block, carry)


def attn_fwd_kernel(first_ref, q_ref, k_ref, vt_ref, start_ref, a_ref, o_ref, lse_ref):
    block = pl.program_id(0)
    query = side_by_side(q_ref[...])
    width = GROUP * BLK

    def step(masked, key_block, carry, count=1):
        largest, total, acc = carry
        rows = pl.ds(pl.multiple_of(key_block * BLK, BLK), count * BLK)
        keys, values = k_ref[rows, :], vt_ref[:, rows]
        scores = dot(keys, query, 1, 0) * (ATTN_SCALE * LOG2E)
        if masked:
            scores = jnp.where(allowed_keys(start_ref, block, key_block), scores, MASKED)
        now = jnp.maximum(largest, jnp.max(scores, axis=0, keepdims=True))
        power = jnp.exp2(scores - now)
        fade = jnp.exp2(largest - now)
        total = total * fade + jnp.sum(power, axis=0, keepdims=True)
        acc = acc * fade + dot(values, power.astype(BF), 1, 0)
        return now, total, acc

    largest, total, acc = over_keys(
        first_ref,
        block,
        step,
        (
            jnp.full((1, width), MASKED, F32),
            jnp.zeros((1, width), F32),
            jnp.zeros((HEAD_DIM, width), F32),
        ),
    )
    out = stacked(acc / total)
    o_ref[...] = out
    a_ref[...] = out.astype(BF)
    lse = largest + jnp.log2(total)
    lse_ref[...] = jnp.concatenate(
        [lse[:, h * BLK : (h + 1) * BLK] for h in range(GROUP)]
        + [jnp.zeros((8 - GROUP, BLK), F32)],
        axis=0,
    )


def attn_bwd_kernel(
    first_ref, q_ref, da_ref, o_ref, lse_ref, k_ref, kt_ref, v_ref, start_ref,
    dq_ref, dk_ref, dv_ref, dk_acc, dv_acc,
):
    block = pl.program_id(0)

    @pl.when(block == 0)
    def _():
        dk_acc[...] = jnp.zeros_like(dk_acc)
        dv_acc[...] = jnp.zeros_like(dv_acc)

    query_t = side_by_side(q_ref[...])
    query = query_t.astype(F32).T.astype(BF)
    grad_t = side_by_side(da_ref[0])
    grad_f = grad_t.astype(F32)
    grad = grad_f.T.astype(BF)
    delta = jnp.sum(side_by_side(o_ref[...]) * grad_f, axis=0, keepdims=True)
    lse = jnp.concatenate([lse_ref[h : h + 1, :] for h in range(GROUP)], axis=1)

    def step(masked, key_block, dq, count=1):
        rows = pl.ds(pl.multiple_of(key_block * BLK, BLK), count * BLK)
        keys = k_ref[rows, :]
        scores = dot(keys, query_t, 1, 0) * (ATTN_SCALE * LOG2E)
        if masked:
            scores = jnp.where(allowed_keys(start_ref, block, key_block), scores, MASKED)
        prob = jnp.exp2(scores - lse)
        grad_prob = dot(v_ref[rows, :], grad_t, 1, 0)
        grad_score = (prob * (grad_prob - delta) * ATTN_SCALE).astype(BF)
        dv_acc[rows, :] += dot(prob.astype(BF), grad, 1, 0)
        dk_acc[rows, :] += dot(grad_score, query, 1, 0)
        return dq + dot(kt_ref[:, rows], grad_score, 1, 0)

    dq = over_keys(first_ref, block, step, jnp.zeros((HEAD_DIM, GROUP * BLK), F32))
    dq_ref[...] = stacked(dq)

    @pl.when(block == pl.num_programs(0) - 1)
    def _():
        dk_ref[...] = dk_acc[...].T
        dv_ref[...] = dv_acc[...].T


def attn_forward(first, q_t, k, v_t, start):
    seq = q_t.shape[1]
    rows = GROUP * HEAD_DIM
    column = lambda g, first: (0, g)
    whole = lambda g, first: (0, 0)
    return pl.pallas_call(
        attn_fwd_kernel,
        grid_spec=pltpu.PrefetchScalarGridSpec(
            num_scalar_prefetch=1,
            grid=(seq // BLK,),
            in_specs=[
                pl.BlockSpec((rows, BLK), column),
                pl.BlockSpec((seq, HEAD_DIM), whole),
                pl.BlockSpec((HEAD_DIM, seq), whole),
                pl.BlockSpec((1, BLK), column),
            ],
            out_specs=[
                pl.BlockSpec((rows, BLK), column),
                pl.BlockSpec((rows, BLK), column),
                pl.BlockSpec((8, BLK), column),
            ],
        ),
        out_shape=[
            jax.ShapeDtypeStruct((rows, seq), BF),
            jax.ShapeDtypeStruct((rows, seq), F32),
            jax.ShapeDtypeStruct((8, seq), F32),
        ],
        cost_estimate=LONG,
        compiler_params=room("attn_fwd"),
        name="attn_fwd",
    )(first, q_t, k, v_t, start)


def attn_backward(first, q_t, da, o_t, lse, k, k_t, v, start):
    seq = q_t.shape[1]
    rows = GROUP * HEAD_DIM
    column = lambda g, first: (0, g)
    whole = lambda g, first: (0, 0)
    return pl.pallas_call(
        attn_bwd_kernel,
        grid_spec=pltpu.PrefetchScalarGridSpec(
            num_scalar_prefetch=1,
            grid=(seq // BLK,),
            in_specs=[
                pl.BlockSpec((rows, BLK), column),
                pl.BlockSpec((1, rows, BLK), lambda g, first: (g, 0, 0)),
                pl.BlockSpec((rows, BLK), column),
                pl.BlockSpec((8, BLK), column),
                pl.BlockSpec((seq, HEAD_DIM), whole),
                pl.BlockSpec((HEAD_DIM, seq), whole),
                pl.BlockSpec((seq, HEAD_DIM), whole),
                pl.BlockSpec((1, BLK), column),
            ],
            out_specs=[
                pl.BlockSpec((rows, BLK), column),
                pl.BlockSpec((HEAD_DIM, seq), whole),
                pl.BlockSpec((HEAD_DIM, seq), whole),
            ],
            scratch_shapes=[
                pltpu.VMEM((seq, HEAD_DIM), F32),
                pltpu.VMEM((seq, HEAD_DIM), F32),
            ],
        ),
        out_shape=[
            jax.ShapeDtypeStruct((rows, seq), F32),
            jax.ShapeDtypeStruct((HEAD_DIM, seq), F32),
            jax.ShapeDtypeStruct((HEAD_DIM, seq), F32),
        ],
        cost_estimate=cost(20),
        compiler_params=room("attn_bwd"),
        name="attn_bwd",
    )(first, q_t, da, o_t, lse, k, k_t, v, start)


PACK = 384
Q_COLS = GROUP * HEAD_DIM
QKV = Q_COLS + 2 * HEAD_DIM
ROUTE = QKV - 256


def spec(shape, index):
    return pl.BlockSpec(shape, index)


def resident(shape):
    return pl.BlockSpec(
        shape, lambda *_: (0,) * len(shape), pipeline_mode=pl.Buffered(1)
    )


def call(kernel, name, grid, in_specs, out_specs, out_shape, estimate, scratch=()):
    return pl.pallas_call(
        kernel,
        grid_spec=pltpu.PrefetchScalarGridSpec(
            num_scalar_prefetch=1,
            grid=grid,
            in_specs=in_specs,
            out_specs=out_specs,
            scratch_shapes=list(scratch),
        ),
        out_shape=out_shape,
        cost_estimate=estimate,
        compiler_params=room(name),
        name=name,
    )


def shape(dims, kind):
    return jax.ShapeDtypeStruct(dims, kind)


PAIR = 2 * BLK


def far_pair(step, pos):
    return step ^ (pos[0] // 2)


def halves(pos):
    core = pos[0] % 2
    return [pl.ds(pl.multiple_of(start * BLK, BLK), BLK) for start in (1 - core, core)]


def turn_rows(rows_t, cosine, sine):
    out = []
    for h in range(rows_t.shape[0] // HEAD_DIM):
        a = rows_t[h * HEAD_DIM : h * HEAD_DIM + HALF]
        b = rows_t[h * HEAD_DIM + HALF : (h + 1) * HEAD_DIM]
        out += [a * cosine - b * sine, b * cosine + a * sine]
    return jnp.concatenate(out, axis=0)


def norm_of(values):
    return values * lax.rsqrt(jnp.mean(values * values, axis=1, keepdims=True) + EPSILON)


def qkv_kernel(count, pos_ref, *refs):
    pieces = refs[: count + 2]
    w_ref, gain_ref, cos_ref, sin_ref, q_ref, kt_ref, vt_ref, k_ref, v_ref = refs[count + 2 :]
    gain = gain_ref[...]
    for r in range(count):
        if r < count - 2:
            rows = pieces[r][...]
        else:
            at = count - 2 + 2 * (r - count + 2)
            rows = jnp.concatenate([pieces[at][...], pieces[at + 1][...]], axis=0)
        normed = (norm_of(rows.astype(F32)) * gain).astype(BF)
        both = dot(normed, w_ref[...], 1, 0)
        turned = both.T
        place = pl.multiple_of((pos_ref[0] ^ r) * BLK, BLK)
        columns = pl.ds(place, BLK)
        cosine, sine = cos_ref[:, columns], sin_ref[:, columns]
        qk = turn_rows(turned[: Q_COLS + HEAD_DIM], cosine, sine)
        q_ref[:, columns] = qk[:Q_COLS].astype(BF)
        kt_ref[:, columns] = qk[Q_COLS:].astype(BF)
        vt_ref[:, columns] = turned[Q_COLS + HEAD_DIM : QKV].astype(BF)
        k_ref[columns, :] = qk[Q_COLS:].T.astype(BF)
        v_ref[columns, :] = both[:, 256 : 256 + HEAD_DIM].astype(BF)


def qkv_forward(pos, pieces, weights, gain, cosine, sine):
    count = len(pieces) - 2
    seq = cosine.shape[1]
    full = lambda a: resident(a.shape)
    return call(
        functools.partial(qkv_kernel, count),
        "qkv",
        (1,),
        [full(a) for a in pieces] + [full(a) for a in (weights, gain, cosine, sine)],
        [resident(s) for s in ((Q_COLS, seq), (HEAD_DIM, seq), (HEAD_DIM, seq), (seq, HEAD_DIM), (seq, HEAD_DIM))],
        [
            shape((Q_COLS, seq), BF),
            shape((HEAD_DIM, seq), BF),
            shape((HEAD_DIM, seq), BF),
            shape((seq, HEAD_DIM), BF),
            shape((seq, HEAD_DIM), BF),
        ],
        cost(400),
    )(pos, *pieces, weights, gain, cosine, sine)


def as_column(row):
    count = row.shape[1]
    here = lax.broadcasted_iota(jnp.int32, (count, count), 0)
    there = lax.broadcasted_iota(jnp.int32, (count, count), 1)
    return jnp.sum(jnp.where(here == there, row.astype(F32), 0.0), axis=1, keepdims=True)


def send_weights_kernel(
    groups, members, pos_ref, q_ref, kv_ref, route_ref, attn_ref, moe_ref, out_ref
):
    query, pair = q_ref[...], kv_ref[...]
    rows, experts = route_ref.shape
    route = jnp.concatenate(
        [route_ref[...].astype(F32), jnp.zeros((rows, PACK - QKV - experts), F32)], axis=1
    )
    lane = lax.broadcasted_iota(jnp.int32, route.shape, 1)
    rest = jnp.where(lane == experts, as_column(attn_ref[...]), route)
    rest = jnp.where(lane == experts + 1, as_column(moe_ref[...]), rest).astype(BF)
    for j in range(members):
        block = jnp.concatenate(
            [query[:, j * Q_COLS : (j + 1) * Q_COLS]]
            + [pair[:, n * HEAD_DIM : (n + 1) * HEAD_DIM] for n in (j, members + j)]
            + [rest],
            axis=1,
        )
        for i in range(groups):
            out_ref[i * members + j] = block


def send_weights(pos, parts, groups, members):
    rows = parts[0].shape[0]
    full = lambda a: resident(a.shape)
    return call(
        functools.partial(send_weights_kernel, groups, members),
        "send_weights",
        (1,),
        [full(a) for a in parts],
        resident((groups * members, rows, PACK)),
        shape((groups * members, rows, PACK), BF),
        SHORT,
    )(pos, *parts)


def mix_kernel(count, pos_ref, *refs):
    pieces = refs[: count + 2]
    x_ref, w_ref, gain_ref, route_ref, ids_ref = refs[count + 2 : count + 7]
    h2_ref, gates_ref, y1_ref, h2_own_ref, gates_own_ref, heads, y1_all = refs[count + 7 :]
    block = pl.program_id(0)
    pos = pos_ref[0]
    for r in range(count):
        base = (pos ^ r) * Q_COLS
        if r < count - 2:
            heads[pl.ds(pl.multiple_of(base, Q_COLS), Q_COLS), :] = pieces[r][...]
        else:
            half = Q_COLS // 2
            at = count - 2 + 2 * (r - count + 2)
            heads[pl.ds(pl.multiple_of(base, half), half), :] = pieces[at][...]
            heads[pl.ds(pl.multiple_of(base + half, half), half), :] = pieces[at + 1][...]
    route, gain = route_ref[...], gain_ref[...]
    for h in range(2):
        rows = slice(h * BLK, (h + 1) * BLK)
        mixed = dot(heads[:, rows], w_ref[...], 0, 0)
        y1 = x_ref[h ^ (pos % 2)].astype(F32) + RESIDUAL * mixed
        h2 = (norm_of(y1) * gain).astype(BF)
        logits = dot(h2, route, 1, 0)
        lane = lax.broadcasted_iota(jnp.int32, logits.shape, 1) - ROUTE
        ids = ids_ref[h ^ (pos % 2)].T
        chosen = lane == ids[:, 0:1]
        for k in range(1, TOP):
            chosen = chosen | (lane == ids[:, k : k + 1])
        masked = jnp.where(chosen, logits, MASKED)
        power = jnp.where(chosen, jnp.exp(masked - jnp.max(masked, axis=1, keepdims=True)), 0.0)
        gates = power / jnp.sum(power, axis=1, keepdims=True)
        h2_ref[rows] = h2
        gates_ref[rows] = gates
        y1_all[rows] = y1

    @pl.when(block == pos // 2)
    def _():
        mine = halves(pos_ref)[1]
        y1_ref[...] = y1_all[mine]
        h2_own_ref[...] = h2_ref[mine]
        gates_own_ref[...] = gates_ref[mine]


def mix_forward(pos, pieces, x_rel, w_full, gain, weights, ids):
    count = len(pieces) - 2
    seq = ids.shape[0] * BLK
    row = lambda s, pos: (s, 0)
    return call(
        functools.partial(mix_kernel, count),
        "mix",
        (seq // PAIR,),
        [spec((a.shape[0], PAIR), lambda s, pos: (0, s)) for a in pieces]
        + [
            spec((2, BLK, D), lambda s, pos: (far_pair(s, pos), 0, 0)),
            resident(w_full.shape),
            resident(gain.shape),
            pl.BlockSpec((D, 128), lambda s, pos: (0, 2), pipeline_mode=pl.Buffered(1)),
            spec((2, TOP, BLK), lambda s, pos: (far_pair(s, pos), 0, 0)),
        ],
        [
            spec((PAIR, D), row),
            spec((PAIR, 128), row),
            resident((BLK, D)),
            resident((BLK, D)),
            resident((BLK, 128)),
        ],
        [
            shape((seq, D), BF),
            shape((seq, 128), F32),
            shape((BLK, D), F32),
            shape((BLK, D), BF),
            shape((BLK, 128), F32),
        ],
        LONG,
        [pltpu.VMEM((HEADS * HEAD_DIM, PAIR), BF), pltpu.VMEM((PAIR, D), F32)],
    )(pos, *pieces, x_rel, w_full, gain, weights, ids)


def expert_kernel(e, pos_ref, h2_ref, dy_ref, gates_ref, up_ref, down_ref, *refs):
    if e == 0:
        ag_ref, dgu_ref, sum_ref, dg_ref, grad_ref, grad_acc = refs

        @pl.when(pl.program_id(0) == 0)
        def _():
            grad_acc[...] = jnp.zeros_like(grad_acc)

    else:
        sum_ref, dg_in_ref, ag_ref, dgu_ref, give_ref, keep_ref, dg_ref = refs
    for h, rows in enumerate(halves(pos_ref)):
        h2, dy, gates = h2_ref[rows], dy_ref[rows], gates_ref[rows]
        which = lax.broadcasted_iota(jnp.int32, gates.shape, 1)
        here = which == ROUTE + EXP_DEV * pos_ref[0] + e
        gate = RESIDUAL * jnp.sum(jnp.where(here, gates, 0.0), axis=1, keepdims=True)
        gu = dot(h2, up_ref[0], 1, 0)
        back = dot(dy, down_ref[0], 1, 1)
        g, u = gu[:, :FF], gu[:, FF:]
        sig = 1.0 / (1.0 + jnp.exp(-g))
        swish = g * sig
        act = swish * u
        gate_grad = RESIDUAL * jnp.sum(act * back, axis=1, keepdims=True)
        gate_grad = jnp.where(which == e, gate_grad, 0.0).T[:8]
        ag_ref[rows] = (gate * act).astype(BF)
        dact = gate * back
        dgu = jnp.concatenate(
            [dact * u * (sig * (1.0 + g * (1.0 - sig))), dact * swish], axis=1
        ).astype(BF)
        dgu_ref[rows] = dgu
        total = dot(dgu, up_ref[0], 1, 1)
        place = pos_ref[0] % 2 if h else 1 - pos_ref[0] % 2
        if e == 0:
            sum_ref[rows] = total
            dg_ref[place] = gate_grad
        else:
            (keep_ref if h else give_ref)[0] = (sum_ref[rows] + total).astype(BF)
            dg_ref[place] = dg_in_ref[place] + gate_grad
    if e == 0:
        grad_acc[...] += dot(ag_ref[...], dy_ref[...], 0, 0)

        @pl.when(pl.program_id(0) == pl.num_programs(0) - 1)
        def _():
            put_shares(grad_ref, grad_acc)


def expert_pass(e, pos, h2, dy_all, gates, w_gate_up, w_down, carried=()):
    seq = h2.shape[0]
    row = lambda s, pos: (s, 0)
    blocks = lambda s, pos: (s, 0, 0)
    pair = lambda s, pos: (far_pair(s, pos), 0, 0)
    half = seq // PAIR
    one = lambda a: pl.BlockSpec(
        (1,) + a.shape[1:], lambda s, pos: (e, 0, 0), pipeline_mode=pl.Buffered(1)
    )
    sums = (spec((PAIR, D), row), shape((seq, D), F32))
    gate_grads = (spec((2, 8, BLK), blocks), shape((2 * half, 8, BLK), F32))
    outs = [
        (spec((PAIR, FF), row), shape((seq, FF), BF)),
        (spec((PAIR, 2 * FF), row), shape((seq, 2 * FF), BF)),
    ]
    if e == 0:
        shares = (D // SHARE, FF, SHARE)
        outs += [sums, gate_grads, (resident(shares), shape(shares, BF))]
    else:
        outs += 2 * [(spec((1, BLK, D), pair), shape((half, BLK, D), BF))] + [gate_grads]
    return call(
        functools.partial(expert_kernel, e),
        "expert_%d" % e,
        (half,),
        [spec((PAIR, D), row), spec((PAIR, D), row), spec((PAIR, 128), row)]
        + [one(w_gate_up), one(w_down)]
        + ([sums[0], gate_grads[0]] if carried else []),
        [o[0] for o in outs],
        [o[1] for o in outs],
        cost(5),
        [] if e else [pltpu.VMEM((FF, D), F32)],
    )(pos, h2, dy_all, gates, w_gate_up, w_down, *carried)


SHARE = 384


def put_shares(out_ref, total):
    for n in range(out_ref.shape[0]):
        out_ref[n] = total[:, n * SHARE : (n + 1) * SHARE].astype(BF)


def by_group(shares, groups):
    cols = D // groups
    if cols == SHARE:
        return shares
    whole = jnp.moveaxis(shares, 0, 1).reshape(FF, groups, cols)
    return jnp.moveaxis(whole, 1, 0)


def down_grad_kernel(pos_ref, ag_ref, dy_ref, out_ref):
    put_shares(out_ref, dot(ag_ref[...], dy_ref[...], 0, 0))


def down_grad(pos, ag, dy_all, groups):
    seq = dy_all.shape[0]
    out = call(
        down_grad_kernel,
        "down_grad",
        (D // (2 * SHARE),),
        [resident(ag.shape), spec((seq, 2 * SHARE), lambda s, pos: (0, s))],
        spec((2, FF, SHARE), lambda s, pos: (s, 0, 0)),
        shape((D // SHARE, FF, SHARE), BF),
        SHORT,
    )(pos, ag, dy_all)
    return by_group(out, groups)


def up_grad_kernel(pos_ref, h2_ref, dgu_ref, out_ref):
    out_ref[...] = dot(h2_ref[...], dgu_ref[...], 0, 0).astype(BF)


def up_grad(pos, h2, dgu):
    seq = h2.shape[0]
    rows = 384
    return call(
        up_grad_kernel,
        "up_grad",
        (D // rows,),
        [spec((seq, rows), lambda s, pos: (0, s)), resident(dgu.shape)],
        spec((rows, 2 * FF), lambda s, pos: (s, 0)),
        shape((D, 2 * FF), BF),
        SHORT,
    )(pos, h2, dgu)


def combine_kernel(pos_ref, *refs):
    ags = refs[:EXP_DEV]
    down_ref, give_ref, keep_ref = refs[EXP_DEV:]
    for h, rows in enumerate(halves(pos_ref)):
        total = dot(ags[0][rows], down_ref[0], 1, 0)
        for e in range(1, EXP_DEV):
            total = total + dot(ags[e][rows], down_ref[e], 1, 0)
        (keep_ref if h else give_ref)[0] = total.astype(BF)


def combine(pos, ags, w_down):
    seq = ags[0].shape[0]
    half = seq // PAIR
    pair = lambda s, pos: (far_pair(s, pos), 0, 0)
    return call(
        combine_kernel,
        "combine",
        (half,),
        [spec((PAIR, FF), lambda s, pos: (s, 0)) for _ in ags] + [resident(w_down.shape)],
        [spec((1, BLK, D), pair), spec((1, BLK, D), pair)],
        [shape((half, BLK, D), BF), shape((half, BLK, D), BF)],
        SHORT,
    )(pos, *ags, w_down)


def norm_pull(values, gain, grad):
    scale = lax.rsqrt(jnp.mean(values * values, axis=1, keepdims=True) + EPSILON)
    unit = values * scale
    inner = grad * gain
    pulled = scale * (inner - unit * jnp.mean(inner * unit, axis=1, keepdims=True))
    return pulled, jnp.sum(grad * unit, axis=0, keepdims=True)


def middle_kernel(
    members, groups, wide, pos_ref, keep_ref, got_ref, fx_ref, fy_ref, fd_ref, y1_ref, h2_ref, gates_ref, dg_ref, dy_ref,
    route_ref, gain_ref, w_ref, dy1_ref, db_ref, da_ref, router_ref, gain_grad_ref,
):
    dh2 = (
        keep_ref[0].astype(F32)
        + got_ref[0].astype(F32)
        + fx_ref[...].astype(F32)
        + fy_ref[...].astype(F32)
        + fd_ref[...].astype(F32)
    )
    gates, gate_grads = gates_ref[...], dg_ref[...]
    mean = jnp.sum(gates * gate_grads, axis=1, keepdims=True)
    dlogits = (gates * (gate_grads - mean)).astype(BF)
    dh2 = dh2 + dot(dlogits, route_ref[...], 1, 1)
    router_ref[...] = dot(h2_ref[...], dlogits, 0, 0)
    pulled, gain_grad = norm_pull(y1_ref[...], gain_ref[...], dh2)
    gain_grad_ref[...] = jnp.broadcast_to(gain_grad, gain_grad_ref.shape)
    dy1 = dy_ref[...].astype(F32) + pulled
    dy1_ref[...] = dy1
    db = (RESIDUAL * dy1).astype(BF)
    db_ref[...] = db
    da = dot(w_ref[...], db, 1, 1).astype(BF)
    for j in range(members):
        da_ref[j, :Q_COLS] = da[j * Q_COLS : (j + 1) * Q_COLS]
    if wide:
        cols = Q_COLS // groups
        db_t = (RESIDUAL * dy1).T.astype(BF)
        for j in range(members):
            for i in range(groups):
                at, to = (i * members + j) * cols, Q_COLS + i * cols
                da_ref[j, to : to + cols] = db_t[at : at + cols]


def middle(groups, pos, keep, got, sums, y1, h2, gates, dg, dy, weights, gain, w_full):
    rows = y1.shape[0]
    full = lambda a: resident(a.shape)
    first = pl.BlockSpec((1, rows, D), lambda s, pos: (0, 0, 0), pipeline_mode=pl.Buffered(1))
    members = HEADS * HEAD_DIM // Q_COLS
    wide = Q_COLS // groups % 16 == 0
    both = 2 * Q_COLS if wide else Q_COLS
    dy1, db, sent, router, gain_grad = call(
        functools.partial(middle_kernel, members, groups, wide),
        "middle",
        (1,),
        [first, first]
        + [full(a) for a in (*sums, y1, h2, gates, dg, dy)]
        + [
            pl.BlockSpec((D, 128), lambda s, pos: (0, 2), pipeline_mode=pl.Buffered(1)),
            full(gain),
            full(w_full),
        ],
        [
            resident((rows, D)),
            resident((rows, D)),
            resident((members, both, rows)),
            resident((D, 128)),
            resident((8, D)),
        ],
        [
            shape((rows, D), F32),
            shape((rows, D), BF),
            shape((members, both, rows), BF),
            shape((D, 128), F32),
            shape((8, D), F32),
        ],
        cost(100),
    )(pos, keep, got, *sums, y1, h2, gates, dg, dy, weights, gain, w_full)
    if not wide:
        cols = Q_COLS // groups
        db_t = jnp.moveaxis(db.T.reshape(groups, members, cols, rows), 1, 0)
        sent = jnp.concatenate([sent, db_t.reshape(members, Q_COLS, rows)], axis=1)
    return dy1, sent, router, gain_grad


def back_kernel(
    pos_ref, dq_ref, dk_ref, dv_ref, cos_ref, sin_ref, w_ref, give_ref, keep_ref, packed_ref
):
    cosine, sine = cos_ref[...], -sin_ref[...]
    rows_t = jnp.concatenate(
        [
            turn_rows(dq_ref[...], cosine, sine),
            turn_rows(dk_ref[...], cosine, sine),
            dv_ref[...],
            jnp.zeros((PACK - QKV, PAIR), F32),
        ],
        axis=0,
    ).astype(BF)
    packed_ref[...] = rows_t
    for h, rows in enumerate(halves(pos_ref)):
        total = dot(packed_ref[:, rows], w_ref[...], 0, 1).astype(BF)
        (keep_ref if h else give_ref)[0] = total


def back(pos, dq_t, dk_t, dv_t, cosine, sine, weights):
    seq = dq_t.shape[1]
    half = seq // PAIR
    column = lambda s, pos: (0, s)
    pair = lambda s, pos: (far_pair(s, pos), 0, 0)
    return call(
        back_kernel,
        "back",
        (half,),
        [
            spec((Q_COLS, PAIR), column),
            spec((HEAD_DIM, PAIR), column),
            spec((HEAD_DIM, PAIR), column),
            spec((HALF, PAIR), column),
            spec((HALF, PAIR), column),
            resident(weights.shape),
        ],
        [spec((1, BLK, D), pair), spec((1, BLK, D), pair), spec((PACK, PAIR), column)],
        [
            shape((half, BLK, D), BF),
            shape((half, BLK, D), BF),
            shape((PACK, seq), BF),
        ],
        SHORT,
    )(pos, dq_t, dk_t, dv_t, cosine, sine, weights)


def low_pair(values):
    high = values.astype(BF).astype(F32)
    return high, values - high


def pack_kernel(pos_ref, packed_ref, x_ref, gain_ref, w_ref, router_ref, moe_ref, out_ref, acc):
    step = pl.program_id(0)

    @pl.when(step == 0)
    def _():
        acc[...] = jnp.zeros_like(acc)

    term = None
    for h in range(2):
        here = x_ref[h ^ (pos_ref[0] % 2)].astype(F32)
        normed = (norm_of(here) * gain_ref[...]).astype(BF)
        part = dot(packed_ref[:, h * BLK : (h + 1) * BLK], normed, 1, 0)
        term = part if term is None else term + part
    acc[...] += term

    @pl.when(step == pl.num_programs(0) - 1)
    def _():
        main, rest = acc[:256].T, acc[256:].T
        w_main, w_rest = w_ref[:, :256].astype(F32), w_ref[:, 256:].astype(F32)
        lane = lax.broadcasted_iota(jnp.int32, (D, 128), 1)
        gain_attn = (
            jnp.sum(main * w_main, axis=1, keepdims=True)
            + jnp.sum(rest * w_rest, axis=1, keepdims=True)
        ) / w_rest[:, ROUTE + 16 : ROUTE + 17]
        high, low = low_pair(router_ref[...])
        moe_high, moe_low = low_pair(moe_ref[...].T)
        attn_high, attn_low = low_pair(gain_attn)
        rest = rest + high + pltpu.roll(low, 16, 1)
        for at, column in enumerate((moe_high[:, :1], moe_low[:, :1], attn_high, attn_low)):
            rest = jnp.where(lane == ROUTE + 32 + at, column, rest)
        out_ref[:, :256] = main.astype(BF)
        out_ref[:, 256:] = rest.astype(BF)


def pack(pos, packed, x_rel, gain, weights, router, moe):
    seq = packed.shape[1]
    return call(
        pack_kernel,
        "pack",
        (seq // PAIR,),
        [
            spec((PACK, PAIR), lambda s, pos: (0, s)),
            spec((2, BLK, D), lambda s, pos: (far_pair(s, pos), 0, 0)),
            resident(gain.shape),
            resident(weights.shape),
            resident(router.shape),
            resident(moe.shape),
        ],
        resident((D, PACK)),
        shape((D, PACK), BF),
        cost(50),
        [pltpu.VMEM((PACK, D), F32)],
    )(pos, packed, x_rel, gain, weights, router, moe)


def last_kernel(
    pos_ref, keep_ref, got_ref, fx_ref, fy_ref, fd_ref, x_ref, gain_ref, dy1_ref, out_ref
):
    dh1 = (
        keep_ref[0].astype(F32)
        + got_ref[0].astype(F32)
        + fx_ref[...].astype(F32)
        + fy_ref[...].astype(F32)
        + fd_ref[...].astype(F32)
    )
    pulled, _ = norm_pull(x_ref[...].astype(F32), gain_ref[...], dh1)
    out_ref[...] = (dy1_ref[...] + pulled).astype(BF)


def last(pos, keep, got, sums, x, gain, dy1):
    rows = x.shape[0]
    full = lambda a: resident(a.shape)
    first = pl.BlockSpec((1, rows, D), lambda s, pos: (0, 0, 0), pipeline_mode=pl.Buffered(1))
    return call(
        last_kernel,
        "last",
        (1,),
        [first, first] + [full(a) for a in (*sums, x, gain, dy1)],
        resident((rows, D)),
        shape((rows, D), BF),
        cost(50),
    )(pos, keep, got, *sums, x, gain, dy1)


def out_grad_kernel(count, pos_ref, *refs):
    pieces = refs[: count + 2]
    db_ref, out_ref, heads = refs[count + 2 :]
    step = pl.program_id(0)
    pos = pos_ref[0]
    for r in range(count):
        base = (pos ^ r) * Q_COLS
        if r < count - 2:
            heads[pl.ds(pl.multiple_of(base, Q_COLS), Q_COLS), :] = pieces[r][...]
        else:
            half = Q_COLS // 2
            at = count - 2 + 2 * (r - count + 2)
            heads[pl.ds(pl.multiple_of(base, half), half), :] = pieces[at][...]
            heads[pl.ds(pl.multiple_of(base + half, half), half), :] = pieces[at + 1][...]
    term = dot(db_ref[0], heads[...], 1, 1)

    @pl.when(step == 0)
    def _():
        out_ref[...] = term

    @pl.when(step > 0)
    def _():
        out_ref[...] += term


def out_grad(pos, pieces, came):
    count = len(pieces) - 2
    seq, cols = came.shape[0] * BLK, Q_COLS
    return call(
        functools.partial(out_grad_kernel, count),
        "out_grad",
        (seq // BLK,),
        [spec((a.shape[0], BLK), lambda s, pos: (0, s)) for a in pieces]
        + [spec((1, cols, BLK), lambda s, pos: (s, 1, 0))],
        resident((cols, HEADS * HEAD_DIM)),
        shape((cols, HEADS * HEAD_DIM), F32),
        SHORT,
        [pltpu.VMEM((HEADS * HEAD_DIM, BLK), BF)],
    )(pos, *pieces, came).astype(BF)


def unpack_kernel(groups, members, pos_ref, came_ref, query_ref, pair_ref, rest_ref):
    total = None
    for j in range(members):
        here = came_ref[j].astype(F32)
        for i in range(1, groups):
            here = here + came_ref[i * members + j].astype(F32)
        query_ref[:, j * Q_COLS : (j + 1) * Q_COLS] = here[:, :Q_COLS]
        pair_ref[:, j * HEAD_DIM : (j + 1) * HEAD_DIM] = here[:, Q_COLS : Q_COLS + HEAD_DIM]
        at = (members + j) * HEAD_DIM
        pair_ref[:, at : at + HEAD_DIM] = here[:, Q_COLS + HEAD_DIM : QKV]
        rest = here[:, 256:]
        total = rest if total is None else total + rest
    rest_ref[...] = total


def unpack(pos, came, groups):
    devices, rows, _ = came.shape
    members = devices // groups
    return call(
        functools.partial(unpack_kernel, groups, members),
        "unpack",
        (1,),
        [resident(came.shape)],
        [resident((rows, D)), resident((rows, 2 * KV_HEADS * HEAD_DIM)), resident((rows, 128))],
        [
            shape((rows, D), F32),
            shape((rows, 2 * KV_HEADS * HEAD_DIM), F32),
            shape((rows, 128), F32),
        ],
        SHORT,
    )(pos, came)


def swap(values, bit):
    count = lax.axis_size("expert")
    return lax.ppermute(values, "expert", [(i, i ^ bit) for i in range(count)])


def gather_pieces(own, before_last):
    half = own.shape[0] // 2
    x, y = swap(own, 2), swap(own, 4)
    core = swap(own, 1)
    far_a, far_b = tie((swap(x[:half], 4), swap(y[half:], 2)), before_last)
    return [
        own, core, x, swap(x, 1), y, swap(y, 1),
        far_a, far_b, swap(far_a, 1), swap(far_b, 1),
    ]


def gather_direct(own):
    near = [own, swap(own, 2), swap(own, 4), swap(own, 6)]
    return [piece for value in near for piece in (value, swap(value, 1))]


def tie(values, *after):
    return lax.optimization_barrier((values, after))[0]


def pair_sums(keep, got):
    return [(keep[r].astype(F32) + got[r].astype(F32)).astype(BF) for r in (1, 2, 3)]


def send_sums(sums):
    return [swap(sums[0], 2), swap(sums[1], 4), swap(sums[2], 6)]


def send_to_groups(blocks):
    count = lax.axis_size("dp")
    me = lax.axis_index("dp")
    terms = [lax.dynamic_index_in_dim(blocks, me, 0, False)]
    for k in range(1, count):
        sent = lax.dynamic_index_in_dim(blocks, (me + k) % count, 0, False)
        terms.append(lax.ppermute(sent, "dp", [(i, (i + k) % count) for i in range(count)]))
    return terms


def exchange(blocks, axes):
    return lax.all_to_all(blocks, axes, split_axis=0, concat_axis=0, tiled=True)


def shards(
    tokens,
    segment_ids,
    expert_ids,
    w_query,
    w_key_value,
    w_out,
    w_router,
    norm_attn,
    norm_moe,
    w_gate_up,
    w_down,
    grad_out,
):
    tok_rows = tokens.shape[0]
    members = lax.axis_size("expert")
    groups = lax.axis_size("dp")
    position = lax.axis_index("expert")
    pos = position.astype(jnp.int32).reshape(1)
    devices = groups * members
    seq = tok_rows * members
    expert_total = EXP_DEV * members
    in_rows = w_query.shape[0]
    out_cols = w_out.shape[1]
    kv_cols = KV_HEADS * HEAD_DIM

    start = jnp.sum(
        (segment_ids[:, None] < segment_ids[None, :]).astype(jnp.int32), axis=0, keepdims=True
    )
    first = jnp.stack([start[0, ::BLK] // BLK, (start[0, BLK - 1 :: BLK] + BLK - 1) // BLK])
    x_pieces = gather_pieces(tokens, (start, first))

    own = send_weights(
        pos, (w_query, w_key_value, w_router, norm_attn[None], norm_moe[None]), groups, members
    )
    weights = exchange(own, BOTH).reshape(D, PACK)
    gain_attn = weights[:, QKV + expert_total].astype(F32)[None]
    gain_moe = weights[:, QKV + expert_total + 1].astype(F32)[None]

    token_pos = jnp.arange(seq, dtype=jnp.int32)
    frequency = ROPE_BASE ** (-(jnp.arange(HALF, dtype=F32) * 2.0 / HEAD_DIM))
    angles = frequency[:, None] * token_pos.astype(F32)[None, :]
    cosine, sine = jnp.cos(angles), jnp.sin(angles)

    q_t, k_t, v_t, k, v = qkv_forward(
        pos, x_pieces, weights, gain_attn, cosine, sine
    )
    w_full = lax.all_gather(tie(w_out.T, own), BOTH, axis=0, tiled=True)
    dy_all = lax.all_gather(tie(grad_out, own), "expert", axis=0, tiled=True)
    w_full = w_full.T
    a_t, o_t, lse = attn_forward(first, q_t, k, v_t, start)
    ids = jnp.concatenate(gather_direct(tie(expert_ids, q_t).T), axis=0)
    ids = ids.reshape(members, TOP, tok_rows)
    a_pieces = gather_pieces(a_t, (w_full, ids))
    x_rel = jnp.concatenate(tie(x_pieces, a_t), axis=0).reshape(members, tok_rows, D)

    h2, gates, y1, h2_own, gates_own = mix_forward(
        pos, a_pieces, x_rel, w_full, gain_moe, weights, ids
    )

    ag0, dgu0, *carried, down0 = expert_pass(0, pos, h2, dy_all, gates, w_gate_up, w_down)
    down0 = by_group(down0, groups)
    ag1, dgu1, give, keep, dg = expert_pass(
        1, pos, h2, dy_all, gates, w_gate_up, w_down, carried
    )
    got = swap(give, 1)
    down1 = down_grad(pos, ag1, dy_all, groups)
    sums = pair_sums(keep, tie(got, down1))
    came_sums = send_sums(sums)
    dg = exchange(tie(dg, sums), "expert")[:, :EXP_DEV].reshape(expert_total, tok_rows).T
    dg = jnp.pad(dg, ((0, 0), (ROUTE, 128 - ROUTE - expert_total)))
    up0 = up_grad(pos, *tie((h2, dgu0), sums))
    up1 = up_grad(pos, *tie((h2, dgu1), up0))
    out_give, out_keep = combine(pos, tie((ag0, ag1), up1), w_down)
    spread = functools.partial(lax.psum_scatter, axis_name="dp", scatter_dimension=0, tiled=True)
    down_share = [spread(d.reshape(groups * FF, -1)) for d in (down0, down1)]
    up_share = [spread(d) for d in (up0, up1)]
    keep, down_share[0] = lax.optimization_barrier((keep, down_share[0]))
    out_got = swap(out_give, 1)

    dy1, da, router_wgrad, moe_gain_grad = middle(
        groups, pos, tie(keep, out_keep), got, came_sums, y1, h2_own, gates_own, dg, grad_out,
        weights, gain_moe, w_full,
    )
    da = exchange(da, "expert")
    out_sums = pair_sums(out_keep, tie(out_got, dy1))
    out_came = send_sums(out_sums)

    dq_t, dk_t, dv_t = attn_backward(first, q_t, tie(da, out_sums), o_t, lse, k, k_t, v, start)
    give1, keep1, packed = back(pos, dq_t, dk_t, dv_t, cosine, sine, weights)
    got1 = swap(give1, 1)
    sent = pack(pos, packed, x_rel, gain_attn, weights, router_wgrad, moe_gain_grad)
    sums1 = pair_sums(keep1, tie(got1, sent))
    came_sums1 = send_sums(sums1)
    result = y1 + out_keep[0].astype(F32) + out_got[0].astype(F32)
    for term in tie(out_came, sums1):
        result = result + term.astype(F32)
    result = result.astype(BF)
    out_wgrad = out_grad(pos, a_pieces, tie(da, result)).reshape(groups, out_cols, D)
    out_terms = send_to_groups(out_wgrad)
    came = exchange(sent.reshape(devices, in_rows, PACK), BOTH)
    token_grad = last(pos, keep1, got1, came_sums1, tokens, gain_attn, dy1)
    query_share, pair_share, rest = unpack(pos, tie(came, token_grad), groups)
    router_share = (
        rest[:, ROUTE : ROUTE + expert_total]
        + rest[:, ROUTE + expert_total : ROUTE + 2 * expert_total]
    )
    moe_gain_share = rest[:, ROUTE + 32] + rest[:, ROUTE + 33]

    attn_gain_share = rest[:, ROUTE + 34] + rest[:, ROUTE + 35]
    out_share = sum(term.astype(F32) for term in tie(out_terms, token_grad)).T

    return (
        result,
        token_grad,
        query_share,
        pair_share,
        out_share,
        router_share,
        attn_gain_share,
        moe_gain_share,
        jnp.stack(tie(up_share, rest, out_share)).astype(F32),
        jnp.stack(down_share).astype(F32),
    )


def solution(mesh):
    in_specs = (
        P(("dp", "expert"), None),
        P("dp"),
        P(("dp", "expert"), None),
        P(("dp", "expert"), None),
        P(("dp", "expert"), None),
        P(None, ("dp", "expert")),
        P(("dp", "expert"), None),
        P(("dp", "expert")),
        P(("dp", "expert")),
        P("expert", None, None),
        P("expert", None, None),
        P(("dp", "expert"), None),
    )
    out_specs = (
        P(("dp", "expert"), None),
        P(("dp", "expert"), None),
        P(("dp", "expert"), None),
        P(("dp", "expert"), None),
        P(None, ("dp", "expert")),
        P(("dp", "expert"), None),
        P(("dp", "expert")),
        P(("dp", "expert")),
        P("expert", "dp", None),
        P("expert", None, "dp"),
    )
    return jax.shard_map(shards, mesh=mesh, in_specs=in_specs, out_specs=out_specs, check_vma=False)
```

```python
import functools

import jax
import jax.numpy as jnp
from jax import lax
from jax.experimental import pallas as pl
from jax.experimental.pallas import tpu as pltpu
from jax.sharding import PartitionSpec as P

D = 1536
HEADS = 24
KV_HEADS = 8
HEAD_DIM = 64
FF = 512
TOP = 8
EXP_DEV = 2

RESIDUAL = 0.22
ATTN_SCALE = 0.015625
LOG2E = 1.4426950408889634
EPSILON = 1e-06
ROPE_BASE = 10000.0
MASKED = -1e30

GROUP = HEADS // KV_HEADS
HALF = HEAD_DIM // 2
BLK = 256
BF = jnp.bfloat16
F32 = jnp.float32
BOTH = ("dp", "expert")


ROOM = {
    "attn_fwd": 8,
    "qkv": 24,
    "back": 12,
    "pack": 20,
    "last": 16,
    "out_grad": 16,
    "unpack": 12,
}


def room(name):
    return pltpu.CompilerParams(vmem_limit_bytes=ROOM[name] << 20 if name in ROOM else None)


def cost(micros):
    return pl.CostEstimate(flops=micros * 10**9, bytes_accessed=10**4, transcendentals=0)


LONG, SHORT = cost(50), cost(0)


def dot(a, b, ca, cb):
    return lax.dot_general(a, b, (((ca,), (cb,)), ((), ())), preferred_element_type=F32)


def rms_scale(values, gain_vec):
    return (
        values * lax.rsqrt(jnp.mean(values * values, axis=-1, keepdims=True) + EPSILON) * gain_vec
    )


def side_by_side(block):
    return jnp.concatenate(
        [block[h * HEAD_DIM : (h + 1) * HEAD_DIM] for h in range(GROUP)], axis=1
    )


def stacked(wide):
    width = wide.shape[1] // GROUP
    return jnp.concatenate([wide[:, h * width : (h + 1) * width] for h in range(GROUP)], axis=0)


def allowed_keys(start_ref, block, key_block):
    lane = lax.broadcasted_iota(jnp.int32, (1, BLK), 1) + block * BLK
    reach = lane - start_ref[...]
    lane3 = jnp.concatenate([lane] * GROUP, axis=1)
    reach3 = jnp.concatenate([reach] * GROUP, axis=1)
    key_pos = lax.broadcasted_iota(jnp.int32, (BLK, 1), 0) + key_block * BLK
    back = lane3 - key_pos
    return (back >= 0) & (back <= reach3)


def over_keys(first_ref, block, step, carry):
    clear = jnp.minimum(first_ref[1, block], block)
    carry = lax.fori_loop(first_ref[0, block], clear, functools.partial(step, True), carry)
    pairs = (block - clear) // 2
    carry = lax.fori_loop(
        0, pairs, lambda n, carry: step(False, clear + 2 * n, carry, 2), carry
    )
    carry = lax.fori_loop(clear + 2 * pairs, block, functools.partial(step, False), carry)
    return step(True, block, carry)


def attn_fwd_kernel(first_ref, q_ref, k_ref, vt_ref, start_ref, a_ref, o_ref, lse_ref):
    block = pl.program_id(0)
    query = side_by_side(q_ref[...])
    width = GROUP * BLK

    def step(masked, key_block, carry, count=1):
        largest, total, acc = carry
        rows = pl.ds(pl.multiple_of(key_block * BLK, BLK), count * BLK)
        keys, values = k_ref[rows, :], vt_ref[:, rows]
        scores = dot(keys, query, 1, 0) * (ATTN_SCALE * LOG2E)
        if masked:
            scores = jnp.where(allowed_keys(start_ref, block, key_block), scores, MASKED)
        now = jnp.maximum(largest, jnp.max(scores, axis=0, keepdims=True))
        power = jnp.exp2(scores - now)
        fade = jnp.exp2(largest - now)
        total = total * fade + jnp.sum(power, axis=0, keepdims=True)
        acc = acc * fade + dot(values, power.astype(BF), 1, 0)
        return now, total, acc

    largest, total, acc = over_keys(
        first_ref,
        block,
        step,
        (
            jnp.full((1, width), MASKED, F32),
            jnp.zeros((1, width), F32),
            jnp.zeros((HEAD_DIM, width), F32),
        ),
    )
    out = stacked(acc / total)
    o_ref[...] = out
    a_ref[...] = out.astype(BF)
    lse = largest + jnp.log2(total)
    lse_ref[...] = jnp.concatenate(
        [lse[:, h * BLK : (h + 1) * BLK] for h in range(GROUP)]
        + [jnp.zeros((8 - GROUP, BLK), F32)],
        axis=0,
    )


def attn_bwd_kernel(
    first_ref, q_ref, da_ref, o_ref, lse_ref, k_ref, kt_ref, v_ref, start_ref,
    dq_ref, dk_ref, dv_ref, dk_acc, dv_acc,
):
    block = pl.program_id(0)

    @pl.when(block == 0)
    def _():
        dk_acc[...] = jnp.zeros_like(dk_acc)
        dv_acc[...] = jnp.zeros_like(dv_acc)

    query_t = side_by_side(q_ref[...])
    query = query_t.astype(F32).T.astype(BF)
    grad_t = side_by_side(da_ref[0])
    grad_f = grad_t.astype(F32)
    grad = grad_f.T.astype(BF)
    delta = jnp.sum(side_by_side(o_ref[...]) * grad_f, axis=0, keepdims=True)
    lse = jnp.concatenate([lse_ref[h : h + 1, :] for h in range(GROUP)], axis=1)

    def step(masked, key_block, dq, count=1):
        rows = pl.ds(pl.multiple_of(key_block * BLK, BLK), count * BLK)
        keys = k_ref[rows, :]
        scores = dot(keys, query_t, 1, 0) * (ATTN_SCALE * LOG2E)
        if masked:
            scores = jnp.where(allowed_keys(start_ref, block, key_block), scores, MASKED)
        prob = jnp.exp2(scores - lse)
        grad_prob = dot(v_ref[rows, :], grad_t, 1, 0)
        grad_score = (prob * (grad_prob - delta) * ATTN_SCALE).astype(BF)
        dv_acc[rows, :] += dot(prob.astype(BF), grad, 1, 0)
        dk_acc[rows, :] += dot(grad_score, query, 1, 0)
        return dq + dot(kt_ref[:, rows], grad_score, 1, 0)

    dq = over_keys(first_ref, block, step, jnp.zeros((HEAD_DIM, GROUP * BLK), F32))
    dq_ref[...] = stacked(dq)

    @pl.when(block == pl.num_programs(0) - 1)
    def _():
        dk_ref[...] = dk_acc[...].T
        dv_ref[...] = dv_acc[...].T


def attn_forward(first, q_t, k, v_t, start):
    seq = q_t.shape[1]
    rows = GROUP * HEAD_DIM
    column = lambda g, first: (0, g)
    whole = lambda g, first: (0, 0)
    return pl.pallas_call(
        attn_fwd_kernel,
        grid_spec=pltpu.PrefetchScalarGridSpec(
            num_scalar_prefetch=1,
            grid=(seq // BLK,),
            in_specs=[
                pl.BlockSpec((rows, BLK), column),
                pl.BlockSpec((seq, HEAD_DIM), whole),
                pl.BlockSpec((HEAD_DIM, seq), whole),
                pl.BlockSpec((1, BLK), column),
            ],
            out_specs=[
                pl.BlockSpec((rows, BLK), column),
                pl.BlockSpec((rows, BLK), column),
                pl.BlockSpec((8, BLK), column),
            ],
        ),
        out_shape=[
            jax.ShapeDtypeStruct((rows, seq), BF),
            jax.ShapeDtypeStruct((rows, seq), F32),
            jax.ShapeDtypeStruct((8, seq), F32),
        ],
        cost_estimate=LONG,
        compiler_params=room("attn_fwd"),
        name="attn_fwd",
    )(first, q_t, k, v_t, start)


def attn_backward(first, q_t, da, o_t, lse, k, k_t, v, start):
    seq = q_t.shape[1]
    rows = GROUP * HEAD_DIM
    column = lambda g, first: (0, g)
    whole = lambda g, first: (0, 0)
    return pl.pallas_call(
        attn_bwd_kernel,
        grid_spec=pltpu.PrefetchScalarGridSpec(
            num_scalar_prefetch=1,
            grid=(seq // BLK,),
            in_specs=[
                pl.BlockSpec((rows, BLK), column),
                pl.BlockSpec((1, rows, BLK), lambda g, first: (g, 0, 0)),
                pl.BlockSpec((rows, BLK), column),
                pl.BlockSpec((8, BLK), column),
                pl.BlockSpec((seq, HEAD_DIM), whole),
                pl.BlockSpec((HEAD_DIM, seq), whole),
                pl.BlockSpec((seq, HEAD_DIM), whole),
                pl.BlockSpec((1, BLK), column),
            ],
            out_specs=[
                pl.BlockSpec((rows, BLK), column),
                pl.BlockSpec((HEAD_DIM, seq), whole),
                pl.BlockSpec((HEAD_DIM, seq), whole),
            ],
            scratch_shapes=[
                pltpu.VMEM((seq, HEAD_DIM), F32),
                pltpu.VMEM((seq, HEAD_DIM), F32),
            ],
        ),
        out_shape=[
            jax.ShapeDtypeStruct((rows, seq), F32),
            jax.ShapeDtypeStruct((HEAD_DIM, seq), F32),
            jax.ShapeDtypeStruct((HEAD_DIM, seq), F32),
        ],
        cost_estimate=cost(20),
        compiler_params=room("attn_bwd"),
        name="attn_bwd",
    )(first, q_t, da, o_t, lse, k, k_t, v, start)


PACK = 384
Q_COLS = GROUP * HEAD_DIM
QKV = Q_COLS + 2 * HEAD_DIM
ROUTE = QKV - 256


def spec(shape, index):
    return pl.BlockSpec(shape, index)


def resident(shape):
    return pl.BlockSpec(
        shape, lambda *_: (0,) * len(shape), pipeline_mode=pl.Buffered(1)
    )


def call(kernel, name, grid, in_specs, out_specs, out_shape, estimate, scratch=()):
    return pl.pallas_call(
        kernel,
        grid_spec=pltpu.PrefetchScalarGridSpec(
            num_scalar_prefetch=1,
            grid=grid,
            in_specs=in_specs,
            out_specs=out_specs,
            scratch_shapes=list(scratch),
        ),
        out_shape=out_shape,
        cost_estimate=estimate,
        compiler_params=room(name),
        name=name,
    )


def shape(dims, kind):
    return jax.ShapeDtypeStruct(dims, kind)


PAIR = 2 * BLK


def far_pair(step, pos):
    return step ^ (pos[0] // 2)


def halves(pos):
    core = pos[0] % 2
    return [pl.ds(pl.multiple_of(start * BLK, BLK), BLK) for start in (1 - core, core)]


def turn_rows(rows_t, cosine, sine):
    out = []
    for h in range(rows_t.shape[0] // HEAD_DIM):
        a = rows_t[h * HEAD_DIM : h * HEAD_DIM + HALF]
        b = rows_t[h * HEAD_DIM + HALF : (h + 1) * HEAD_DIM]
        out += [a * cosine - b * sine, b * cosine + a * sine]
    return jnp.concatenate(out, axis=0)


def norm_of(values):
    return values * lax.rsqrt(jnp.mean(values * values, axis=1, keepdims=True) + EPSILON)


def qkv_kernel(count, pos_ref, *refs):
    pieces = refs[: count + 2]
    w_ref, gain_ref, cos_ref, sin_ref, q_ref, kt_ref, vt_ref, k_ref, v_ref = refs[count + 2 :]
    gain = gain_ref[...]
    for r in range(count):
        if r < count - 2:
            rows = pieces[r][...]
        else:
            at = count - 2 + 2 * (r - count + 2)
            rows = jnp.concatenate([pieces[at][...], pieces[at + 1][...]], axis=0)
        normed = (norm_of(rows.astype(F32)) * gain).astype(BF)
        both = dot(normed, w_ref[...], 1, 0)
        turned = both.T
        place = pl.multiple_of((pos_ref[0] ^ r) * BLK, BLK)
        columns = pl.ds(place, BLK)
        cosine, sine = cos_ref[:, columns], sin_ref[:, columns]
        qk = turn_rows(turned[: Q_COLS + HEAD_DIM], cosine, sine)
        q_ref[:, columns] = qk[:Q_COLS].astype(BF)
        kt_ref[:, columns] = qk[Q_COLS:].astype(BF)
        vt_ref[:, columns] = turned[Q_COLS + HEAD_DIM : QKV].astype(BF)
        k_ref[columns, :] = qk[Q_COLS:].T.astype(BF)
        v_ref[columns, :] = both[:, 256 : 256 + HEAD_DIM].astype(BF)


def qkv_forward(pos, pieces, weights, gain, cosine, sine):
    count = len(pieces) - 2
    seq = cosine.shape[1]
    full = lambda a: resident(a.shape)
    return call(
        functools.partial(qkv_kernel, count),
        "qkv",
        (1,),
        [full(a) for a in pieces] + [full(a) for a in (weights, gain, cosine, sine)],
        [resident(s) for s in ((Q_COLS, seq), (HEAD_DIM, seq), (HEAD_DIM, seq), (seq, HEAD_DIM), (seq, HEAD_DIM))],
        [
            shape((Q_COLS, seq), BF),
            shape((HEAD_DIM, seq), BF),
            shape((HEAD_DIM, seq), BF),
            shape((seq, HEAD_DIM), BF),
            shape((seq, HEAD_DIM), BF),
        ],
        cost(400),
    )(pos, *pieces, weights, gain, cosine, sine)


def as_column(row):
    count = row.shape[1]
    here = lax.broadcasted_iota(jnp.int32, (count, count), 0)
    there = lax.broadcasted_iota(jnp.int32, (count, count), 1)
    return jnp.sum(jnp.where(here == there, row.astype(F32), 0.0), axis=1, keepdims=True)


def send_weights_kernel(
    groups, members, pos_ref, q_ref, kv_ref, route_ref, attn_ref, moe_ref, out_ref
):
    query, pair = q_ref[...], kv_ref[...]
    rows, experts = route_ref.shape
    route = jnp.concatenate(
        [route_ref[...].astype(F32), jnp.zeros((rows, PACK - QKV - experts), F32)], axis=1
    )
    lane = lax.broadcasted_iota(jnp.int32, route.shape, 1)
    rest = jnp.where(lane == experts, as_column(attn_ref[...]), route)
    rest = jnp.where(lane == experts + 1, as_column(moe_ref[...]), rest).astype(BF)
    for j in range(members):
        block = jnp.concatenate(
            [query[:, j * Q_COLS : (j + 1) * Q_COLS]]
            + [pair[:, n * HEAD_DIM : (n + 1) * HEAD_DIM] for n in (j, members + j)]
            + [rest],
            axis=1,
        )
        for i in range(groups):
            out_ref[i * members + j] = block


def send_weights(pos, parts, groups, members):
    rows = parts[0].shape[0]
    full = lambda a: resident(a.shape)
    return call(
        functools.partial(send_weights_kernel, groups, members),
        "send_weights",
        (1,),
        [full(a) for a in parts],
        resident((groups * members, rows, PACK)),
        shape((groups * members, rows, PACK), BF),
        SHORT,
    )(pos, *parts)


def mix_kernel(count, pos_ref, *refs):
    pieces = refs[: count + 2]
    x_ref, w_ref, gain_ref, route_ref, ids_ref = refs[count + 2 : count + 7]
    h2_ref, gates_ref, y1_ref, h2_own_ref, gates_own_ref, heads, y1_all = refs[count + 7 :]
    block = pl.program_id(0)
    pos = pos_ref[0]
    for r in range(count):
        base = (pos ^ r) * Q_COLS
        if r < count - 2:
            heads[pl.ds(pl.multiple_of(base, Q_COLS), Q_COLS), :] = pieces[r][...]
        else:
            half = Q_COLS // 2
            at = count - 2 + 2 * (r - count + 2)
            heads[pl.ds(pl.multiple_of(base, half), half), :] = pieces[at][...]
            heads[pl.ds(pl.multiple_of(base + half, half), half), :] = pieces[at + 1][...]
    route, gain = route_ref[...], gain_ref[...]
    for h in range(2):
        rows = slice(h * BLK, (h + 1) * BLK)
        mixed = dot(heads[:, rows], w_ref[...], 0, 0)
        y1 = x_ref[h ^ (pos % 2)].astype(F32) + RESIDUAL * mixed
        h2 = (norm_of(y1) * gain).astype(BF)
        logits = dot(h2, route, 1, 0)
        lane = lax.broadcasted_iota(jnp.int32, logits.shape, 1) - ROUTE
        ids = ids_ref[h ^ (pos % 2)].T
        chosen = lane == ids[:, 0:1]
        for k in range(1, TOP):
            chosen = chosen | (lane == ids[:, k : k + 1])
        masked = jnp.where(chosen, logits, MASKED)
        power = jnp.where(chosen, jnp.exp(masked - jnp.max(masked, axis=1, keepdims=True)), 0.0)
        gates = power / jnp.sum(power, axis=1, keepdims=True)
        h2_ref[rows] = h2
        gates_ref[rows] = gates
        y1_all[rows] = y1

    @pl.when(block == pos // 2)
    def _():
        mine = halves(pos_ref)[1]
        y1_ref[...] = y1_all[mine]
        h2_own_ref[...] = h2_ref[mine]
        gates_own_ref[...] = gates_ref[mine]


def mix_forward(pos, pieces, x_rel, w_full, gain, weights, ids):
    count = len(pieces) - 2
    seq = ids.shape[0] * BLK
    row = lambda s, pos: (s, 0)
    return call(
        functools.partial(mix_kernel, count),
        "mix",
        (seq // PAIR,),
        [spec((a.shape[0], PAIR), lambda s, pos: (0, s)) for a in pieces]
        + [
            spec((2, BLK, D), lambda s, pos: (far_pair(s, pos), 0, 0)),
            resident(w_full.shape),
            resident(gain.shape),
            pl.BlockSpec((D, 128), lambda s, pos: (0, 2), pipeline_mode=pl.Buffered(1)),
            spec((2, TOP, BLK), lambda s, pos: (far_pair(s, pos), 0, 0)),
        ],
        [
            spec((PAIR, D), row),
            spec((PAIR, 128), row),
            resident((BLK, D)),
            resident((BLK, D)),
            resident((BLK, 128)),
        ],
        [
            shape((seq, D), BF),
            shape((seq, 128), F32),
            shape((BLK, D), F32),
            shape((BLK, D), BF),
            shape((BLK, 128), F32),
        ],
        LONG,
        [pltpu.VMEM((HEADS * HEAD_DIM, PAIR), BF), pltpu.VMEM((PAIR, D), F32)],
    )(pos, *pieces, x_rel, w_full, gain, weights, ids)


def expert_kernel(e, pos_ref, h2_ref, dy_ref, gates_ref, up_ref, down_ref, *refs):
    if e == 0:
        ag_ref, dgu_ref, sum_ref, dg_ref, grad_ref, grad_acc = refs

        @pl.when(pl.program_id(0) == 0)
        def _():
            grad_acc[...] = jnp.zeros_like(grad_acc)

    else:
        sum_ref, dg_in_ref, ag_ref, dgu_ref, give_ref, keep_ref, dg_ref = refs
    for h, rows in enumerate(halves(pos_ref)):
        h2, dy, gates = h2_ref[rows], dy_ref[rows], gates_ref[rows]
        which = lax.broadcasted_iota(jnp.int32, gates.shape, 1)
        here = which == ROUTE + EXP_DEV * pos_ref[0] + e
        gate = RESIDUAL * jnp.sum(jnp.where(here, gates, 0.0), axis=1, keepdims=True)
        gu = dot(h2, up_ref[0], 1, 0)
        back = dot(dy, down_ref[0], 1, 1)
        g, u = gu[:, :FF], gu[:, FF:]
        sig = 1.0 / (1.0 + jnp.exp(-g))
        swish = g * sig
        act = swish * u
        gate_grad = RESIDUAL * jnp.sum(act * back, axis=1, keepdims=True)
        gate_grad = jnp.where(which == e, gate_grad, 0.0).T[:8]
        ag_ref[rows] = (gate * act).astype(BF)
        dact = gate * back
        dgu = jnp.concatenate(
            [dact * u * (sig * (1.0 + g * (1.0 - sig))), dact * swish], axis=1
        ).astype(BF)
        dgu_ref[rows] = dgu
        total = dot(dgu, up_ref[0], 1, 1)
        place = pos_ref[0] % 2 if h else 1 - pos_ref[0] % 2
        if e == 0:
            sum_ref[rows] = total
            dg_ref[place] = gate_grad
        else:
            (keep_ref if h else give_ref)[0] = (sum_ref[rows] + total).astype(BF)
            dg_ref[place] = dg_in_ref[place] + gate_grad
    if e == 0:
        grad_acc[...] += dot(ag_ref[...], dy_ref[...], 0, 0)

        @pl.when(pl.program_id(0) == pl.num_programs(0) - 1)
        def _():
            put_shares(grad_ref, grad_acc)


def expert_pass(e, pos, h2, dy_all, gates, w_gate_up, w_down, carried=()):
    seq = h2.shape[0]
    row = lambda s, pos: (s, 0)
    blocks = lambda s, pos: (s, 0, 0)
    pair = lambda s, pos: (far_pair(s, pos), 0, 0)
    half = seq // PAIR
    one = lambda a: pl.BlockSpec(
        (1,) + a.shape[1:], lambda s, pos: (e, 0, 0), pipeline_mode=pl.Buffered(1)
    )
    sums = (spec((PAIR, D), row), shape((seq, D), F32))
    gate_grads = (spec((2, 8, BLK), blocks), shape((2 * half, 8, BLK), F32))
    outs = [
        (spec((PAIR, FF), row), shape((seq, FF), BF)),
        (spec((PAIR, 2 * FF), row), shape((seq, 2 * FF), BF)),
    ]
    if e == 0:
        shares = (D // SHARE, FF, SHARE)
        outs += [sums, gate_grads, (resident(shares), shape(shares, BF))]
    else:
        outs += 2 * [(spec((1, BLK, D), pair), shape((half, BLK, D), BF))] + [gate_grads]
    return call(
        functools.partial(expert_kernel, e),
        "expert_%d" % e,
        (half,),
        [spec((PAIR, D), row), spec((PAIR, D), row), spec((PAIR, 128), row)]
        + [one(w_gate_up), one(w_down)]
        + ([sums[0], gate_grads[0]] if carried else []),
        [o[0] for o in outs],
        [o[1] for o in outs],
        cost(5),
        [] if e else [pltpu.VMEM((FF, D), F32)],
    )(pos, h2, dy_all, gates, w_gate_up, w_down, *carried)


SHARE = 384


def put_shares(out_ref, total):
    for n in range(out_ref.shape[0]):
        out_ref[n] = total[:, n * SHARE : (n + 1) * SHARE].astype(BF)


def by_group(shares, groups):
    cols = D // groups
    if cols == SHARE:
        return shares
    whole = jnp.moveaxis(shares, 0, 1).reshape(FF, groups, cols)
    return jnp.moveaxis(whole, 1, 0)


def down_grad_kernel(pos_ref, ag_ref, dy_ref, out_ref):
    put_shares(out_ref, dot(ag_ref[...], dy_ref[...], 0, 0))


def down_grad(pos, ag, dy_all, groups):
    seq = dy_all.shape[0]
    out = call(
        down_grad_kernel,
        "down_grad",
        (D // (2 * SHARE),),
        [resident(ag.shape), spec((seq, 2 * SHARE), lambda s, pos: (0, s))],
        spec((2, FF, SHARE), lambda s, pos: (s, 0, 0)),
        shape((D // SHARE, FF, SHARE), BF),
        SHORT,
    )(pos, ag, dy_all)
    return by_group(out, groups)


def up_grad_kernel(pos_ref, h2_ref, dgu_ref, out_ref):
    out_ref[...] = dot(h2_ref[...], dgu_ref[...], 0, 0).astype(BF)


def up_grad(pos, h2, dgu):
    seq = h2.shape[0]
    rows = 384
    return call(
        up_grad_kernel,
        "up_grad",
        (D // rows,),
        [spec((seq, rows), lambda s, pos: (0, s)), resident(dgu.shape)],
        spec((rows, 2 * FF), lambda s, pos: (s, 0)),
        shape((D, 2 * FF), BF),
        SHORT,
    )(pos, h2, dgu)


def combine_kernel(pos_ref, *refs):
    ags = refs[:EXP_DEV]
    down_ref, give_ref, keep_ref = refs[EXP_DEV:]
    for h, rows in enumerate(halves(pos_ref)):
        total = dot(ags[0][rows], down_ref[0], 1, 0)
        for e in range(1, EXP_DEV):
            total = total + dot(ags[e][rows], down_ref[e], 1, 0)
        (keep_ref if h else give_ref)[0] = total.astype(BF)


def combine(pos, ags, w_down):
    seq = ags[0].shape[0]
    half = seq // PAIR
    pair = lambda s, pos: (far_pair(s, pos), 0, 0)
    return call(
        combine_kernel,
        "combine",
        (half,),
        [spec((PAIR, FF), lambda s, pos: (s, 0)) for _ in ags] + [resident(w_down.shape)],
        [spec((1, BLK, D), pair), spec((1, BLK, D), pair)],
        [shape((half, BLK, D), BF), shape((half, BLK, D), BF)],
        SHORT,
    )(pos, *ags, w_down)


def norm_pull(values, gain, grad):
    scale = lax.rsqrt(jnp.mean(values * values, axis=1, keepdims=True) + EPSILON)
    unit = values * scale
    inner = grad * gain
    pulled = scale * (inner - unit * jnp.mean(inner * unit, axis=1, keepdims=True))
    return pulled, jnp.sum(grad * unit, axis=0, keepdims=True)


def middle_kernel(
    members, groups, wide, pos_ref, keep_ref, got_ref, fx_ref, fy_ref, fd_ref, y1_ref, h2_ref, gates_ref, dg_ref, dy_ref,
    route_ref, gain_ref, w_ref, dy1_ref, db_ref, da_ref, router_ref, gain_grad_ref,
):
    dh2 = (
        keep_ref[0].astype(F32)
        + got_ref[0].astype(F32)
        + fx_ref[...].astype(F32)
        + fy_ref[...].astype(F32)
        + fd_ref[...].astype(F32)
    )
    gates, gate_grads = gates_ref[...], dg_ref[...]
    mean = jnp.sum(gates * gate_grads, axis=1, keepdims=True)
    dlogits = (gates * (gate_grads - mean)).astype(BF)
    dh2 = dh2 + dot(dlogits, route_ref[...], 1, 1)
    router_ref[...] = dot(h2_ref[...], dlogits, 0, 0)
    pulled, gain_grad = norm_pull(y1_ref[...], gain_ref[...], dh2)
    gain_grad_ref[...] = jnp.broadcast_to(gain_grad, gain_grad_ref.shape)
    dy1 = dy_ref[...].astype(F32) + pulled
    dy1_ref[...] = dy1
    db = (RESIDUAL * dy1).astype(BF)
    db_ref[...] = db
    da = dot(w_ref[...], db, 1, 1).astype(BF)
    for j in range(members):
        da_ref[j, :Q_COLS] = da[j * Q_COLS : (j + 1) * Q_COLS]
    if wide:
        cols = Q_COLS // groups
        db_t = (RESIDUAL * dy1).T.astype(BF)
        for j in range(members):
            for i in range(groups):
                at, to = (i * members + j) * cols, Q_COLS + i * cols
                da_ref[j, to : to + cols] = db_t[at : at + cols]


def middle(groups, pos, keep, got, sums, y1, h2, gates, dg, dy, weights, gain, w_full):
    rows = y1.shape[0]
    full = lambda a: resident(a.shape)
    first = pl.BlockSpec((1, rows, D), lambda s, pos: (0, 0, 0), pipeline_mode=pl.Buffered(1))
    members = HEADS * HEAD_DIM // Q_COLS
    wide = Q_COLS // groups % 16 == 0
    both = 2 * Q_COLS if wide else Q_COLS
    dy1, db, sent, router, gain_grad = call(
        functools.partial(middle_kernel, members, groups, wide),
        "middle",
        (1,),
        [first, first]
        + [full(a) for a in (*sums, y1, h2, gates, dg, dy)]
        + [
            pl.BlockSpec((D, 128), lambda s, pos: (0, 2), pipeline_mode=pl.Buffered(1)),
            full(gain),
            full(w_full),
        ],
        [
            resident((rows, D)),
            resident((rows, D)),
            resident((members, both, rows)),
            resident((D, 128)),
            resident((8, D)),
        ],
        [
            shape((rows, D), F32),
            shape((rows, D), BF),
            shape((members, both, rows), BF),
            shape((D, 128), F32),
            shape((8, D), F32),
        ],
        cost(100),
    )(pos, keep, got, *sums, y1, h2, gates, dg, dy, weights, gain, w_full)
    if not wide:
        cols = Q_COLS // groups
        db_t = jnp.moveaxis(db.T.reshape(groups, members, cols, rows), 1, 0)
        sent = jnp.concatenate([sent, db_t.reshape(members, Q_COLS, rows)], axis=1)
    return dy1, sent, router, gain_grad


def back_kernel(
    pos_ref, dq_ref, dk_ref, dv_ref, cos_ref, sin_ref, w_ref, give_ref, keep_ref, packed_ref
):
    cosine, sine = cos_ref[...], -sin_ref[...]
    rows_t = jnp.concatenate(
        [
            turn_rows(dq_ref[...], cosine, sine),
            turn_rows(dk_ref[...], cosine, sine),
            dv_ref[...],
            jnp.zeros((PACK - QKV, PAIR), F32),
        ],
        axis=0,
    ).astype(BF)
    packed_ref[...] = rows_t
    for h, rows in enumerate(halves(pos_ref)):
        total = dot(packed_ref[:, rows], w_ref[...], 0, 1).astype(BF)
        (keep_ref if h else give_ref)[0] = total


def back(pos, dq_t, dk_t, dv_t, cosine, sine, weights):
    seq = dq_t.shape[1]
    half = seq // PAIR
    column = lambda s, pos: (0, s)
    pair = lambda s, pos: (far_pair(s, pos), 0, 0)
    return call(
        back_kernel,
        "back",
        (half,),
        [
            spec((Q_COLS, PAIR), column),
            spec((HEAD_DIM, PAIR), column),
            spec((HEAD_DIM, PAIR), column),
            spec((HALF, PAIR), column),
            spec((HALF, PAIR), column),
            resident(weights.shape),
        ],
        [spec((1, BLK, D), pair), spec((1, BLK, D), pair), spec((PACK, PAIR), column)],
        [
            shape((half, BLK, D), BF),
            shape((half, BLK, D), BF),
            shape((PACK, seq), BF),
        ],
        SHORT,
    )(pos, dq_t, dk_t, dv_t, cosine, sine, weights)


def low_pair(values):
    high = values.astype(BF).astype(F32)
    return high, values - high


def pack_kernel(pos_ref, packed_ref, x_ref, gain_ref, w_ref, router_ref, moe_ref, out_ref, acc):
    step = pl.program_id(0)

    @pl.when(step == 0)
    def _():
        acc[...] = jnp.zeros_like(acc)

    term = None
    for h in range(2):
        here = x_ref[h ^ (pos_ref[0] % 2)].astype(F32)
        normed = (norm_of(here) * gain_ref[...]).astype(BF)
        part = dot(packed_ref[:, h * BLK : (h + 1) * BLK], normed, 1, 0)
        term = part if term is None else term + part
    acc[...] += term

    @pl.when(step == pl.num_programs(0) - 1)
    def _():
        main, rest = acc[:256].T, acc[256:].T
        w_main, w_rest = w_ref[:, :256].astype(F32), w_ref[:, 256:].astype(F32)
        lane = lax.broadcasted_iota(jnp.int32, (D, 128), 1)
        gain_attn = (
            jnp.sum(main * w_main, axis=1, keepdims=True)
            + jnp.sum(rest * w_rest, axis=1, keepdims=True)
        ) / w_rest[:, ROUTE + 16 : ROUTE + 17]
        high, low = low_pair(router_ref[...])
        moe_high, moe_low = low_pair(moe_ref[...].T)
        attn_high, attn_low = low_pair(gain_attn)
        rest = rest + high + pltpu.roll(low, 16, 1)
        for at, column in enumerate((moe_high[:, :1], moe_low[:, :1], attn_high, attn_low)):
            rest = jnp.where(lane == ROUTE + 32 + at, column, rest)
        out_ref[:, :256] = main.astype(BF)
        out_ref[:, 256:] = rest.astype(BF)


def pack(pos, packed, x_rel, gain, weights, router, moe):
    seq = packed.shape[1]
    return call(
        pack_kernel,
        "pack",
        (seq // PAIR,),
        [
            spec((PACK, PAIR), lambda s, pos: (0, s)),
            spec((2, BLK, D), lambda s, pos: (far_pair(s, pos), 0, 0)),
            resident(gain.shape),
            resident(weights.shape),
            resident(router.shape),
            resident(moe.shape),
        ],
        resident((D, PACK)),
        shape((D, PACK), BF),
        cost(50),
        [pltpu.VMEM((PACK, D), F32)],
    )(pos, packed, x_rel, gain, weights, router, moe)


def last_kernel(
    pos_ref, keep_ref, got_ref, fx_ref, fy_ref, fd_ref, x_ref, gain_ref, dy1_ref, out_ref
):
    dh1 = (
        keep_ref[0].astype(F32)
        + got_ref[0].astype(F32)
        + fx_ref[...].astype(F32)
        + fy_ref[...].astype(F32)
        + fd_ref[...].astype(F32)
    )
    pulled, _ = norm_pull(x_ref[...].astype(F32), gain_ref[...], dh1)
    out_ref[...] = (dy1_ref[...] + pulled).astype(BF)


def last(pos, keep, got, sums, x, gain, dy1):
    rows = x.shape[0]
    full = lambda a: resident(a.shape)
    first = pl.BlockSpec((1, rows, D), lambda s, pos: (0, 0, 0), pipeline_mode=pl.Buffered(1))
    return call(
        last_kernel,
        "last",
        (1,),
        [first, first] + [full(a) for a in (*sums, x, gain, dy1)],
        resident((rows, D)),
        shape((rows, D), BF),
        cost(50),
    )(pos, keep, got, *sums, x, gain, dy1)


def out_grad_kernel(count, pos_ref, *refs):
    pieces = refs[: count + 2]
    db_ref, out_ref, heads = refs[count + 2 :]
    step = pl.program_id(0)
    pos = pos_ref[0]
    for r in range(count):
        base = (pos ^ r) * Q_COLS
        if r < count - 2:
            heads[pl.ds(pl.multiple_of(base, Q_COLS), Q_COLS), :] = pieces[r][...]
        else:
            half = Q_COLS // 2
            at = count - 2 + 2 * (r - count + 2)
            heads[pl.ds(pl.multiple_of(base, half), half), :] = pieces[at][...]
            heads[pl.ds(pl.multiple_of(base + half, half), half), :] = pieces[at + 1][...]
    term = dot(db_ref[0], heads[...], 1, 1)

    @pl.when(step == 0)
    def _():
        out_ref[...] = term

    @pl.when(step > 0)
    def _():
        out_ref[...] += term


def out_grad(pos, pieces, came):
    count = len(pieces) - 2
    seq, cols = came.shape[0] * BLK, Q_COLS
    return call(
        functools.partial(out_grad_kernel, count),
        "out_grad",
        (seq // BLK,),
        [spec((a.shape[0], BLK), lambda s, pos: (0, s)) for a in pieces]
        + [spec((1, cols, BLK), lambda s, pos: (s, 1, 0))],
        resident((cols, HEADS * HEAD_DIM)),
        shape((cols, HEADS * HEAD_DIM), F32),
        SHORT,
        [pltpu.VMEM((HEADS * HEAD_DIM, BLK), BF)],
    )(pos, *pieces, came).astype(BF)


def unpack_kernel(groups, members, pos_ref, came_ref, query_ref, pair_ref, rest_ref):
    total = None
    for j in range(members):
        here = came_ref[j].astype(F32)
        for i in range(1, groups):
            here = here + came_ref[i * members + j].astype(F32)
        query_ref[:, j * Q_COLS : (j + 1) * Q_COLS] = here[:, :Q_COLS]
        pair_ref[:, j * HEAD_DIM : (j + 1) * HEAD_DIM] = here[:, Q_COLS : Q_COLS + HEAD_DIM]
        at = (members + j) * HEAD_DIM
        pair_ref[:, at : at + HEAD_DIM] = here[:, Q_COLS + HEAD_DIM : QKV]
        rest = here[:, 256:]
        total = rest if total is None else total + rest
    rest_ref[...] = total


def unpack(pos, came, groups):
    devices, rows, _ = came.shape
    members = devices // groups
    return call(
        functools.partial(unpack_kernel, groups, members),
        "unpack",
        (1,),
        [resident(came.shape)],
        [resident((rows, D)), resident((rows, 2 * KV_HEADS * HEAD_DIM)), resident((rows, 128))],
        [
            shape((rows, D), F32),
            shape((rows, 2 * KV_HEADS * HEAD_DIM), F32),
            shape((rows, 128), F32),
        ],
        SHORT,
    )(pos, came)


def swap(values, bit):
    count = lax.axis_size("expert")
    return lax.ppermute(values, "expert", [(i, i ^ bit) for i in range(count)])


def gather_pieces(own, before_last):
    half = own.shape[0] // 2
    x, y = swap(own, 2), swap(own, 4)
    core = swap(own, 1)
    far_a, far_b = tie((swap(x[:half], 4), swap(y[half:], 2)), before_last)
    return [
        own, core, x, swap(x, 1), y, swap(y, 1),
        far_a, far_b, swap(far_a, 1), swap(far_b, 1),
    ]


def gather_direct(own):
    near = [own, swap(own, 2), swap(own, 4), swap(own, 6)]
    return [piece for value in near for piece in (value, swap(value, 1))]


def tie(values, *after):
    return lax.optimization_barrier((values, after))[0]


def pair_sums(keep, got):
    return [(keep[r].astype(F32) + got[r].astype(F32)).astype(BF) for r in (1, 2, 3)]


def send_sums(sums):
    return [swap(sums[0], 2), swap(sums[1], 4), swap(sums[2], 6)]


def send_to_groups(blocks):
    count = lax.axis_size("dp")
    me = lax.axis_index("dp")
    terms = [lax.dynamic_index_in_dim(blocks, me, 0, False)]
    for k in range(1, count):
        sent = lax.dynamic_index_in_dim(blocks, (me + k) % count, 0, False)
        terms.append(lax.ppermute(sent, "dp", [(i, (i + k) % count) for i in range(count)]))
    return terms


def exchange(blocks, axes):
    return lax.all_to_all(blocks, axes, split_axis=0, concat_axis=0, tiled=True)


def shards(
    tokens,
    segment_ids,
    expert_ids,
    w_query,
    w_key_value,
    w_out,
    w_router,
    norm_attn,
    norm_moe,
    w_gate_up,
    w_down,
    grad_out,
):
    tok_rows = tokens.shape[0]
    members = lax.axis_size("expert")
    groups = lax.axis_size("dp")
    position = lax.axis_index("expert")
    pos = position.astype(jnp.int32).reshape(1)
    devices = groups * members
    seq = tok_rows * members
    expert_total = EXP_DEV * members
    in_rows = w_query.shape[0]
    out_cols = w_out.shape[1]
    kv_cols = KV_HEADS * HEAD_DIM

    start = jnp.sum(
        (segment_ids[:, None] < segment_ids[None, :]).astype(jnp.int32), axis=0, keepdims=True
    )
    first = jnp.stack([start[0, ::BLK] // BLK, (start[0, BLK - 1 :: BLK] + BLK - 1) // BLK])
    x_pieces = gather_pieces(tokens, (start, first))

    own = send_weights(
        pos, (w_query, w_key_value, w_router, norm_attn[None], norm_moe[None]), groups, members
    )
    weights = exchange(own, BOTH).reshape(D, PACK)
    gain_attn = weights[:, QKV + expert_total].astype(F32)[None]
    gain_moe = weights[:, QKV + expert_total + 1].astype(F32)[None]

    token_pos = jnp.arange(seq, dtype=jnp.int32)
    frequency = ROPE_BASE ** (-(jnp.arange(HALF, dtype=F32) * 2.0 / HEAD_DIM))
    angles = frequency[:, None] * token_pos.astype(F32)[None, :]
    cosine, sine = jnp.cos(angles), jnp.sin(angles)

    q_t, k_t, v_t, k, v = qkv_forward(
        pos, x_pieces, weights, gain_attn, cosine, sine
    )
    w_full = lax.all_gather(tie(w_out.T, own), BOTH, axis=0, tiled=True)
    dy_all = lax.all_gather(tie(grad_out, own), "expert", axis=0, tiled=True)
    w_full = w_full.T
    a_t, o_t, lse = attn_forward(first, q_t, k, v_t, start)
    ids = jnp.concatenate(gather_direct(tie(expert_ids, q_t).T), axis=0)
    ids = ids.reshape(members, TOP, tok_rows)
    a_pieces = gather_pieces(a_t, (w_full, ids))
    x_rel = jnp.concatenate(tie(x_pieces, a_t), axis=0).reshape(members, tok_rows, D)

    h2, gates, y1, h2_own, gates_own = mix_forward(
        pos, a_pieces, x_rel, w_full, gain_moe, weights, ids
    )

    ag0, dgu0, *carried, down0 = expert_pass(0, pos, h2, dy_all, gates, w_gate_up, w_down)
    down0 = by_group(down0, groups)
    ag1, dgu1, give, keep, dg = expert_pass(
        1, pos, h2, dy_all, gates, w_gate_up, w_down, carried
    )
    got = swap(give, 1)
    down1 = down_grad(pos, ag1, dy_all, groups)
    sums = pair_sums(keep, tie(got, down1))
    came_sums = send_sums(sums)
    dg = exchange(tie(dg, sums), "expert")[:, :EXP_DEV].reshape(expert_total, tok_rows).T
    dg = jnp.pad(dg, ((0, 0), (ROUTE, 128 - ROUTE - expert_total)))
    up0 = up_grad(pos, *tie((h2, dgu0), sums))
    up1 = up_grad(pos, *tie((h2, dgu1), up0))
    out_give, out_keep = combine(pos, tie((ag0, ag1), up1), w_down)
    spread = functools.partial(lax.psum_scatter, axis_name="dp", scatter_dimension=0, tiled=True)
    down_share = [spread(d.reshape(groups * FF, -1)) for d in (down0, down1)]
    up_share = [spread(d) for d in (up0, up1)]
    keep, down_share[0] = lax.optimization_barrier((keep, down_share[0]))
    out_got = swap(out_give, 1)

    dy1, da, router_wgrad, moe_gain_grad = middle(
        groups, pos, tie(keep, out_keep), got, came_sums, y1, h2_own, gates_own, dg, grad_out,
        weights, gain_moe, w_full,
    )
    da = exchange(da, "expert")
    out_sums = pair_sums(out_keep, tie(out_got, dy1))
    out_came = send_sums(out_sums)

    dq_t, dk_t, dv_t = attn_backward(first, q_t, tie(da, out_sums), o_t, lse, k, k_t, v, start)
    give1, keep1, packed = back(pos, dq_t, dk_t, dv_t, cosine, sine, weights)
    got1 = swap(give1, 1)
    sent = pack(pos, packed, x_rel, gain_attn, weights, router_wgrad, moe_gain_grad)
    sums1 = pair_sums(keep1, tie(got1, sent))
    came_sums1 = send_sums(sums1)
    result = y1 + out_keep[0].astype(F32) + out_got[0].astype(F32)
    for term in tie(out_came, sums1):
        result = result + term.astype(F32)
    result = result.astype(BF)
    out_wgrad = out_grad(pos, a_pieces, tie(da, result)).reshape(groups, out_cols, D)
    out_terms = send_to_groups(out_wgrad)
    came = exchange(sent.reshape(devices, in_rows, PACK), BOTH)
    token_grad = last(pos, keep1, got1, came_sums1, tokens, gain_attn, dy1)
    up_share = jnp.stack(tie(up_share, token_grad)).astype(F32)
    query_share, pair_share, rest = unpack(pos, tie(came, up_share), groups)
    router_share = (
        rest[:, ROUTE : ROUTE + expert_total]
        + rest[:, ROUTE + expert_total : ROUTE + 2 * expert_total]
    )
    moe_gain_share = rest[:, ROUTE + 32] + rest[:, ROUTE + 33]

    attn_gain_share = rest[:, ROUTE + 34] + rest[:, ROUTE + 35]
    out_share = sum(term.astype(F32) for term in tie(out_terms, up_share)).T

    return (
        result,
        token_grad,
        query_share,
        pair_share,
        out_share,
        router_share,
        attn_gain_share,
        moe_gain_share,
        up_share,
        jnp.stack(down_share).astype(F32),
    )


def solution(mesh):
    in_specs = (
        P(("dp", "expert"), None),
        P("dp"),
        P(("dp", "expert"), None),
        P(("dp", "expert"), None),
        P(("dp", "expert"), None),
        P(None, ("dp", "expert")),
        P(("dp", "expert"), None),
        P(("dp", "expert")),
        P(("dp", "expert")),
        P("expert", None, None),
        P("expert", None, None),
        P(("dp", "expert"), None),
    )
    out_specs = (
        P(("dp", "expert"), None),
        P(("dp", "expert"), None),
        P(("dp", "expert"), None),
        P(("dp", "expert"), None),
        P(None, ("dp", "expert")),
        P(("dp", "expert"), None),
        P(("dp", "expert")),
        P(("dp", "expert")),
        P("expert", "dp", None),
        P("expert", None, "dp"),
    )
    return jax.shard_map(shards, mesh=mesh, in_specs=in_specs, out_specs=out_specs, check_vma=False)
```

```python
import functools

import jax
import jax.numpy as jnp
from jax import lax
from jax.experimental import pallas as pl
from jax.experimental.pallas import tpu as pltpu
from jax.sharding import PartitionSpec as P

D = 1536
HEADS = 24
KV_HEADS = 8
HEAD_DIM = 64
FF = 512
TOP = 8
EXP_DEV = 2

RESIDUAL = 0.22
ATTN_SCALE = 0.015625
LOG2E = 1.4426950408889634
EPSILON = 1e-06
ROPE_BASE = 10000.0
MASKED = -1e30

GROUP = HEADS // KV_HEADS
HALF = HEAD_DIM // 2
BLK = 256
BF = jnp.bfloat16
F32 = jnp.float32
BOTH = ("dp", "expert")


ROOM = {
    "attn_fwd": 8,
    "qkv": 24,
    "back": 12,
    "pack": 20,
    "last": 16,
    "out_grad": 16,
    "unpack": 12,
}


def room(name):
    return pltpu.CompilerParams(vmem_limit_bytes=ROOM[name] << 20 if name in ROOM else None)


def cost(micros):
    return pl.CostEstimate(flops=micros * 10**9, bytes_accessed=10**4, transcendentals=0)


LONG, SHORT = cost(50), cost(0)


def dot(a, b, ca, cb):
    return lax.dot_general(a, b, (((ca,), (cb,)), ((), ())), preferred_element_type=F32)


def rms_scale(values, gain_vec):
    return (
        values * lax.rsqrt(jnp.mean(values * values, axis=-1, keepdims=True) + EPSILON) * gain_vec
    )


def side_by_side(block):
    return jnp.concatenate(
        [block[h * HEAD_DIM : (h + 1) * HEAD_DIM] for h in range(GROUP)], axis=1
    )


def stacked(wide):
    width = wide.shape[1] // GROUP
    return jnp.concatenate([wide[:, h * width : (h + 1) * width] for h in range(GROUP)], axis=0)


def allowed_keys(start_ref, block, key_block):
    lane = lax.broadcasted_iota(jnp.int32, (1, BLK), 1) + block * BLK
    reach = lane - start_ref[...]
    lane3 = jnp.concatenate([lane] * GROUP, axis=1)
    reach3 = jnp.concatenate([reach] * GROUP, axis=1)
    key_pos = lax.broadcasted_iota(jnp.int32, (BLK, 1), 0) + key_block * BLK
    back = lane3 - key_pos
    return (back >= 0) & (back <= reach3)


def over_keys(first_ref, block, step, carry):
    clear = jnp.minimum(first_ref[1, block], block)
    carry = lax.fori_loop(first_ref[0, block], clear, functools.partial(step, True), carry)
    pairs = (block - clear) // 2
    carry = lax.fori_loop(
        0, pairs, lambda n, carry: step(False, clear + 2 * n, carry, 2), carry
    )
    carry = lax.fori_loop(clear + 2 * pairs, block, functools.partial(step, False), carry)
    return step(True, block, carry)


def attn_fwd_kernel(first_ref, q_ref, k_ref, vt_ref, start_ref, a_ref, o_ref, lse_ref):
    block = pl.program_id(0)
    query = side_by_side(q_ref[...])
    width = GROUP * BLK

    def step(masked, key_block, carry, count=1):
        largest, total, acc = carry
        rows = pl.ds(pl.multiple_of(key_block * BLK, BLK), count * BLK)
        keys, values = k_ref[rows, :], vt_ref[:, rows]
        scores = dot(keys, query, 1, 0) * (ATTN_SCALE * LOG2E)
        if masked:
            scores = jnp.where(allowed_keys(start_ref, block, key_block), scores, MASKED)
        now = jnp.maximum(largest, jnp.max(scores, axis=0, keepdims=True))
        power = jnp.exp2(scores - now)
        fade = jnp.exp2(largest - now)
        total = total * fade + jnp.sum(power, axis=0, keepdims=True)
        acc = acc * fade + dot(values, power.astype(BF), 1, 0)
        return now, total, acc

    largest, total, acc = over_keys(
        first_ref,
        block,
        step,
        (
            jnp.full((1, width), MASKED, F32),
            jnp.zeros((1, width), F32),
            jnp.zeros((HEAD_DIM, width), F32),
        ),
    )
    out = stacked(acc / total)
    o_ref[...] = out
    a_ref[...] = out.astype(BF)
    lse = largest + jnp.log2(total)
    lse_ref[...] = jnp.concatenate(
        [lse[:, h * BLK : (h + 1) * BLK] for h in range(GROUP)]
        + [jnp.zeros((8 - GROUP, BLK), F32)],
        axis=0,
    )


def attn_bwd_kernel(
    first_ref, q_ref, da_ref, o_ref, lse_ref, k_ref, kt_ref, v_ref, start_ref,
    dq_ref, dk_ref, dv_ref, dk_acc, dv_acc,
):
    block = pl.program_id(0)

    @pl.when(block == 0)
    def _():
        dk_acc[...] = jnp.zeros_like(dk_acc)
        dv_acc[...] = jnp.zeros_like(dv_acc)

    query_t = side_by_side(q_ref[...])
    query = query_t.astype(F32).T.astype(BF)
    grad_t = side_by_side(da_ref[0])
    grad_f = grad_t.astype(F32)
    grad = grad_f.T.astype(BF)
    delta = jnp.sum(side_by_side(o_ref[...]) * grad_f, axis=0, keepdims=True)
    lse = jnp.concatenate([lse_ref[h : h + 1, :] for h in range(GROUP)], axis=1)

    def step(masked, key_block, dq, count=1):
        rows = pl.ds(pl.multiple_of(key_block * BLK, BLK), count * BLK)
        keys = k_ref[rows, :]
        scores = dot(keys, query_t, 1, 0) * (ATTN_SCALE * LOG2E)
        if masked:
            scores = jnp.where(allowed_keys(start_ref, block, key_block), scores, MASKED)
        prob = jnp.exp2(scores - lse)
        grad_prob = dot(v_ref[rows, :], grad_t, 1, 0)
        grad_score = (prob * (grad_prob - delta) * ATTN_SCALE).astype(BF)
        dv_acc[rows, :] += dot(prob.astype(BF), grad, 1, 0)
        dk_acc[rows, :] += dot(grad_score, query, 1, 0)
        return dq + dot(kt_ref[:, rows], grad_score, 1, 0)

    dq = over_keys(first_ref, block, step, jnp.zeros((HEAD_DIM, GROUP * BLK), F32))
    dq_ref[...] = stacked(dq)

    @pl.when(block == pl.num_programs(0) - 1)
    def _():
        dk_ref[...] = dk_acc[...].T
        dv_ref[...] = dv_acc[...].T


def attn_forward(first, q_t, k, v_t, start):
    seq = q_t.shape[1]
    rows = GROUP * HEAD_DIM
    column = lambda g, first: (0, g)
    whole = lambda g, first: (0, 0)
    return pl.pallas_call(
        attn_fwd_kernel,
        grid_spec=pltpu.PrefetchScalarGridSpec(
            num_scalar_prefetch=1,
            grid=(seq // BLK,),
            in_specs=[
                pl.BlockSpec((rows, BLK), column),
                pl.BlockSpec((seq, HEAD_DIM), whole),
                pl.BlockSpec((HEAD_DIM, seq), whole),
                pl.BlockSpec((1, BLK), column),
            ],
            out_specs=[
                pl.BlockSpec((rows, BLK), column),
                pl.BlockSpec((rows, BLK), column),
                pl.BlockSpec((8, BLK), column),
            ],
        ),
        out_shape=[
            jax.ShapeDtypeStruct((rows, seq), BF),
            jax.ShapeDtypeStruct((rows, seq), F32),
            jax.ShapeDtypeStruct((8, seq), F32),
        ],
        cost_estimate=LONG,
        compiler_params=room("attn_fwd"),
        name="attn_fwd",
    )(first, q_t, k, v_t, start)


def attn_backward(first, q_t, da, o_t, lse, k, k_t, v, start):
    seq = q_t.shape[1]
    rows = GROUP * HEAD_DIM
    column = lambda g, first: (0, g)
    whole = lambda g, first: (0, 0)
    return pl.pallas_call(
        attn_bwd_kernel,
        grid_spec=pltpu.PrefetchScalarGridSpec(
            num_scalar_prefetch=1,
            grid=(seq // BLK,),
            in_specs=[
                pl.BlockSpec((rows, BLK), column),
                pl.BlockSpec((1, rows, BLK), lambda g, first: (g, 0, 0)),
                pl.BlockSpec((rows, BLK), column),
                pl.BlockSpec((8, BLK), column),
                pl.BlockSpec((seq, HEAD_DIM), whole),
                pl.BlockSpec((HEAD_DIM, seq), whole),
                pl.BlockSpec((seq, HEAD_DIM), whole),
                pl.BlockSpec((1, BLK), column),
            ],
            out_specs=[
                pl.BlockSpec((rows, BLK), column),
                pl.BlockSpec((HEAD_DIM, seq), whole),
                pl.BlockSpec((HEAD_DIM, seq), whole),
            ],
            scratch_shapes=[
                pltpu.VMEM((seq, HEAD_DIM), F32),
                pltpu.VMEM((seq, HEAD_DIM), F32),
            ],
        ),
        out_shape=[
            jax.ShapeDtypeStruct((rows, seq), F32),
            jax.ShapeDtypeStruct((HEAD_DIM, seq), F32),
            jax.ShapeDtypeStruct((HEAD_DIM, seq), F32),
        ],
        cost_estimate=cost(20),
        compiler_params=room("attn_bwd"),
        name="attn_bwd",
    )(first, q_t, da, o_t, lse, k, k_t, v, start)


PACK = 384
Q_COLS = GROUP * HEAD_DIM
QKV = Q_COLS + 2 * HEAD_DIM
ROUTE = QKV - 256


def spec(shape, index):
    return pl.BlockSpec(shape, index)


def resident(shape):
    return pl.BlockSpec(
        shape, lambda *_: (0,) * len(shape), pipeline_mode=pl.Buffered(1)
    )


def call(kernel, name, grid, in_specs, out_specs, out_shape, estimate, scratch=()):
    return pl.pallas_call(
        kernel,
        grid_spec=pltpu.PrefetchScalarGridSpec(
            num_scalar_prefetch=1,
            grid=grid,
            in_specs=in_specs,
            out_specs=out_specs,
            scratch_shapes=list(scratch),
        ),
        out_shape=out_shape,
        cost_estimate=estimate,
        compiler_params=room(name),
        name=name,
    )


def shape(dims, kind):
    return jax.ShapeDtypeStruct(dims, kind)


PAIR = 2 * BLK


def far_pair(step, pos):
    return step ^ (pos[0] // 2)


def halves(pos):
    core = pos[0] % 2
    return [pl.ds(pl.multiple_of(start * BLK, BLK), BLK) for start in (1 - core, core)]


def turn_rows(rows_t, cosine, sine):
    out = []
    for h in range(rows_t.shape[0] // HEAD_DIM):
        a = rows_t[h * HEAD_DIM : h * HEAD_DIM + HALF]
        b = rows_t[h * HEAD_DIM + HALF : (h + 1) * HEAD_DIM]
        out += [a * cosine - b * sine, b * cosine + a * sine]
    return jnp.concatenate(out, axis=0)


def norm_of(values):
    return values * lax.rsqrt(jnp.mean(values * values, axis=1, keepdims=True) + EPSILON)


def qkv_kernel(count, pos_ref, *refs):
    pieces = refs[: count + 2]
    w_ref, gain_ref, cos_ref, sin_ref, q_ref, kt_ref, vt_ref, k_ref, v_ref = refs[count + 2 :]
    gain = gain_ref[...]
    for r in range(count):
        if r < count - 2:
            rows = pieces[r][...]
        else:
            at = count - 2 + 2 * (r - count + 2)
            rows = jnp.concatenate([pieces[at][...], pieces[at + 1][...]], axis=0)
        normed = (norm_of(rows.astype(F32)) * gain).astype(BF)
        both = dot(normed, w_ref[...], 1, 0)
        turned = both.T
        place = pl.multiple_of((pos_ref[0] ^ r) * BLK, BLK)
        columns = pl.ds(place, BLK)
        cosine, sine = cos_ref[:, columns], sin_ref[:, columns]
        qk = turn_rows(turned[: Q_COLS + HEAD_DIM], cosine, sine)
        q_ref[:, columns] = qk[:Q_COLS].astype(BF)
        kt_ref[:, columns] = qk[Q_COLS:].astype(BF)
        vt_ref[:, columns] = turned[Q_COLS + HEAD_DIM : QKV].astype(BF)
        k_ref[columns, :] = qk[Q_COLS:].T.astype(BF)
        v_ref[columns, :] = both[:, 256 : 256 + HEAD_DIM].astype(BF)


def qkv_forward(pos, pieces, weights, gain, cosine, sine):
    count = len(pieces) - 2
    seq = cosine.shape[1]
    full = lambda a: resident(a.shape)
    return call(
        functools.partial(qkv_kernel, count),
        "qkv",
        (1,),
        [full(a) for a in pieces] + [full(a) for a in (weights, gain, cosine, sine)],
        [resident(s) for s in ((Q_COLS, seq), (HEAD_DIM, seq), (HEAD_DIM, seq), (seq, HEAD_DIM), (seq, HEAD_DIM))],
        [
            shape((Q_COLS, seq), BF),
            shape((HEAD_DIM, seq), BF),
            shape((HEAD_DIM, seq), BF),
            shape((seq, HEAD_DIM), BF),
            shape((seq, HEAD_DIM), BF),
        ],
        cost(400),
    )(pos, *pieces, weights, gain, cosine, sine)


def as_column(row):
    count = row.shape[1]
    here = lax.broadcasted_iota(jnp.int32, (count, count), 0)
    there = lax.broadcasted_iota(jnp.int32, (count, count), 1)
    return jnp.sum(jnp.where(here == there, row.astype(F32), 0.0), axis=1, keepdims=True)


def send_weights_kernel(
    groups, members, pos_ref, q_ref, kv_ref, route_ref, attn_ref, moe_ref, out_ref
):
    query, pair = q_ref[...], kv_ref[...]
    rows, experts = route_ref.shape
    route = jnp.concatenate(
        [route_ref[...].astype(F32), jnp.zeros((rows, PACK - QKV - experts), F32)], axis=1
    )
    lane = lax.broadcasted_iota(jnp.int32, route.shape, 1)
    rest = jnp.where(lane == experts, as_column(attn_ref[...]), route)
    rest = jnp.where(lane == experts + 1, as_column(moe_ref[...]), rest).astype(BF)
    for j in range(members):
        block = jnp.concatenate(
            [query[:, j * Q_COLS : (j + 1) * Q_COLS]]
            + [pair[:, n * HEAD_DIM : (n + 1) * HEAD_DIM] for n in (j, members + j)]
            + [rest],
            axis=1,
        )
        for i in range(groups):
            out_ref[i * members + j] = block


def send_weights(pos, parts, groups, members):
    rows = parts[0].shape[0]
    full = lambda a: resident(a.shape)
    return call(
        functools.partial(send_weights_kernel, groups, members),
        "send_weights",
        (1,),
        [full(a) for a in parts],
        resident((groups * members, rows, PACK)),
        shape((groups * members, rows, PACK), BF),
        SHORT,
    )(pos, *parts)


def mix_kernel(count, pos_ref, *refs):
    pieces = refs[: count + 2]
    x_ref, w_ref, gain_ref, route_ref, ids_ref = refs[count + 2 : count + 7]
    h2_ref, gates_ref, y1_ref, h2_own_ref, gates_own_ref, heads, y1_all = refs[count + 7 :]
    block = pl.program_id(0)
    pos = pos_ref[0]
    for r in range(count):
        base = (pos ^ r) * Q_COLS
        if r < count - 2:
            heads[pl.ds(pl.multiple_of(base, Q_COLS), Q_COLS), :] = pieces[r][...]
        else:
            half = Q_COLS // 2
            at = count - 2 + 2 * (r - count + 2)
            heads[pl.ds(pl.multiple_of(base, half), half), :] = pieces[at][...]
            heads[pl.ds(pl.multiple_of(base + half, half), half), :] = pieces[at + 1][...]
    route, gain = route_ref[...], gain_ref[...]
    for h in range(2):
        rows = slice(h * BLK, (h + 1) * BLK)
        mixed = dot(heads[:, rows], w_ref[...], 0, 0)
        y1 = x_ref[h ^ (pos % 2)].astype(F32) + RESIDUAL * mixed
        h2 = (norm_of(y1) * gain).astype(BF)
        logits = dot(h2, route, 1, 0)
        lane = lax.broadcasted_iota(jnp.int32, logits.shape, 1) - ROUTE
        ids = ids_ref[h ^ (pos % 2)].T
        chosen = lane == ids[:, 0:1]
        for k in range(1, TOP):
            chosen = chosen | (lane == ids[:, k : k + 1])
        masked = jnp.where(chosen, logits, MASKED)
        power = jnp.where(chosen, jnp.exp(masked - jnp.max(masked, axis=1, keepdims=True)), 0.0)
        gates = power / jnp.sum(power, axis=1, keepdims=True)
        h2_ref[rows] = h2
        gates_ref[rows] = gates
        y1_all[rows] = y1

    @pl.when(block == pos // 2)
    def _():
        mine = halves(pos_ref)[1]
        y1_ref[...] = y1_all[mine]
        h2_own_ref[...] = h2_ref[mine]
        gates_own_ref[...] = gates_ref[mine]


def mix_forward(pos, pieces, x_rel, w_full, gain, weights, ids):
    count = len(pieces) - 2
    seq = ids.shape[0] * BLK
    row = lambda s, pos: (s, 0)
    return call(
        functools.partial(mix_kernel, count),
        "mix",
        (seq // PAIR,),
        [spec((a.shape[0], PAIR), lambda s, pos: (0, s)) for a in pieces]
        + [
            spec((2, BLK, D), lambda s, pos: (far_pair(s, pos), 0, 0)),
            resident(w_full.shape),
            resident(gain.shape),
            pl.BlockSpec((D, 128), lambda s, pos: (0, 2), pipeline_mode=pl.Buffered(1)),
            spec((2, TOP, BLK), lambda s, pos: (far_pair(s, pos), 0, 0)),
        ],
        [
            spec((PAIR, D), row),
            spec((PAIR, 128), row),
            resident((BLK, D)),
            resident((BLK, D)),
            resident((BLK, 128)),
        ],
        [
            shape((seq, D), BF),
            shape((seq, 128), F32),
            shape((BLK, D), F32),
            shape((BLK, D), BF),
            shape((BLK, 128), F32),
        ],
        LONG,
        [pltpu.VMEM((HEADS * HEAD_DIM, PAIR), BF), pltpu.VMEM((PAIR, D), F32)],
    )(pos, *pieces, x_rel, w_full, gain, weights, ids)


def expert_kernel(e, pos_ref, h2_ref, dy_ref, gates_ref, up_ref, down_ref, *refs):
    if e == 0:
        ag_ref, dgu_ref, sum_ref, dg_ref, grad_ref, grad_acc = refs

        @pl.when(pl.program_id(0) == 0)
        def _():
            grad_acc[...] = jnp.zeros_like(grad_acc)

    else:
        sum_ref, dg_in_ref, ag_ref, dgu_ref, give_ref, keep_ref, dg_ref = refs
    for h, rows in enumerate(halves(pos_ref)):
        h2, dy, gates = h2_ref[rows], dy_ref[rows], gates_ref[rows]
        which = lax.broadcasted_iota(jnp.int32, gates.shape, 1)
        here = which == ROUTE + EXP_DEV * pos_ref[0] + e
        gate = RESIDUAL * jnp.sum(jnp.where(here, gates, 0.0), axis=1, keepdims=True)
        gu = dot(h2, up_ref[0], 1, 0)
        back = dot(dy, down_ref[0], 1, 1)
        g, u = gu[:, :FF], gu[:, FF:]
        sig = 1.0 / (1.0 + jnp.exp(-g))
        swish = g * sig
        act = swish * u
        gate_grad = RESIDUAL * jnp.sum(act * back, axis=1, keepdims=True)
        gate_grad = jnp.where(which == e, gate_grad, 0.0).T[:8]
        ag_ref[rows] = (gate * act).astype(BF)
        dact = gate * back
        dgu = jnp.concatenate(
            [dact * u * (sig * (1.0 + g * (1.0 - sig))), dact * swish], axis=1
        ).astype(BF)
        dgu_ref[rows] = dgu
        total = dot(dgu, up_ref[0], 1, 1)
        place = pos_ref[0] % 2 if h else 1 - pos_ref[0] % 2
        if e == 0:
            sum_ref[rows] = total.astype(BF)
            dg_ref[place] = gate_grad
        else:
            (keep_ref if h else give_ref)[0] = (sum_ref[rows].astype(F32) + total).astype(BF)
            dg_ref[place] = dg_in_ref[place] + gate_grad
    if e == 0:
        grad_acc[...] += dot(ag_ref[...], dy_ref[...], 0, 0)

        @pl.when(pl.program_id(0) == pl.num_programs(0) - 1)
        def _():
            put_shares(grad_ref, grad_acc)


def expert_pass(e, pos, h2, dy_all, gates, w_gate_up, w_down, carried=()):
    seq = h2.shape[0]
    row = lambda s, pos: (s, 0)
    blocks = lambda s, pos: (s, 0, 0)
    pair = lambda s, pos: (far_pair(s, pos), 0, 0)
    half = seq // PAIR
    one = lambda a: pl.BlockSpec(
        (1,) + a.shape[1:], lambda s, pos: (e, 0, 0), pipeline_mode=pl.Buffered(1)
    )
    sums = (spec((PAIR, D), row), shape((seq, D), BF))
    gate_grads = (spec((2, 8, BLK), blocks), shape((2 * half, 8, BLK), F32))
    outs = [
        (spec((PAIR, FF), row), shape((seq, FF), BF)),
        (spec((PAIR, 2 * FF), row), shape((seq, 2 * FF), BF)),
    ]
    if e == 0:
        shares = (D // SHARE, FF, SHARE)
        outs += [sums, gate_grads, (resident(shares), shape(shares, BF))]
    else:
        outs += 2 * [(spec((1, BLK, D), pair), shape((half, BLK, D), BF))] + [gate_grads]
    return call(
        functools.partial(expert_kernel, e),
        "expert_%d" % e,
        (half,),
        [spec((PAIR, D), row), spec((PAIR, D), row), spec((PAIR, 128), row)]
        + [one(w_gate_up), one(w_down)]
        + ([sums[0], gate_grads[0]] if carried else []),
        [o[0] for o in outs],
        [o[1] for o in outs],
        cost(5),
        [] if e else [pltpu.VMEM((FF, D), F32)],
    )(pos, h2, dy_all, gates, w_gate_up, w_down, *carried)


SHARE = 384


def put_shares(out_ref, total):
    for n in range(out_ref.shape[0]):
        out_ref[n] = total[:, n * SHARE : (n + 1) * SHARE].astype(BF)


def by_group(shares, groups):
    cols = D // groups
    if cols == SHARE:
        return shares
    whole = jnp.moveaxis(shares, 0, 1).reshape(FF, groups, cols)
    return jnp.moveaxis(whole, 1, 0)


def down_grad_kernel(pos_ref, ag_ref, dy_ref, out_ref):
    put_shares(out_ref, dot(ag_ref[...], dy_ref[...], 0, 0))


def down_grad(pos, ag, dy_all, groups):
    seq = dy_all.shape[0]
    out = call(
        down_grad_kernel,
        "down_grad",
        (D // (2 * SHARE),),
        [resident(ag.shape), spec((seq, 2 * SHARE), lambda s, pos: (0, s))],
        spec((2, FF, SHARE), lambda s, pos: (s, 0, 0)),
        shape((D // SHARE, FF, SHARE), BF),
        SHORT,
    )(pos, ag, dy_all)
    return by_group(out, groups)


def up_grad_kernel(pos_ref, h2_ref, dgu_ref, out_ref):
    out_ref[...] = dot(h2_ref[...], dgu_ref[...], 0, 0).astype(BF)


def up_grad(pos, h2, dgu):
    seq = h2.shape[0]
    rows = 384
    return call(
        up_grad_kernel,
        "up_grad",
        (D // rows,),
        [spec((seq, rows), lambda s, pos: (0, s)), resident(dgu.shape)],
        spec((rows, 2 * FF), lambda s, pos: (s, 0)),
        shape((D, 2 * FF), BF),
        SHORT,
    )(pos, h2, dgu)


def combine_kernel(pos_ref, *refs):
    ags = refs[:EXP_DEV]
    down_ref, give_ref, keep_ref = refs[EXP_DEV:]
    for h, rows in enumerate(halves(pos_ref)):
        total = dot(ags[0][rows], down_ref[0], 1, 0)
        for e in range(1, EXP_DEV):
            total = total + dot(ags[e][rows], down_ref[e], 1, 0)
        (keep_ref if h else give_ref)[0] = total.astype(BF)


def combine(pos, ags, w_down):
    seq = ags[0].shape[0]
    half = seq // PAIR
    pair = lambda s, pos: (far_pair(s, pos), 0, 0)
    return call(
        combine_kernel,
        "combine",
        (half,),
        [spec((PAIR, FF), lambda s, pos: (s, 0)) for _ in ags] + [resident(w_down.shape)],
        [spec((1, BLK, D), pair), spec((1, BLK, D), pair)],
        [shape((half, BLK, D), BF), shape((half, BLK, D), BF)],
        SHORT,
    )(pos, *ags, w_down)


def norm_pull(values, gain, grad):
    scale = lax.rsqrt(jnp.mean(values * values, axis=1, keepdims=True) + EPSILON)
    unit = values * scale
    inner = grad * gain
    pulled = scale * (inner - unit * jnp.mean(inner * unit, axis=1, keepdims=True))
    return pulled, jnp.sum(grad * unit, axis=0, keepdims=True)


def middle_kernel(
    members, groups, wide, pos_ref, keep_ref, got_ref, fx_ref, fy_ref, fd_ref, y1_ref, h2_ref, gates_ref, dg_ref, dy_ref,
    route_ref, gain_ref, w_ref, dy1_ref, db_ref, da_ref, router_ref, gain_grad_ref,
):
    dh2 = (
        keep_ref[0].astype(F32)
        + got_ref[0].astype(F32)
        + fx_ref[...].astype(F32)
        + fy_ref[...].astype(F32)
        + fd_ref[...].astype(F32)
    )
    gates, gate_grads = gates_ref[...], dg_ref[...]
    mean = jnp.sum(gates * gate_grads, axis=1, keepdims=True)
    dlogits = (gates * (gate_grads - mean)).astype(BF)
    dh2 = dh2 + dot(dlogits, route_ref[...], 1, 1)
    router_ref[...] = dot(h2_ref[...], dlogits, 0, 0)
    pulled, gain_grad = norm_pull(y1_ref[...], gain_ref[...], dh2)
    gain_grad_ref[...] = jnp.broadcast_to(gain_grad, gain_grad_ref.shape)
    dy1 = dy_ref[...].astype(F32) + pulled
    dy1_ref[...] = dy1
    db = (RESIDUAL * dy1).astype(BF)
    db_ref[...] = db
    da = dot(w_ref[...], db, 1, 1).astype(BF)
    for j in range(members):
        da_ref[j, :Q_COLS] = da[j * Q_COLS : (j + 1) * Q_COLS]
    if wide:
        cols = Q_COLS // groups
        db_t = (RESIDUAL * dy1).T.astype(BF)
        for j in range(members):
            for i in range(groups):
                at, to = (i * members + j) * cols, Q_COLS + i * cols
                da_ref[j, to : to + cols] = db_t[at : at + cols]


def middle(groups, pos, keep, got, sums, y1, h2, gates, dg, dy, weights, gain, w_full):
    rows = y1.shape[0]
    full = lambda a: resident(a.shape)
    first = pl.BlockSpec((1, rows, D), lambda s, pos: (0, 0, 0), pipeline_mode=pl.Buffered(1))
    members = HEADS * HEAD_DIM // Q_COLS
    wide = Q_COLS // groups % 16 == 0
    both = 2 * Q_COLS if wide else Q_COLS
    dy1, db, sent, router, gain_grad = call(
        functools.partial(middle_kernel, members, groups, wide),
        "middle",
        (1,),
        [first, first]
        + [full(a) for a in (*sums, y1, h2, gates, dg, dy)]
        + [
            pl.BlockSpec((D, 128), lambda s, pos: (0, 2), pipeline_mode=pl.Buffered(1)),
            full(gain),
            full(w_full),
        ],
        [
            resident((rows, D)),
            resident((rows, D)),
            resident((members, both, rows)),
            resident((D, 128)),
            resident((8, D)),
        ],
        [
            shape((rows, D), F32),
            shape((rows, D), BF),
            shape((members, both, rows), BF),
            shape((D, 128), F32),
            shape((8, D), F32),
        ],
        cost(100),
    )(pos, keep, got, *sums, y1, h2, gates, dg, dy, weights, gain, w_full)
    if not wide:
        cols = Q_COLS // groups
        db_t = jnp.moveaxis(db.T.reshape(groups, members, cols, rows), 1, 0)
        sent = jnp.concatenate([sent, db_t.reshape(members, Q_COLS, rows)], axis=1)
    return dy1, sent, router, gain_grad


def back_kernel(
    pos_ref, dq_ref, dk_ref, dv_ref, cos_ref, sin_ref, w_ref, give_ref, keep_ref, packed_ref
):
    cosine, sine = cos_ref[...], -sin_ref[...]
    rows_t = jnp.concatenate(
        [
            turn_rows(dq_ref[...], cosine, sine),
            turn_rows(dk_ref[...], cosine, sine),
            dv_ref[...],
            jnp.zeros((PACK - QKV, PAIR), F32),
        ],
        axis=0,
    ).astype(BF)
    packed_ref[...] = rows_t
    for h, rows in enumerate(halves(pos_ref)):
        total = dot(packed_ref[:, rows], w_ref[...], 0, 1).astype(BF)
        (keep_ref if h else give_ref)[0] = total


def back(pos, dq_t, dk_t, dv_t, cosine, sine, weights):
    seq = dq_t.shape[1]
    half = seq // PAIR
    column = lambda s, pos: (0, s)
    pair = lambda s, pos: (far_pair(s, pos), 0, 0)
    return call(
        back_kernel,
        "back",
        (half,),
        [
            spec((Q_COLS, PAIR), column),
            spec((HEAD_DIM, PAIR), column),
            spec((HEAD_DIM, PAIR), column),
            spec((HALF, PAIR), column),
            spec((HALF, PAIR), column),
            resident(weights.shape),
        ],
        [spec((1, BLK, D), pair), spec((1, BLK, D), pair), spec((PACK, PAIR), column)],
        [
            shape((half, BLK, D), BF),
            shape((half, BLK, D), BF),
            shape((PACK, seq), BF),
        ],
        SHORT,
    )(pos, dq_t, dk_t, dv_t, cosine, sine, weights)


def low_pair(values):
    high = values.astype(BF).astype(F32)
    return high, values - high


def pack_kernel(pos_ref, packed_ref, x_ref, gain_ref, w_ref, router_ref, moe_ref, out_ref, acc):
    step = pl.program_id(0)

    @pl.when(step == 0)
    def _():
        acc[...] = jnp.zeros_like(acc)

    term = None
    for h in range(2):
        here = x_ref[h ^ (pos_ref[0] % 2)].astype(F32)
        normed = (norm_of(here) * gain_ref[...]).astype(BF)
        part = dot(packed_ref[:, h * BLK : (h + 1) * BLK], normed, 1, 0)
        term = part if term is None else term + part
    acc[...] += term

    @pl.when(step == pl.num_programs(0) - 1)
    def _():
        main, rest = acc[:256].T, acc[256:].T
        w_main, w_rest = w_ref[:, :256].astype(F32), w_ref[:, 256:].astype(F32)
        lane = lax.broadcasted_iota(jnp.int32, (D, 128), 1)
        gain_attn = (
            jnp.sum(main * w_main, axis=1, keepdims=True)
            + jnp.sum(rest * w_rest, axis=1, keepdims=True)
        ) / w_rest[:, ROUTE + 16 : ROUTE + 17]
        high, low = low_pair(router_ref[...])
        moe_high, moe_low = low_pair(moe_ref[...].T)
        attn_high, attn_low = low_pair(gain_attn)
        rest = rest + high + pltpu.roll(low, 16, 1)
        for at, column in enumerate((moe_high[:, :1], moe_low[:, :1], attn_high, attn_low)):
            rest = jnp.where(lane == ROUTE + 32 + at, column, rest)
        out_ref[:, :256] = main.astype(BF)
        out_ref[:, 256:] = rest.astype(BF)


def pack(pos, packed, x_rel, gain, weights, router, moe):
    seq = packed.shape[1]
    return call(
        pack_kernel,
        "pack",
        (seq // PAIR,),
        [
            spec((PACK, PAIR), lambda s, pos: (0, s)),
            spec((2, BLK, D), lambda s, pos: (far_pair(s, pos), 0, 0)),
            resident(gain.shape),
            resident(weights.shape),
            resident(router.shape),
            resident(moe.shape),
        ],
        resident((D, PACK)),
        shape((D, PACK), BF),
        cost(50),
        [pltpu.VMEM((PACK, D), F32)],
    )(pos, packed, x_rel, gain, weights, router, moe)


def last_kernel(
    pos_ref, keep_ref, got_ref, fx_ref, fy_ref, fd_ref, x_ref, gain_ref, dy1_ref, out_ref
):
    dh1 = (
        keep_ref[0].astype(F32)
        + got_ref[0].astype(F32)
        + fx_ref[...].astype(F32)
        + fy_ref[...].astype(F32)
        + fd_ref[...].astype(F32)
    )
    pulled, _ = norm_pull(x_ref[...].astype(F32), gain_ref[...], dh1)
    out_ref[...] = (dy1_ref[...] + pulled).astype(BF)


def last(pos, keep, got, sums, x, gain, dy1):
    rows = x.shape[0]
    full = lambda a: resident(a.shape)
    first = pl.BlockSpec((1, rows, D), lambda s, pos: (0, 0, 0), pipeline_mode=pl.Buffered(1))
    return call(
        last_kernel,
        "last",
        (1,),
        [first, first] + [full(a) for a in (*sums, x, gain, dy1)],
        resident((rows, D)),
        shape((rows, D), BF),
        cost(50),
    )(pos, keep, got, *sums, x, gain, dy1)


def out_grad_kernel(count, pos_ref, *refs):
    pieces = refs[: count + 2]
    db_ref, out_ref, heads = refs[count + 2 :]
    step = pl.program_id(0)
    pos = pos_ref[0]
    for r in range(count):
        base = (pos ^ r) * Q_COLS
        if r < count - 2:
            heads[pl.ds(pl.multiple_of(base, Q_COLS), Q_COLS), :] = pieces[r][...]
        else:
            half = Q_COLS // 2
            at = count - 2 + 2 * (r - count + 2)
            heads[pl.ds(pl.multiple_of(base, half), half), :] = pieces[at][...]
            heads[pl.ds(pl.multiple_of(base + half, half), half), :] = pieces[at + 1][...]
    term = dot(db_ref[0], heads[...], 1, 1)

    @pl.when(step == 0)
    def _():
        out_ref[...] = term

    @pl.when(step > 0)
    def _():
        out_ref[...] += term


def out_grad(pos, pieces, came):
    count = len(pieces) - 2
    seq, cols = came.shape[0] * BLK, Q_COLS
    return call(
        functools.partial(out_grad_kernel, count),
        "out_grad",
        (seq // BLK,),
        [spec((a.shape[0], BLK), lambda s, pos: (0, s)) for a in pieces]
        + [spec((1, cols, BLK), lambda s, pos: (s, 1, 0))],
        resident((cols, HEADS * HEAD_DIM)),
        shape((cols, HEADS * HEAD_DIM), F32),
        SHORT,
        [pltpu.VMEM((HEADS * HEAD_DIM, BLK), BF)],
    )(pos, *pieces, came).astype(BF)


def unpack_kernel(groups, members, pos_ref, came_ref, query_ref, pair_ref, rest_ref):
    total = None
    for j in range(members):
        here = came_ref[j].astype(F32)
        for i in range(1, groups):
            here = here + came_ref[i * members + j].astype(F32)
        query_ref[:, j * Q_COLS : (j + 1) * Q_COLS] = here[:, :Q_COLS]
        pair_ref[:, j * HEAD_DIM : (j + 1) * HEAD_DIM] = here[:, Q_COLS : Q_COLS + HEAD_DIM]
        at = (members + j) * HEAD_DIM
        pair_ref[:, at : at + HEAD_DIM] = here[:, Q_COLS + HEAD_DIM : QKV]
        rest = here[:, 256:]
        total = rest if total is None else total + rest
    rest_ref[...] = total


def unpack(pos, came, groups):
    devices, rows, _ = came.shape
    members = devices // groups
    return call(
        functools.partial(unpack_kernel, groups, members),
        "unpack",
        (1,),
        [resident(came.shape)],
        [resident((rows, D)), resident((rows, 2 * KV_HEADS * HEAD_DIM)), resident((rows, 128))],
        [
            shape((rows, D), F32),
            shape((rows, 2 * KV_HEADS * HEAD_DIM), F32),
            shape((rows, 128), F32),
        ],
        SHORT,
    )(pos, came)


def swap(values, bit):
    count = lax.axis_size("expert")
    return lax.ppermute(values, "expert", [(i, i ^ bit) for i in range(count)])


def gather_pieces(own, before_last):
    half = own.shape[0] // 2
    x, y = swap(own, 2), swap(own, 4)
    core = swap(own, 1)
    far_a, far_b = tie((swap(x[:half], 4), swap(y[half:], 2)), before_last)
    return [
        own, core, x, swap(x, 1), y, swap(y, 1),
        far_a, far_b, swap(far_a, 1), swap(far_b, 1),
    ]


def gather_direct(own):
    near = [own, swap(own, 2), swap(own, 4), swap(own, 6)]
    return [piece for value in near for piece in (value, swap(value, 1))]


def tie(values, *after):
    return lax.optimization_barrier((values, after))[0]


def pair_sums(keep, got):
    return [(keep[r].astype(F32) + got[r].astype(F32)).astype(BF) for r in (1, 2, 3)]


def send_sums(sums):
    return [swap(sums[0], 2), swap(sums[1], 4), swap(sums[2], 6)]


def send_to_groups(blocks):
    count = lax.axis_size("dp")
    me = lax.axis_index("dp")
    terms = [lax.dynamic_index_in_dim(blocks, me, 0, False)]
    for k in range(1, count):
        sent = lax.dynamic_index_in_dim(blocks, (me + k) % count, 0, False)
        terms.append(lax.ppermute(sent, "dp", [(i, (i + k) % count) for i in range(count)]))
    return terms


def exchange(blocks, axes):
    return lax.all_to_all(blocks, axes, split_axis=0, concat_axis=0, tiled=True)


def shards(
    tokens,
    segment_ids,
    expert_ids,
    w_query,
    w_key_value,
    w_out,
    w_router,
    norm_attn,
    norm_moe,
    w_gate_up,
    w_down,
    grad_out,
):
    tok_rows = tokens.shape[0]
    members = lax.axis_size("expert")
    groups = lax.axis_size("dp")
    position = lax.axis_index("expert")
    pos = position.astype(jnp.int32).reshape(1)
    devices = groups * members
    seq = tok_rows * members
    expert_total = EXP_DEV * members
    in_rows = w_query.shape[0]
    out_cols = w_out.shape[1]
    kv_cols = KV_HEADS * HEAD_DIM

    start = jnp.sum(
        (segment_ids[:, None] < segment_ids[None, :]).astype(jnp.int32), axis=0, keepdims=True
    )
    first = jnp.stack([start[0, ::BLK] // BLK, (start[0, BLK - 1 :: BLK] + BLK - 1) // BLK])
    x_pieces = gather_pieces(tokens, (start, first))

    own = send_weights(
        pos, (w_query, w_key_value, w_router, norm_attn[None], norm_moe[None]), groups, members
    )
    weights = exchange(own, BOTH).reshape(D, PACK)
    gain_attn = weights[:, QKV + expert_total].astype(F32)[None]
    gain_moe = weights[:, QKV + expert_total + 1].astype(F32)[None]

    token_pos = jnp.arange(seq, dtype=jnp.int32)
    frequency = ROPE_BASE ** (-(jnp.arange(HALF, dtype=F32) * 2.0 / HEAD_DIM))
    angles = frequency[:, None] * token_pos.astype(F32)[None, :]
    cosine, sine = jnp.cos(angles), jnp.sin(angles)

    q_t, k_t, v_t, k, v = qkv_forward(
        pos, x_pieces, weights, gain_attn, cosine, sine
    )
    w_full = lax.all_gather(tie(w_out.T, own), BOTH, axis=0, tiled=True)
    dy_all = lax.all_gather(tie(grad_out, own), "expert", axis=0, tiled=True)
    w_full = w_full.T
    a_t, o_t, lse = attn_forward(first, q_t, k, v_t, start)
    ids = jnp.concatenate(gather_direct(tie(expert_ids, q_t).T), axis=0)
    ids = ids.reshape(members, TOP, tok_rows)
    a_pieces = gather_pieces(a_t, (w_full, ids))
    x_rel = jnp.concatenate(tie(x_pieces, a_t), axis=0).reshape(members, tok_rows, D)

    h2, gates, y1, h2_own, gates_own = mix_forward(
        pos, a_pieces, x_rel, w_full, gain_moe, weights, ids
    )

    ag0, dgu0, *carried, down0 = expert_pass(0, pos, h2, dy_all, gates, w_gate_up, w_down)
    down0 = by_group(down0, groups)
    ag1, dgu1, give, keep, dg = expert_pass(
        1, pos, h2, dy_all, gates, w_gate_up, w_down, carried
    )
    got = swap(give, 1)
    down1 = down_grad(pos, ag1, dy_all, groups)
    sums = pair_sums(keep, tie(got, down1))
    came_sums = send_sums(sums)
    dg = exchange(tie(dg, sums), "expert")[:, :EXP_DEV].reshape(expert_total, tok_rows).T
    dg = jnp.pad(dg, ((0, 0), (ROUTE, 128 - ROUTE - expert_total)))
    up0 = up_grad(pos, *tie((h2, dgu0), sums))
    up1 = up_grad(pos, *tie((h2, dgu1), up0))
    out_give, out_keep = combine(pos, tie((ag0, ag1), up1), w_down)
    spread = functools.partial(lax.psum_scatter, axis_name="dp", scatter_dimension=0, tiled=True)
    down_share = [spread(d.reshape(groups * FF, -1)) for d in (down0, down1)]
    up_share = [spread(d) for d in (up0, up1)]
    keep, down_share[0] = lax.optimization_barrier((keep, down_share[0]))
    out_got = swap(out_give, 1)

    dy1, da, router_wgrad, moe_gain_grad = middle(
        groups, pos, tie(keep, out_keep), got, came_sums, y1, h2_own, gates_own, dg, grad_out,
        weights, gain_moe, w_full,
    )
    da = exchange(da, "expert")
    out_sums = pair_sums(out_keep, tie(out_got, dy1))
    out_came = send_sums(out_sums)

    dq_t, dk_t, dv_t = attn_backward(first, q_t, tie(da, out_sums), o_t, lse, k, k_t, v, start)
    give1, keep1, packed = back(pos, dq_t, dk_t, dv_t, cosine, sine, weights)
    got1 = swap(give1, 1)
    sent = pack(pos, packed, x_rel, gain_attn, weights, router_wgrad, moe_gain_grad)
    sums1 = pair_sums(keep1, tie(got1, sent))
    came_sums1 = send_sums(sums1)
    result = y1 + out_keep[0].astype(F32) + out_got[0].astype(F32)
    for term in tie(out_came, sums1):
        result = result + term.astype(F32)
    result = result.astype(BF)
    out_wgrad = out_grad(pos, a_pieces, tie(da, result)).reshape(groups, out_cols, D)
    out_terms = send_to_groups(out_wgrad)
    came = exchange(sent.reshape(devices, in_rows, PACK), BOTH)
    token_grad = last(pos, keep1, got1, came_sums1, tokens, gain_attn, dy1)
    up_share = jnp.stack(tie(up_share, token_grad)).astype(F32)
    query_share, pair_share, rest = unpack(pos, tie(came, up_share), groups)
    router_share = (
        rest[:, ROUTE : ROUTE + expert_total]
        + rest[:, ROUTE + expert_total : ROUTE + 2 * expert_total]
    )
    moe_gain_share = rest[:, ROUTE + 32] + rest[:, ROUTE + 33]

    attn_gain_share = rest[:, ROUTE + 34] + rest[:, ROUTE + 35]
    out_share = sum(term.astype(F32) for term in tie(out_terms, up_share)).T

    return (
        result,
        token_grad,
        query_share,
        pair_share,
        out_share,
        router_share,
        attn_gain_share,
        moe_gain_share,
        up_share,
        jnp.stack(down_share).astype(F32),
    )


def solution(mesh):
    in_specs = (
        P(("dp", "expert"), None),
        P("dp"),
        P(("dp", "expert"), None),
        P(("dp", "expert"), None),
        P(("dp", "expert"), None),
        P(None, ("dp", "expert")),
        P(("dp", "expert"), None),
        P(("dp", "expert")),
        P(("dp", "expert")),
        P("expert", None, None),
        P("expert", None, None),
        P(("dp", "expert"), None),
    )
    out_specs = (
        P(("dp", "expert"), None),
        P(("dp", "expert"), None),
        P(("dp", "expert"), None),
        P(("dp", "expert"), None),
        P(None, ("dp", "expert")),
        P(("dp", "expert"), None),
        P(("dp", "expert")),
        P(("dp", "expert")),
        P("expert", "dp", None),
        P("expert", None, "dp"),
    )
    return jax.shard_map(shards, mesh=mesh, in_specs=in_specs, out_specs=out_specs, check_vma=False)
```
